32 devices in a mesh: dp: 16 (over z, y, x), fsdp: 2 (over core).
Axes of the slice: x: 2, y: 2, z: 4, core: 2. Of those that a mesh axis runs over, the one named last changes fastest.
Arguments:
- inputs: float32 [64, 28, 28, 1024], P('dp', 'fsdp'), may hold values from -6 to 6
- cotangent: float32 [64, 28, 28, 1024], P('dp', 'fsdp'), may hold values from -6 to 6
- clip_index: int32 [64], replicated, may hold values from 0 to 9, never falling along the last dimension, each value on 1 to 8 neighbouring positions
- reduce_weight: float32 [2, 1024, 256], P(None, ('dp', 'fsdp')), may hold values from -0.1875 to 0.1875
- mixing_weight: float32 [2, 256, 256], P(None, ('dp', 'fsdp')), may hold values from -0.375 to 0.375
- depthwise: float32 [2, 256, 27], P(None, ('dp', 'fsdp')), may hold values from -1.25 to 1.25
- expand_weight: float32 [2, 256, 1024], P(None, ('dp', 'fsdp')), may hold values from -0.375 to 0.375
- gain_narrow: float32 [2, 256], P(None, ('dp', 'fsdp')), may hold values from 0.1 to 1.9
- bias_narrow: float32 [2, 256], P(None, ('dp', 'fsdp')), may hold values from -3 to 3
- gain_depth: float32 [2, 256], P(None, ('dp', 'fsdp')), may hold values from 0.1 to 1.9
- bias_depth: float32 [2, 256], P(None, ('dp', 'fsdp')), may hold values from -3 to 3
- gain_wide: float32 [2, 1024], P(None, ('dp', 'fsdp')), may hold values from 0.1 to 1.9
- bias_wide: float32 [2, 1024], P(None, ('dp', 'fsdp')), may hold values from -3 to 3
- momentum_reduce_weight: float32 [2, 1024, 256], P(None, ('dp', 'fsdp')), may hold values from -2048 to 2048
- momentum_mixing_weight: float32 [2, 256, 256], P(None, ('dp', 'fsdp')), may hold values from -2048 to 2048
- momentum_depthwise: float32 [2, 256, 27], P(None, ('dp', 'fsdp')), may hold values from -2048 to 2048
- momentum_expand_weight: float32 [2, 256, 1024], P(None, ('dp', 'fsdp')), may hold values from -2048 to 2048
- momentum_gain_narrow: float32 [2, 256], P(None, ('dp', 'fsdp')), may hold values from -2048 to 2048
- momentum_bias_narrow: float32 [2, 256], P(None, ('dp', 'fsdp')), may hold values from -2048 to 2048
- momentum_gain_depth: float32 [2, 256], P(None, ('dp', 'fsdp')), may hold values from -2048 to 2048
- momentum_bias_depth: float32 [2, 256], P(None, ('dp', 'fsdp')), may hold values from -2048 to 2048
- momentum_gain_wide: float32 [2, 1024], P(None, ('dp', 'fsdp')), may hold values from -2048 to 2048
- momentum_bias_wide: float32 [2, 1024], P(None, ('dp', 'fsdp')), may hold values from -2048 to 2048
Outputs:
- block_out: float32 [64, 28, 28, 1024], P('dp', 'fsdp')
- pooled: float32 [10, 1024], replicated
- gradient_inputs: float32 [64, 28, 28, 1024], P('dp', 'fsdp')
- gradient_reduce_weight: float32 [2, 1024, 256], P(None, ('dp', 'fsdp'))
- gradient_mixing_weight: float32 [2, 256, 256], P(None, ('dp', 'fsdp'))
- gradient_depthwise: float32 [2, 256, 27], P(None, ('dp', 'fsdp'))
- gradient_expand_weight: float32 [2, 256, 1024], P(None, ('dp', 'fsdp'))
- gradient_gain_narrow: float32 [2, 256], P(None, ('dp', 'fsdp'))
- gradient_bias_narrow: float32 [2, 256], P(None, ('dp', 'fsdp'))
- gradient_gain_depth: float32 [2, 256], P(None, ('dp', 'fsdp'))
- gradient_bias_depth: float32 [2, 256], P(None, ('dp', 'fsdp'))
- gradient_gain_wide: float32 [2, 1024], P(None, ('dp', 'fsdp'))
- gradient_bias_wide: float32 [2, 1024], P(None, ('dp', 'fsdp'))
- velocity_reduce_weight: float32 [2, 1024, 256], P(None, ('dp', 'fsdp'))
- velocity_mixing_weight: float32 [2, 256, 256], P(None, ('dp', 'fsdp'))
- velocity_depthwise: float32 [2, 256, 27], P(None, ('dp', 'fsdp'))
- velocity_expand_weight: float32 [2, 256, 1024], P(None, ('dp', 'fsdp'))
- velocity_gain_narrow: float32 [2, 256], P(None, ('dp', 'fsdp'))
- velocity_bias_narrow: float32 [2, 256], P(None, ('dp', 'fsdp'))
- velocity_gain_depth: float32 [2, 256], P(None, ('dp', 'fsdp'))
- velocity_bias_depth: float32 [2, 256], P(None, ('dp', 'fsdp'))
- velocity_gain_wide: float32 [2, 1024], P(None, ('dp', 'fsdp'))
- velocity_bias_wide: float32 [2, 1024], P(None, ('dp', 'fsdp'))
- updated_reduce_weight: float32 [2, 1024, 256], P(None, ('dp', 'fsdp'))
- updated_mixing_weight: float32 [2, 256, 256], P(None, ('dp', 'fsdp'))
- updated_depthwise: float32 [2, 256, 27], P(None, ('dp', 'fsdp'))
- updated_expand_weight: float32 [2, 256, 1024], P(None, ('dp', 'fsdp'))
- updated_gain_narrow: float32 [2, 256], P(None, ('dp', 'fsdp'))
- updated_bias_narrow: float32 [2, 256], P(None, ('dp', 'fsdp'))
- updated_gain_depth: float32 [2, 256], P(None, ('dp', 'fsdp'))
- updated_bias_depth: float32 [2, 256], P(None, ('dp', 'fsdp'))
- updated_gain_wide: float32 [2, 1024], P(None, ('dp', 'fsdp'))
- updated_bias_wide: float32 [2, 1024], P(None, ('dp', 'fsdp'))
The draws below stay inside these ranges and needn't reach their ends.
Inputs may be any that keep to these rules, and one draw needn't show every extreme that they name: `clip_index`: clip numbers never fall along the frames; each of the 10 clips holds 1 to 8 frames, and one holds exactly 8.
All inputs are finite; a program needn't handle non-finite values.
Results may differ from the reference program's by a relative error of at most 0.0085.
Values sent between devices are 32-bit elements; how exact they have to be, the bound alone decides.
No kernel may reach another device: no remote copies, remote signals or barrier semaphores. Data moves between devices by JAX's collectives and lax.ppermute only.
A program may use at most 192 MiB of HBM per device.

```python
import math
import jax
import jax.numpy as jnp
import numpy as np
from jax import lax

D = 1024
B = 256
H = 28
W = 28
CLIP_MAX = 8
NF = 64
CLIPS = 10


def block_levels(rng, dims, pieces, smallest, largest):
    factor_of = 1.0
    for dim, shards_of in pieces:
        draws = jax.random.uniform(jax.random.fold_in(jax.random.fold_in(rng, 6), dim), (shards_of,), jnp.float32, smallest / len(pieces), largest / len(pieces))
        factor_of = factor_of * jnp.repeat(jnp.exp(draws), dims[dim] // shards_of).reshape((-1,) + (1,) * (len(dims) - 1 - dim))
    return factor_of


def profile(amount, total, reach, slope):
    weights = [(1 << 20) // math.isqrt(grade ** slope) + 1 for grade in range(2, amount + 1)]
    spare, holding = total - reach - (amount - 1), [1] * (amount - 1)
    while spare > 0:
        movable = [i for i in range(amount - 1) if holding[i] < reach]
        mass, budget = sum([weights[i] for i in movable]), spare
        for i in movable:
            more = min(reach - holding[i], max(1, budget * weights[i] // mass), spare)
            holding[i] = holding[i] + more
            spare = spare - more
    return np.array([reach] + holding)


def ragged(key, count, total, bound, slope):
    if count == 2:
        one = jax.random.randint(key, (), max(1, total - bound), min(bound, total - 1) + 1)
        return jnp.stack([one, total - one])
    sizes = jnp.asarray(profile(count, total, bound, slope), jnp.int32)
    couples = (count - 1) // 2
    donor, taker = sizes[1:1 + 2 * couples:2], sizes[2:2 + 2 * couples:2]
    room = jnp.minimum(donor - 1, bound - taker)
    shifted = jax.random.randint(jax.random.fold_in(key, 1), (couples,), 0, 1 << 20) % (room + 1)
    sizes = sizes.at[1:1 + 2 * couples:2].set(donor - shifted).at[2:2 + 2 * couples:2].set(taker + shifted)
    return sizes[jax.random.permutation(jax.random.fold_in(key, 2), count)]


def normal_values(key, dims, width, reach, cuts=(), held_as=jnp.bfloat16):
    level = block_levels(key, dims, cuts, -0.22, 0.18) if cuts else 1.0
    drawn = jax.random.normal(key, dims, jnp.float32) * width * level
    return jnp.minimum(jnp.maximum(drawn, -reach), reach).astype(held_as)


def setup_inputs(seed: int = 0) -> dict:
    key_of = jax.random.split(jax.random.key(seed), 24)
    inputs = normal_values(key_of[0], (NF, H, W, D), 1.0, 6.0, ((0, 16), (1, 2)), jnp.float32)
    cotangent = normal_values(key_of[1], (NF, H, W, D), 1.0, 6.0, ((0, 16), (1, 2)), jnp.float32)
    clip_index = jnp.searchsorted(jnp.cumsum(ragged(key_of[2], CLIPS, NF, CLIP_MAX, 0)), jnp.arange(NF), side="right").astype(jnp.int32)
    reduce_weight = normal_values(key_of[3], (2, D, B), D ** -0.5, 0.1875, ((1, 32),), jnp.float32)
    mixing_weight = normal_values(key_of[4], (2, B, B), B ** -0.5, 0.375, ((1, 32),), jnp.float32)
    depthwise = normal_values(key_of[5], (2, B, 27), 27 ** -0.5, 1.25, ((1, 32),), jnp.float32)
    expand_weight = normal_values(key_of[6], (2, B, D), B ** -0.5, 0.375, ((1, 32),), jnp.float32)
    gain_narrow = jnp.clip(1.0 + 0.18 * jax.random.normal(key_of[7], (2, B), jnp.float32), 0.1, 1.9)
    bias_narrow = normal_values(key_of[8], (2, B), 0.5, 3.0, ((1, 32),), jnp.float32)
    gain_depth = jnp.clip(1.0 + 0.18 * jax.random.normal(key_of[9], (2, B), jnp.float32), 0.1, 1.9)
    bias_depth = normal_values(key_of[10], (2, B), 0.5, 3.0, ((1, 32),), jnp.float32)
    gain_wide = jnp.clip(1.0 + 0.18 * jax.random.normal(key_of[11], (2, D), jnp.float32), 0.1, 1.9)
    bias_wide = normal_values(key_of[12], (2, D), 0.5, 3.0, ((1, 32),), jnp.float32)
    momentum_reduce_weight = normal_values(key_of[13], (2, D, B), (H * W // 2), 2048.0, ((1, 32),), jnp.float32)
    momentum_mixing_weight = normal_values(key_of[14], (2, B, B), (H * W // 2), 2048.0, ((1, 32),), jnp.float32)
    momentum_depthwise = normal_values(key_of[15], (2, B, 27), (H * W // 2), 2048.0, ((1, 32),), jnp.float32)
    momentum_expand_weight = normal_values(key_of[16], (2, B, D), (H * W // 2), 2048.0, ((1, 32),), jnp.float32)
    momentum_gain_narrow = normal_values(key_of[17], (2, B), (H * W // 2), 2048.0, ((1, 32),), jnp.float32)
    momentum_bias_narrow = normal_values(key_of[18], (2, B), (H * W // 2), 2048.0, ((1, 32),), jnp.float32)
    momentum_gain_depth = normal_values(key_of[19], (2, B), (H * W // 2), 2048.0, ((1, 32),), jnp.float32)
    momentum_bias_depth = normal_values(key_of[20], (2, B), (H * W // 2), 2048.0, ((1, 32),), jnp.float32)
    momentum_gain_wide = normal_values(key_of[21], (2, D), (H * W // 2), 2048.0, ((1, 32),), jnp.float32)
    momentum_bias_wide = normal_values(key_of[22], (2, D), (H * W // 2), 2048.0, ((1, 32),), jnp.float32)
    return dict(inputs=inputs, cotangent=cotangent, clip_index=clip_index, reduce_weight=reduce_weight, mixing_weight=mixing_weight, depthwise=depthwise, expand_weight=expand_weight, gain_narrow=gain_narrow, bias_narrow=bias_narrow, gain_depth=gain_depth, bias_depth=bias_depth, gain_wide=gain_wide, bias_wide=bias_wide, momentum_reduce_weight=momentum_reduce_weight, momentum_mixing_weight=momentum_mixing_weight, momentum_depthwise=momentum_depthwise, momentum_expand_weight=momentum_expand_weight, momentum_gain_narrow=momentum_gain_narrow, momentum_bias_narrow=momentum_bias_narrow, momentum_gain_depth=momentum_gain_depth, momentum_bias_depth=momentum_bias_depth, momentum_gain_wide=momentum_gain_wide, momentum_bias_wide=momentum_bias_wide)


EPSILON = 1e-05
MOMENTUM = 0.9
LEARN_RATE = 0.0001
HIGHEST = lax.Precision.HIGHEST

@jax.custom_vjp
def low(v):
    return lax.optimization_barrier(v.astype(jnp.bfloat16)).astype(jnp.float32)

@jax.custom_vjp
def low_back(v):
    return v

def low_keep(v):
    return (low(v), None)

def low_pass(kept, grad):
    return (grad,)

def back_keep(v):
    return (v, None)

def back_low(kept, grad):
    return (low(grad),)
low.defvjp(low_keep, low_pass)
low_back.defvjp(back_keep, back_low)

def keep_table(clip_index):
    edge = jnp.full((1,), -1, jnp.int32)
    padded = jnp.concatenate([edge, clip_index.astype(jnp.int32), edge])
    centre = padded[1:-1]
    before = (padded[:-2] == centre).astype(jnp.float32)
    after = (padded[2:] == centre).astype(jnp.float32)
    return jnp.stack([before, jnp.ones(centre.shape, jnp.float32), after])

def stencil(field, kernel, keep_mask):
    frames, rows, columns = (field.shape[0], field.shape[1], field.shape[2])
    padded = jnp.pad(field, ((1, 1), (1, 1), (1, 1), (0, 0)))
    result = jnp.zeros(field.shape, jnp.float32)
    for offset_time in range(3):
        partial_sum = jnp.zeros(field.shape, jnp.float32)
        for offset_row in range(3):
            for offset_col in range(3):
                tap_weight = kernel[:, offset_time * 9 + offset_row * 3 + offset_col]
                partial_sum = partial_sum + padded[offset_time:offset_time + frames, offset_row:offset_row + rows, offset_col:offset_col + columns, :] * tap_weight
        result = result + keep_mask[offset_time][:, None, None, None] * partial_sum
    return result

def dense(field, weight):
    shape = field.shape
    flat = jnp.dot(field.reshape(-1, shape[3]), weight, precision=HIGHEST, preferred_element_type=jnp.float32)
    return flat.reshape(shape[:3] + (weight.shape[1],))

def batch_norm(values, gain, bias):
    average = lax.optimization_barrier(jnp.mean(values, axis=(0, 1, 2)))
    centred = values - average
    variance = lax.optimization_barrier(jnp.mean(centred * centred, axis=(0, 1, 2)))
    return gain * centred * lax.rsqrt(variance + EPSILON) + bias

def bottleneck(field, weights, keep_mask):
    reduce_full, mixing_full, depth_full, expand_full, gain_narrow, bias_narrow, gain_depth, bias_depth, gain_wide, bias_wide = weights
    first = jax.nn.relu(batch_norm(dense(field, reduce_full), gain_narrow, bias_narrow))
    mixed = dense(first, mixing_full)
    second = jax.nn.relu(batch_norm(stencil(mixed, depth_full, keep_mask), gain_depth, bias_depth))
    return jax.nn.relu(batch_norm(dense(second, expand_full), gain_wide, bias_wide) + field)

def reference(inputs, cotangent, clip_index, reduce_weight, mixing_weight, depthwise, expand_weight, gain_narrow, bias_narrow, gain_depth, bias_depth, gain_wide, bias_wide, momentum_reduce_weight, momentum_mixing_weight, momentum_depthwise, momentum_expand_weight, momentum_gain_narrow, momentum_bias_narrow, momentum_gain_depth, momentum_bias_depth, momentum_gain_wide, momentum_bias_wide):
    keep_mask = keep_table(clip_index)
    params = (reduce_weight, mixing_weight, depthwise, expand_weight, gain_narrow, bias_narrow, gain_depth, bias_depth, gain_wide, bias_wide)
    momenta = (momentum_reduce_weight, momentum_mixing_weight, momentum_depthwise, momentum_expand_weight, momentum_gain_narrow, momentum_bias_narrow, momentum_gain_depth, momentum_bias_depth, momentum_gain_wide, momentum_bias_wide)

    def forward(field, weights):
        for position in range(2):
            field = bottleneck(field, tuple((item[position] for item in weights)), keep_mask)
        return field
    block_out, pullback = jax.vjp(forward, inputs, params)
    gradient_inputs, grads = pullback(cotangent)
    clips = clip_index.shape[0] // 6
    labels = jnp.arange(clips, dtype=jnp.int32)
    one_hot = (clip_index.astype(jnp.int32)[None, :] == labels[:, None]).astype(jnp.float32)
    frame_sums = lax.optimization_barrier(jnp.sum(block_out, axis=(1, 2)))
    counts = lax.optimization_barrier(jnp.sum(one_hot, axis=1)) * (block_out.shape[1] * block_out.shape[2])
    clip_sums = lax.optimization_barrier(jnp.sum(one_hot[:, :, None] * frame_sums[None, :, :], axis=1))
    pooled = clip_sums / counts[:, None]
    velocity = [MOMENTUM * momenta[index] + grads[index] for index in range(10)]
    updated = [params[index] - LEARN_RATE * (grads[index] + MOMENTUM * velocity[index]) for index in range(10)]
    return (block_out, pooled, gradient_inputs, grads[0], grads[1], grads[2], grads[3], grads[4], grads[5], grads[6], grads[7], grads[8], grads[9], velocity[0], velocity[1], velocity[2], velocity[3], velocity[4], velocity[5], velocity[6], velocity[7], velocity[8], velocity[9], updated[0], updated[1], updated[2], updated[3], updated[4], updated[5], updated[6], updated[7], updated[8], updated[9])
```

```python
import functools

import jax
import jax.numpy as jnp
from jax import lax
from jax.experimental import pallas as pl
from jax.experimental.pallas import tpu as pltpu
from jax.sharding import PartitionSpec as P

EPSILON = 1e-05
MOMENTUM = 0.9
LEARN_RATE = 0.0001
HIGHEST = lax.Precision.HIGHEST
AX = ("dp", "fsdp")
F32 = jnp.float32
BF16 = jnp.bfloat16
MIB = 1 << 20

VM = pl.BlockSpec(memory_space=pltpu.VMEM)
SM = pl.BlockSpec(memory_space=pltpu.SMEM)


def params(mib):
    return pltpu.CompilerParams(vmem_limit_bytes=mib * MIB)


def dot6(left, right):
    return jnp.dot(left, right, precision=HIGHEST, preferred_element_type=F32)


def dot6_rt(left, right):
    return lax.dot_general(
        left, right, (((1,), (1,)), ((), ())), precision=HIGHEST, preferred_element_type=F32
    )


def split2(value):
    high = value.astype(BF16)
    return high, (value - high.astype(F32)).astype(BF16)


def dot3(left, right):
    lh, ll = left
    rh, rl = right
    mm = functools.partial(jnp.dot, preferred_element_type=F32)
    return mm(lh, rh) + (mm(lh, rl) + mm(ll, rh))


def columns_of(shape, width):
    col = lax.broadcasted_iota(jnp.int32, shape, len(shape) - 2)
    return col < width


def put_rows(st_ref, first, vec):
    for i in range(vec.shape[1] // 128):
        piece = vec[:, i * 128 : (i + 1) * 128]
        st_ref[:, first + i, :] = jnp.broadcast_to(piece, (st_ref.shape[0], 128))


def take_rows(st_ref, first, channels):
    return jnp.concatenate(
        [st_ref[:, first + i, :] for i in range(channels // 128)], axis=1
    )


def narrow_moments(st_ref, channels, local, total):
    k = channels // 128
    sums = take_rows(st_ref, 0, channels)
    squares = take_rows(st_ref, k, channels)
    mean = jnp.sum(sums, axis=0, keepdims=True) / total
    off = sums / local - mean
    var = (
        jnp.sum(squares, axis=0, keepdims=True)
        + local * jnp.sum(off * off, axis=0, keepdims=True)
    ) / total
    return mean, lax.rsqrt(var + EPSILON)


def sum_frames(frames, piece, channels):
    def step(f, acc):
        return acc + jnp.sum(piece(f), axis=0, keepdims=True)

    return lax.fori_loop(0, frames, step, jnp.zeros((1, channels), F32))


def local_moments(field_ref, width, local):
    frames, rows, padded, channels = field_ref.shape
    size = rows * padded
    total = sum_frames(frames, lambda f: field_ref[f].reshape(size, channels), channels)
    mean = total / local

    def squares(f):
        value = field_ref[f]
        value = jnp.where(columns_of(value.shape, width), value - mean, 0.0)
        return (value * value).reshape(size, channels)

    return total, sum_frames(frames, squares, channels)


def pad_columns(value, padded):
    rows, width, channels = value.shape
    if padded == width:
        return value
    return jnp.concatenate([value, jnp.zeros((rows, padded - width, channels), F32)], axis=1)


STAGES = ((3, 4), (1, 2), (0,))


def slot_mask(slot):
    mask = 0
    for bits in STAGES:
        mask |= (slot & ((1 << len(bits)) - 1)) << bits[0]
        slot >>= len(bits)
    return mask


def order_rows(slots_ref, out_ref, me, lanes=slice(None)):
    count, rows, _ = slots_ref.shape
    for s in range(count):
        where = pl.multiple_of(jnp.bitwise_xor(me, slot_mask(s)) * rows, rows)
        out_ref[pl.ds(where, rows), :] = slots_ref[s, :, lanes]


def k_first(width, me_ref, x_ref, w_ref, a_ref, st_ref, w_scr):
    f = pl.program_id(0)
    frames, rows, padded, narrow = a_ref.shape
    slotted = len(w_ref.shape) == 3

    @pl.when(f == 0)
    def _():
        if slotted:
            order_rows(w_ref, w_scr, me_ref[0])
        else:
            w_scr[...] = w_ref[...]

    x = pad_columns(x_ref[0], padded)
    a = dot6(x.reshape(rows * padded, x.shape[2]), w_scr[...])
    a_ref[f] = a.reshape(rows, padded, narrow)

    @pl.when(f == frames - 1)
    def _():
        total, squares = local_moments(a_ref, width, float(frames * rows * width))
        put_rows(st_ref, 0, total)
        put_rows(st_ref, narrow // 128, squares)


def frame_taps(k_ref, keep_ref, f, frames, lanes, flipped):
    taps = []
    for o in range(3):
        keep = keep_ref[o * frames + f]
        rows = []
        for p in range(3):
            cols = []
            for q in range(3):
                tap = 9 * o + 3 * p + q
                if flipped:
                    tap = 26 - tap
                cols.append(k_ref[tap : tap + 1, lanes] * keep)
            rows.append(cols)
        taps.append(rows)
    return taps


def shifted(value, padded):
    return pltpu.roll(value, 1, 0), value, pltpu.roll(value, padded - 1, 0)


def stencil_into(mp_ref, k_ref, keep_ref, store, frames, rows, padded, flipped):
    for half in range(mp_ref.shape[3] // 128):
        lanes = slice(half * 128, half * 128 + 128)

        def frame(f, carry):
            taps = frame_taps(k_ref, keep_ref, f, frames, lanes, flipped)

            def row(j, older, old):
                new = jnp.zeros((padded, 128), F32)
                for o in range(3):
                    views = shifted(mp_ref[f + o, j, :, lanes], padded)
                    for q in range(3):
                        older = older + views[q] * taps[o][2][q]
                        old = old + views[q] * taps[o][1][q]
                        new = new + views[q] * taps[o][0][q]
                return older, old, new

            zero = jnp.zeros((padded, 128), F32)
            _, _, new = row(0, zero, zero)
            _, old, new = row(1, zero, new)

            def step(j, accs):
                done, old, new = row(j, accs[0], accs[1])
                store(f, j - 2, lanes, done)
                return old, new

            lax.fori_loop(2, rows + 2, step, (old, new))
            return carry

        lax.fori_loop(0, frames, frame, 0)


def k_mix(width, total, keep_ref, a_ref, hp_ref, hn_ref, up_ref, dn_ref, cu_ref, cd_ref, st_in,
          w_ref, k_ref, vec_ref, c_ref, m_ref, mom_ref, st_ref, w_scr, mp_ref, *, slot_lanes):
    frames, rows, padded, narrow = a_ref.shape
    local = float(frames * rows * width)
    size = rows * padded
    top = keep_ref[3 * frames]
    bottom = keep_ref[3 * frames + 1]
    if slot_lanes:
        order_rows(w_ref, w_scr, keep_ref[3 * frames + 2].astype(jnp.int32), slice(0, narrow))
    else:
        w_scr[...] = w_ref[...]
    mean, inverse = narrow_moments(st_in, narrow, local, total)
    mom_ref[0:1, :] = mean
    mom_ref[1:2, :] = inverse
    scale = vec_ref[0:1, :] * inverse
    shift = vec_ref[1:2, :]

    def mixed(value):
        r = jnp.maximum((value - mean) * scale + shift, 0.0)
        r = jnp.where(columns_of(r.shape, width), r, 0.0)
        m = dot6(r.reshape(-1, narrow), w_scr[...])
        return m.reshape(value.shape)

    def own(f, carry):
        m = mixed(a_ref[f])
        m_ref[f] = m
        mp_ref[f + 1, 1 : rows + 1] = m
        return carry

    lax.fori_loop(0, frames, own, 0)
    mp_ref[0, 1 : rows + 1] = mixed(hp_ref[0])
    mp_ref[frames + 1, 1 : rows + 1] = mixed(hn_ref[0])
    mp_ref[1 : frames + 1, 0] = mixed(up_ref[:, 0]) * top
    mp_ref[1 : frames + 1, rows + 1] = mixed(dn_ref[:, 0]) * bottom
    cu = mixed(cu_ref[:, 0]) * top
    cd = mixed(cd_ref[:, 0]) * bottom
    mp_ref[0, 0] = cu[0]
    mp_ref[frames + 1, 0] = cu[1]
    mp_ref[0, rows + 1] = cd[0]
    mp_ref[frames + 1, rows + 1] = cd[1]

    def store(f, r, lanes, value):
        c_ref[f, r, :, lanes] = jnp.where(columns_of(value.shape, width), value, 0.0)

    stencil_into(mp_ref, k_ref, keep_ref, store, frames, rows, padded, False)
    total_c, squares = local_moments(c_ref, width, local)
    put_rows(st_ref, 0, total_c)
    put_rows(st_ref, narrow // 128, squares)


def second_act(c, mom, vec):
    return (c - mom[0:1, :]) * (vec[2:3, :] * mom[1:2, :]) + vec[3:4, :]


def k_expand(width, total, me_ref, c_ref, st_in, w_ref, vec_ref, e_ref, mom_ref, off_ref, st_ref,
             w_out, s_ref, sums_scr, *, slot_lanes):
    f = pl.program_id(0)
    frames, rows, padded, narrow = c_ref.shape
    wide = e_ref.shape[3]
    local = float(frames * rows * width)
    size = rows * padded

    @pl.when(f == 0)
    def _():
        if slot_lanes:
            order_rows(w_ref, w_out, me_ref[0], slice(narrow, narrow + wide))
        else:
            w_out[...] = w_ref[...]
        mean, inverse = narrow_moments(st_in, narrow, local, total)
        mom_ref[0:1, :] = mean
        mom_ref[1:2, :] = inverse
        mom = mom_ref[...]

        def act(g, acc):
            s = jnp.maximum(second_act(c_ref[g], mom, vec_ref), 0.0)
            s = jnp.where(columns_of(s.shape, width), s, 0.0)
            s_ref[g] = s
            return acc + jnp.sum(s.reshape(size, narrow), axis=0, keepdims=True)

        sums = lax.fori_loop(0, frames, act, jnp.zeros((1, narrow), F32))
        sums_scr[0:1, :] = sums / local
        put_rows(st_ref, 0, sums)
        off_ref[...] = dot6(jnp.broadcast_to(sums / local, (8, narrow)), w_out[...])
        sums_scr[1:2, :] = jnp.zeros((1, narrow), F32)

    s = s_ref[f]
    s = jnp.where(columns_of(s.shape, width), s - sums_scr[0:1, :], 0.0)
    e = dot6(s.reshape(size, narrow), w_out[...])
    e_ref[0] = e.reshape(rows, padded, wide)
    part = jnp.sum(e * e, axis=0, keepdims=True)
    k = narrow // 128

    @pl.when(f == 0)
    def _():
        put_rows(st_ref, k, part)

    @pl.when(f > 0)
    def _():
        for i in range(wide // 128):
            st_ref[:, k + i, :] = st_ref[:, k + i, :] + jnp.broadcast_to(
                part[:, i * 128 : (i + 1) * 128], (st_ref.shape[0], 128)
            )


def wide_moments(st_in, w, off, gain, bias, narrow, wide, local, total):
    k = narrow // 128
    s_means = take_rows(st_in, 0, narrow) / local
    squares = take_rows(st_in, k, wide)
    e_means = dot6(s_means, w)
    s_mean = jnp.mean(s_means, axis=0, keepdims=True)
    mean = jnp.mean(e_means, axis=0, keepdims=True)
    away = e_means - mean
    var = (
        jnp.sum(squares, axis=0, keepdims=True)
        + local * jnp.sum(away * away, axis=0, keepdims=True)
    ) / total
    inverse = lax.rsqrt(var + EPSILON)
    scale = gain * inverse
    return scale, (off - mean) * scale + bias, inverse, s_mean


def k_join(width, total, e_ref, x_ref, st_in, off_ref, w_ref, vecw_ref, wr_ref, x_out, a_ref,
           momw_ref, smean_ref, st_ref):
    f = pl.program_id(0)
    frames, rows, padded, narrow = a_ref.shape
    wide = e_ref.shape[3]
    local = float(frames * rows * width)
    size = rows * padded

    @pl.when(f == 0)
    def _():
        scale, shift, inverse, s_mean = wide_moments(
            st_in, w_ref[...], off_ref[0:1, :], vecw_ref[0:1, :], vecw_ref[1:2, :], narrow, wide,
            local, total,
        )
        momw_ref[0:1, :] = scale
        momw_ref[1:2, :] = shift
        momw_ref[2:3, :] = inverse
        smean_ref[0:1, :] = s_mean

    x = pad_columns(x_ref[0], padded)
    z = e_ref[0] * momw_ref[0:1, :] + momw_ref[1:2, :] + x
    z = jnp.where(columns_of(z.shape, width), jnp.maximum(z, 0.0), 0.0)
    x_out[0] = z
    a = dot6(z.reshape(size, wide), wr_ref[...])
    a_ref[f] = a.reshape(rows, padded, narrow)

    @pl.when(f == frames - 1)
    def _():
        total_a, squares = local_moments(a_ref, width, local)
        put_rows(st_ref, 0, total_a)
        put_rows(st_ref, narrow // 128, squares)


def prepare_wide(width, c_ref, mom_ref, vec_ref, smean_ref, w_ref, alpha, st_h, st_l, wt_h, wt_l):
    frames, rows, padded, narrow = c_ref.shape
    size = rows * padded
    mom = mom_ref[...]
    center = smean_ref[0:1, :]

    def act(g, carry):
        s = jnp.maximum(second_act(c_ref[g], mom, vec_ref), 0.0) - center
        s = jnp.where(columns_of(s.shape, width), s, 0.0)
        high, low = split2(s.reshape(size, narrow).T)
        st_h[g] = high
        st_l[g] = low
        return carry

    lax.fori_loop(0, frames, act, 0)
    high, low = split2((w_ref[...] * alpha).T)
    wt_h[...] = high
    wt_l[...] = low


def wide_step(gz, f, u_ref, p_ref, bias_acc, st_h, st_l, wt_h, wt_l):
    size, wide = gz.shape
    _, rows, padded, narrow = u_ref.shape
    parts = split2(gz)
    u = dot3(parts, (wt_h[...], wt_l[...]))
    u_ref[f] = u.reshape(rows, padded, narrow)
    p = dot3((st_h[f], st_l[f]), parts)
    part = jnp.sum(gz, axis=0, keepdims=True)

    @pl.when(f == 0)
    def _():
        p_ref[...] = p
        bias_acc[0:1, :] = part

    @pl.when(f > 0)
    def _():
        p_ref[...] = p_ref[...] + p
        bias_acc[0:1, :] = bias_acc[0:1, :] + part


def wide_finish(p_ref, w_ref, inverse, bias_acc, st_ref):
    wide = w_ref.shape[1]
    gain_sum = jnp.sum(p_ref[...] * w_ref[...], axis=0, keepdims=True) * inverse
    put_rows(st_ref, 0, bias_acc[0:1, :])
    put_rows(st_ref, wide // 128, gain_sum)


def k_turn(width, total, e_ref, x_ref, cot_ref, st_in, off_ref, w_ref, vecw_ref, c_ref, mom_ref,
           vec_ref, out_ref, gz_ref, u_ref, p_ref, momw_ref, smean_ref, pool_ref, st_ref,
           st_h, st_l, wt_h, wt_l, bias_acc):
    f = pl.program_id(0)
    frames, rows, padded, narrow = c_ref.shape
    wide = e_ref.shape[3]
    local = float(frames * rows * width)
    size = rows * padded

    @pl.when(f == 0)
    def _():
        scale, shift, inverse, s_mean = wide_moments(
            st_in, w_ref[...], off_ref[0:1, :], vecw_ref[0:1, :], vecw_ref[1:2, :], narrow, wide,
            local, total,
        )
        momw_ref[0:1, :] = scale
        momw_ref[1:2, :] = shift
        momw_ref[2:3, :] = inverse
        smean_ref[0:1, :] = s_mean
        prepare_wide(width, c_ref, mom_ref, vec_ref, smean_ref, w_ref, scale, st_h, st_l, wt_h, wt_l)

    z = e_ref[0] * momw_ref[0:1, :] + momw_ref[1:2, :] + x_ref[0]
    out = jnp.maximum(z, 0.0)
    out_ref[0] = out[:, :width, :]
    keep = columns_of(z.shape, width)
    pooled = jnp.where(keep, out, 0.0).reshape(size, wide)
    pool_ref[0] = jnp.broadcast_to(jnp.sum(pooled, axis=0, keepdims=True), (8, wide))
    cot = pad_columns(cot_ref[0], padded)
    gz = jnp.where(jnp.logical_and(z > 0.0, keep), cot, 0.0)
    gz_ref[0] = gz
    wide_step(gz.reshape(size, wide), f, u_ref, p_ref, bias_acc, st_h, st_l, wt_h, wt_l)

    @pl.when(f == frames - 1)
    def _():
        wide_finish(p_ref, w_ref, momw_ref[2:3, :], bias_acc, st_ref)


def k_second(width, total, u_ref, c_ref, st_in, w_ref, momw_ref, smean_ref, mom_ref, vec_ref, n_ref,
             gw_ref, st_ref):
    frames, rows, padded, narrow = u_ref.shape
    wide = w_ref.shape[1]
    size = rows * padded
    k = wide // 128
    bias_sum = jnp.sum(take_rows(st_in, 0, wide), axis=0, keepdims=True)
    gain_sum = jnp.sum(take_rows(st_in, k, wide), axis=0, keepdims=True)
    gw_ref[0:1, :] = gain_sum
    gw_ref[1:2, :] = bias_sum
    alpha = momw_ref[0:1, :]
    w = w_ref[...]
    q = dot6_rt(w * (alpha * momw_ref[2:3, :] * (gain_sum / total)), w)
    d = dot6_rt(jnp.broadcast_to(alpha * (bias_sum / total), (8, wide)), w)[0:1, :]
    mom = mom_ref[...]
    center = smean_ref[0:1, :]

    def step(f, accs):
        c = c_ref[f]
        y = second_act(c, mom, vec_ref)
        keep = columns_of(c.shape, width)
        s = jnp.where(keep, jnp.maximum(y, 0.0) - center, 0.0)
        corr = dot6(s.reshape(size, narrow), q).reshape(rows, padded, narrow)
        n = jnp.where(jnp.logical_and(y > 0.0, keep), u_ref[f] - corr - d, 0.0)
        n_ref[f] = n
        xhat = (c - mom[0:1, :]) * mom[1:2, :]
        return (
            accs[0] + jnp.sum(n.reshape(size, narrow), axis=0, keepdims=True),
            accs[1] + jnp.sum((n * xhat).reshape(size, narrow), axis=0, keepdims=True),
        )

    zero = jnp.zeros((1, narrow), F32)
    bias_acc, gain_acc = lax.fori_loop(0, frames, step, (zero, zero))
    put_rows(st_ref, 0, bias_acc)
    put_rows(st_ref, narrow // 128, gain_acc)


def k_expand_grad(width, total, c_ref, p_ref, w_ref, gw_ref, momw_ref, smean_ref, mom_ref, vec_ref,
                  dw_ref):
    frames, rows, padded, narrow = c_ref.shape
    size = rows * padded
    mom = mom_ref[...]
    center = smean_ref[0:1, :]

    def step(f, accs):
        y = second_act(c_ref[f], mom, vec_ref)
        s = jnp.where(columns_of(y.shape, width), jnp.maximum(y, 0.0) - center, 0.0)
        s = s.reshape(size, narrow)
        turned = s.T
        ones = jnp.broadcast_to(jnp.sum(turned, axis=1, keepdims=True), (narrow, 128))
        return accs[0] + dot3(split2(turned), split2(s)), accs[1] + ones

    gram, sums = lax.fori_loop(
        0, frames, step, (jnp.zeros((narrow, narrow), F32), jnp.zeros((narrow, 128), F32))
    )
    alpha = momw_ref[0:1, :]
    gamma = gw_ref[0:1, :] / total * momw_ref[2:3, :]
    beta = gw_ref[1:2, :] / total
    seen = dot3(split2(gram), split2(w_ref[...]))
    dw_ref[...] = alpha * (p_ref[...] - sums[:, 0:1] * beta - seen * gamma)


def k_first_back(width, total, keep_ref, n_ref, np_ref, nn_ref, nu_ref, nd_ref, ncu_ref, ncd_ref,
                 c_ref, cp_ref, cn_ref, cup_ref, cdn_ref, ccu_ref, ccd_ref, st_in, a_ref, w_ref,
                 k_ref, vec_ref, mom1_ref, mom2_ref, gm_ref, n1_ref, gcp_ref, gd_ref, st_ref,
                 wt_h, wt_l):
    frames, rows, padded, narrow = n_ref.shape
    size = rows * padded
    top = keep_ref[3 * frames]
    bottom = keep_ref[3 * frames + 1]
    k = narrow // 128
    bias_sum = jnp.sum(take_rows(st_in, 0, narrow), axis=0, keepdims=True)
    gain_sum = jnp.sum(take_rows(st_in, k, narrow), axis=0, keepdims=True)
    gd_ref[0:1, :] = gain_sum
    gd_ref[1:2, :] = bias_sum
    mom2 = mom2_ref[...]
    alpha = vec_ref[2:3, :] * mom2[1:2, :]
    beta = bias_sum / total
    gamma = gain_sum / total

    def back(n, c):
        xhat = (c - mom2[0:1, :]) * mom2[1:2, :]
        g = alpha * (n - beta - xhat * gamma)
        return jnp.where(columns_of(g.shape, width), g, 0.0)

    def own(f, carry):
        gcp_ref[f + 1, 1 : rows + 1] = back(n_ref[f], c_ref[f])
        return carry

    lax.fori_loop(0, frames, own, 0)
    gcp_ref[0, 1 : rows + 1] = back(np_ref[0], cp_ref[0])
    gcp_ref[frames + 1, 1 : rows + 1] = back(nn_ref[0], cn_ref[0])
    gcp_ref[1 : frames + 1, 0] = back(nu_ref[:, 0], cup_ref[:, 0]) * top
    gcp_ref[1 : frames + 1, rows + 1] = back(nd_ref[:, 0], cdn_ref[:, 0]) * bottom
    cu = back(ncu_ref[:, 0], ccu_ref[:, 0]) * top
    cd = back(ncd_ref[:, 0], ccd_ref[:, 0]) * bottom
    gcp_ref[0, 0] = cu[0]
    gcp_ref[frames + 1, 0] = cu[1]
    gcp_ref[0, rows + 1] = cd[0]
    gcp_ref[frames + 1, rows + 1] = cd[1]

    def store(f, r, lanes, value):
        gm_ref[f, r, :, lanes] = jnp.where(columns_of(value.shape, width), value, 0.0)

    stencil_into(gcp_ref, k_ref, keep_ref, store, frames, rows, padded, True)
    high, low = split2(w_ref[...].T)
    wt_h[...] = high
    wt_l[...] = low
    mom1 = mom1_ref[...]
    scale1 = vec_ref[0:1, :] * mom1[1:2, :]

    def step(f, accs):
        gr = dot3(split2(gm_ref[f].reshape(size, narrow)), (wt_h[...], wt_l[...]))
        off = a_ref[f] - mom1[0:1, :]
        y = off * scale1 + vec_ref[1:2, :]
        keep = jnp.logical_and(y > 0.0, columns_of(y.shape, width))
        n = jnp.where(keep, gr.reshape(rows, padded, narrow), 0.0)
        n1_ref[f] = n
        return (
            accs[0] + jnp.sum(n.reshape(size, narrow), axis=0, keepdims=True),
            accs[1] + jnp.sum((n * (off * mom1[1:2, :])).reshape(size, narrow), axis=0, keepdims=True),
        )

    zero = jnp.zeros((1, narrow), F32)
    bias_acc, gain_acc = lax.fori_loop(0, frames, step, (zero, zero))
    put_rows(st_ref, 0, bias_acc)
    put_rows(st_ref, k, gain_acc)


def k_mix_grads(width, keep_ref, gcp_ref, m_ref, gm_ref, a_ref, vec_ref, mom1_ref, dk_ref, dm_ref,
                acc_ref):
    frames, rows, padded, narrow = m_ref.shape
    size = rows * padded
    mom1 = mom1_ref[...]
    scale1 = vec_ref[0:1, :] * mom1[1:2, :]

    def mixing(f, acc):
        y = (a_ref[f] - mom1[0:1, :]) * scale1 + vec_ref[1:2, :]
        r = jnp.where(columns_of(y.shape, width), jnp.maximum(y, 0.0), 0.0)
        turned = r.reshape(size, narrow).T
        return acc + dot3(split2(turned), split2(gm_ref[f].reshape(size, narrow)))

    dm_ref[...] = lax.fori_loop(0, frames, mixing, jnp.zeros((narrow, narrow), F32))
    acc_ref[...] = jnp.zeros(acc_ref.shape, F32)
    for half in range(narrow // 128):
        lanes = slice(half * 128, half * 128 + 128)

        def frame(f, carry):
            for o in range(3):
                keep = keep_ref[o * frames + f]

                def row(j, accs):
                    views = shifted(gcp_ref[f + o, j, :, lanes], padded)
                    new = []
                    for p in range(3):
                        r = j - p
                        inside = jnp.logical_and(r >= 0, r < rows).astype(F32)
                        m = m_ref[f, jnp.clip(r, 0, rows - 1), :, lanes] * inside
                        for q in range(3):
                            prod = (m * views[q]).reshape(padded // 8, 8, 128)
                            new.append(accs[3 * p + q] + jnp.sum(prod, axis=0))
                    return tuple(new)

                zero = jnp.zeros((8, 128), F32)
                accs = lax.fori_loop(0, rows + 2, row, (zero,) * 9)
                for i in range(9):
                    tap = 26 - (9 * o + i)
                    acc_ref[tap, :, lanes] = acc_ref[tap, :, lanes] + accs[i] * keep
            return carry

        lax.fori_loop(0, frames, frame, 0)
    for tap in range(27):
        dk_ref[tap : tap + 1, :] = jnp.sum(acc_ref[tap], axis=0, keepdims=True)
    dk_ref[27:32, :] = jnp.zeros((5, narrow), F32)


def first_norm_back(width, total, n1_ref, a_ref, st_in, vec_ref, mom1_ref, gn_ref, ga_ref):
    frames, rows, padded, narrow = n1_ref.shape
    k = narrow // 128
    bias_sum = jnp.sum(take_rows(st_in, 0, narrow), axis=0, keepdims=True)
    gain_sum = jnp.sum(take_rows(st_in, k, narrow), axis=0, keepdims=True)
    gn_ref[0:1, :] = gain_sum
    gn_ref[1:2, :] = bias_sum
    mom1 = mom1_ref[...]
    alpha = vec_ref[0:1, :] * mom1[1:2, :]

    def step(f, carry):
        xhat = (a_ref[f] - mom1[0:1, :]) * mom1[1:2, :]
        g = alpha * (n1_ref[f] - bias_sum / total - xhat * (gain_sum / total))
        ga_ref[f] = jnp.where(columns_of(g.shape, width), g, 0.0)
        return carry

    lax.fori_loop(0, frames, step, 0)


def input_grads(ga, x, f, wt_h, wt_l, dwt):
    turned = split2(ga.T)
    dx = dot3(split2(ga), (wt_h[...], wt_l[...]))
    dw = dot3(turned, split2(x))

    @pl.when(f == 0)
    def _():
        dwt[...] = dw

    @pl.when(f > 0)
    def _():
        dwt[...] = dwt[...] + dw

    return dx


def k_between(width, total, n1_ref, a_ref, st_in, vec_ref, mom1_ref, wr_ref, x_ref, gz_in, c_ref,
              mom2_ref, vec2_ref, w_ref, momw_ref, smean_ref, gz_ref, u_ref, p_ref, dw_ref, gn_ref,
              st_ref, ga_ref, wrt_h, wrt_l, dwt, st_h, st_l, wt_h, wt_l, bias_acc):
    f = pl.program_id(0)
    frames, rows, padded, narrow = n1_ref.shape
    wide = x_ref.shape[3]
    size = rows * padded

    @pl.when(f == 0)
    def _():
        first_norm_back(width, total, n1_ref, a_ref, st_in, vec_ref, mom1_ref, gn_ref, ga_ref)
        high, low = split2(wr_ref[...].T)
        wrt_h[...] = high
        wrt_l[...] = low
        prepare_wide(width, c_ref, mom2_ref, vec2_ref, smean_ref, w_ref, momw_ref[0:1, :], st_h, st_l,
                     wt_h, wt_l)

    x = x_ref[0].reshape(size, wide)
    gy = input_grads(ga_ref[f].reshape(size, narrow), x, f, wrt_h, wrt_l, dwt)
    gy = gy + gz_in[0].reshape(size, wide)
    gz = jnp.where(x > 0.0, gy, 0.0)
    gz_ref[0] = gz.reshape(rows, padded, wide)
    wide_step(gz, f, u_ref, p_ref, bias_acc, st_h, st_l, wt_h, wt_l)

    @pl.when(f == frames - 1)
    def _():
        wide_finish(p_ref, w_ref, momw_ref[2:3, :], bias_acc, st_ref)
        dw_ref[...] = dwt[...].T


def k_last(width, total, n1_ref, a_ref, st_in, vec_ref, mom1_ref, wr_ref, x_ref, gz_in, gx_ref,
           dw_ref, gn_ref, ga_ref, wrt_h, wrt_l, dwt):
    f = pl.program_id(0)
    frames, rows, padded, narrow = n1_ref.shape
    wide = gz_in.shape[3]
    size = rows * padded

    @pl.when(f == 0)
    def _():
        first_norm_back(width, total, n1_ref, a_ref, st_in, vec_ref, mom1_ref, gn_ref, ga_ref)
        high, low = split2(wr_ref[...].T)
        wrt_h[...] = high
        wrt_l[...] = low

    x = pad_columns(x_ref[0], padded).reshape(size, wide)
    gy = input_grads(ga_ref[f].reshape(size, narrow), x, f, wrt_h, wrt_l, dwt)
    gy = gy.reshape(rows, padded, wide) + gz_in[0]
    gx_ref[0] = gy[:, :width, :]

    @pl.when(f == frames - 1)
    def _():
        dw_ref[...] = dwt[...].T


def exchange(rows):
    return lax.all_to_all(rows, AX, 0, 0)


def perm(step, shape):
    dp, fs = shape
    pairs = []
    for i in range(dp):
        for j in range(fs):
            a, b = i + step[0], j + step[1]
            if 0 <= a < dp and 0 <= b < fs:
                pairs.append((i * fs + j, a * fs + b))
    return pairs


def halo(field, shape):
    frames, rows = field.shape[0], field.shape[1]
    first, last = field[0:1], field[frames - 1 :]
    move = lambda value, step: lax.ppermute(value, AX, perm(step, shape))
    before = move(last, (1, 0))
    after = move(first, (-1, 0))
    if shape[1] == 2:
        upper = lax.axis_index("fsdp") == 0
        swap = [(i, i ^ 1) for i in range(shape[0] * 2)]
        edge = jnp.where(upper, field[:, rows - 1 :], field[:, 0:1])
        row = lax.ppermute(edge, AX, swap)
        fwd = [(i, (i + 2) ^ 1) for i in range(shape[0] * 2 - 2)]
        bwd = [(i, (i - 2) ^ 1) for i in range(2, shape[0] * 2)]
        corner = jnp.concatenate(
            [lax.ppermute(edge[frames - 1 :], AX, fwd), lax.ppermute(edge[0:1], AX, bwd)]
        )
        return before, after, row, row, corner, corner
    above = move(field[:, rows - 1 :], (0, 1))
    below = move(field[:, 0:1], (0, -1))
    up = jnp.concatenate(
        [move(last[:, rows - 1 :], (1, 1)), move(first[:, rows - 1 :], (-1, 1))]
    )
    down = jnp.concatenate([move(last[:, 0:1], (1, -1)), move(first[:, 0:1], (-1, -1))])
    return before, after, above, below, up, down


def tree_gather(part, devices):
    stack = part[None]
    for bits in STAGES:
        low = bits[0]
        pieces = [stack]
        for step in range(1, 1 << len(bits)):
            mask = step << low
            pieces.append(lax.ppermute(stack, AX, [(i, i ^ mask) for i in range(devices)]))
        stack = jnp.concatenate(pieces, axis=0)
    return stack


def owner_sums(local, devices):
    parts = local.reshape((devices, local.shape[0] // devices) + local.shape[1:])
    return jnp.sum(lax.all_to_all(parts, AX, 0, 0), axis=0)


def body(inputs, cotangent, clip_index, *args):
    weights, momenta = args[:10], args[10:]
    frames, rows, width, wide = inputs.shape
    narrow = weights[0].shape[2]
    padded = -(-width // 8) * 8
    shape = (lax.axis_size("dp"), lax.axis_size("fsdp"))
    devices = shape[0] * shape[1]
    rank = lax.axis_index(AX)
    total = float(frames * rows * width * devices)
    size = rows * padded
    slotted = devices == 32

    share_n, share_w = weights[1].shape[1], weights[6 + 2].shape[1]
    small = jnp.concatenate(
        [weights[2].reshape(-1)]
        + [weights[i].reshape(-1) for i in (4, 5, 6, 7, 8, 9)]
    )
    length = small.shape[0]
    lanes = -(-length // 128) * 128
    small = jnp.pad(small, (0, lanes - length)).reshape(lanes // 128, 128)
    small = lax.all_to_all(jnp.broadcast_to(small[None], (devices,) + small.shape), AX, 0, 0)
    small = small.reshape(devices, lanes)

    def unpack(first, inner):
        n = 1
        for v in inner:
            n *= v
        return first + n, small[:, first : first + n].reshape((devices,) + inner)

    at, taps = unpack(0, (2, share_n, 27))
    taps = jnp.pad(taps.transpose(1, 3, 0, 2).reshape(2, 27, narrow), ((0, 0), (0, 5), (0, 0)))
    rows_n = []
    for _ in range(4):
        at, vec = unpack(at, (2, share_n))
        rows_n.append(vec.transpose(1, 0, 2).reshape(2, narrow))
    rows_w = []
    for _ in range(2):
        at, vec = unpack(at, (2, share_w))
        rows_w.append(vec.transpose(1, 0, 2).reshape(2, wide))
    vec_n = jnp.pad(jnp.stack(rows_n, axis=1), ((0, 0), (0, 4), (0, 0)))
    vec_w = jnp.pad(jnp.stack(rows_w, axis=1), ((0, 0), (0, 6), (0, 0)))

    edge = jnp.full((1,), -1, jnp.int32)
    window = lax.dynamic_slice_in_dim(
        jnp.concatenate([edge, clip_index, edge]), lax.axis_index("dp") * frames, frames + 2
    )
    centre = window[1:-1]
    flags = jnp.concatenate(
        [
            (window[:-2] == centre).astype(F32),
            jnp.ones((frames,), F32),
            (window[2:] == centre).astype(F32),
            (lax.axis_index("fsdp") > 0).astype(F32)[None],
            (lax.axis_index("fsdp") < shape[1] - 1).astype(F32)[None],
            rank.astype(F32)[None],
        ]
    )
    me = rank.astype(jnp.int32)[None]

    gather = lambda part: lax.all_gather(part, AX, axis=0, tiled=True)
    if slotted:
        wr0 = tree_gather(weights[0][0], devices)
        pair0 = tree_gather(
            jnp.concatenate([weights[1][0], weights[3][0]], axis=1), devices
        )
        mix_w0 = exp_w0 = pair0
    else:
        wr0 = gather(weights[0][0])
        mix_w0, exp_w0 = gather(weights[1][0]), gather(weights[3][0])
    later = jnp.concatenate(
        [
            weights[0][1].reshape(-1),
            weights[1][0].reshape(-1),
            weights[1][1].reshape(-1),
            weights[3][1].reshape(-1),
        ]
    ).reshape(-1, 128)
    later = lax.all_gather(later, AX, axis=0, tiled=False).reshape(devices, -1)

    def unpack_later(first, shp):
        n = shp[0] * shp[1]
        return first + n, later[:, first : first + n].reshape(devices * shp[0], shp[1])

    at, wr1 = unpack_later(0, weights[0].shape[1:])
    at, wm0 = unpack_later(at, weights[1].shape[1:])
    at, wm1 = unpack_later(at, weights[1].shape[1:])
    at, we1 = unpack_later(at, weights[3].shape[1:])

    sds = jax.ShapeDtypeStruct
    field_n = sds((frames, rows, padded, narrow), F32)
    field_w = sds((frames, rows, padded, wide), F32)
    stat_n = sds((devices, 2 * narrow // 128, 128), F32)
    stat_e = sds((devices, (narrow + wide) // 128, 128), F32)
    stat_w = sds((devices, 2 * wide // 128, 128), F32)
    mom_n = sds((8, narrow), F32)
    mom_w = sds((8, wide), F32)
    outer = lambda lead, last: pl.BlockSpec((1, lead, last, wide), lambda f: (f, 0, 0, 0))
    whole = lambda s: pl.BlockSpec(s.shape, lambda f: (0,) * len(s.shape))
    scr = pltpu.VMEM
    cst = functools.partial(pl.CostEstimate, transcendentals=0)
    flop_w = 2 * frames * size * narrow * wide

    def first(x, w):
        return pl.pallas_call(
            functools.partial(k_first, width),
            grid=(frames,),
            in_specs=[SM, outer(rows, width), whole(w)],
            out_specs=(whole(field_n), whole(stat_n)),
            out_shape=(field_n, stat_n),
            scratch_shapes=[scr((wide, narrow), F32)],
            compiler_params=params(30),
            cost_estimate=cst(flops=6 * flop_w, bytes_accessed=4 * x.size),
            name="first",
        )(me, x, w)

    def mix(block, a, halos, st, w):
        return pl.pallas_call(
            functools.partial(k_mix, width, total, slot_lanes=len(w.shape) == 3),
            in_specs=[SM] + [VM] * 11,
            out_specs=(VM,) * 4,
            out_shape=(field_n, field_n, mom_n, stat_n),
            scratch_shapes=[
                scr((narrow, narrow), F32),
                scr((frames + 2, rows + 2, padded, narrow), F32),
            ],
            compiler_params=params(30),
            cost_estimate=cst(flops=6 * flop_w, bytes_accessed=8 * a.size),
            name="mix",
        )(flags, a, *halos, st, w, taps[block], vec_n[block])

    def expand(block, c, st, w):
        return pl.pallas_call(
            functools.partial(k_expand, width, total, slot_lanes=len(w.shape) == 3),
            grid=(frames,),
            in_specs=[SM, whole(c), whole(st), whole(w), whole(mom_n)],
            out_specs=(outer(rows, padded), whole(mom_n), whole(mom_w), whole(stat_e),
                       whole(sds((narrow, wide), F32))),
            out_shape=(field_w, mom_n, mom_w, stat_e, sds((narrow, wide), F32)),
            scratch_shapes=[scr(field_n.shape, F32), scr((8, narrow), F32)],
            compiler_params=params(30),
            cost_estimate=cst(flops=6 * flop_w, bytes_accessed=4 * field_w.size),
            name="expand",
        )(me, c, st, w, vec_n[block])

    def join(block, e, x, st, off, we, wr):
        return pl.pallas_call(
            functools.partial(k_join, width, total),
            grid=(frames,),
            in_specs=[outer(rows, padded), outer(rows, x.shape[2]), whole(st), whole(off), whole(we),
                      whole(mom_w), whole(wr)],
            out_specs=(outer(rows, padded), whole(field_n), whole(mom_w), whole(mom_n),
                       whole(stat_n)),
            out_shape=(field_w, field_n, mom_w, mom_n, stat_n),
            compiler_params=params(40),
            cost_estimate=cst(flops=6 * flop_w, bytes_accessed=12 * field_w.size),
            name="join",
        )(e, x, st, off, we, vec_w[block], wr)

    turned = [
        scr((frames, narrow, size), BF16),
        scr((frames, narrow, size), BF16),
        scr((wide, narrow), BF16),
        scr((wide, narrow), BF16),
    ]

    def turn(e, x, st, off, we, c, mom2):
        pool = sds((frames, 8, wide), F32)
        return pl.pallas_call(
            functools.partial(k_turn, width, total),
            grid=(frames,),
            in_specs=[outer(rows, padded), outer(rows, padded), outer(rows, width), whole(st),
                      whole(off), whole(we), whole(mom_w), whole(c), whole(mom_n), whole(mom_n)],
            out_specs=(outer(rows, width), outer(rows, padded), whole(field_n), whole(we),
                       whole(mom_w), whole(mom_n), pl.BlockSpec((1, 8, wide), lambda f: (f, 0, 0)),
                       whole(stat_w)),
            out_shape=(sds(inputs.shape, F32), field_w, field_n, sds((narrow, wide), F32), mom_w,
                       mom_n, pool, stat_w),
            scratch_shapes=turned + [scr((8, wide), F32)],
            compiler_params=params(48),
            cost_estimate=cst(flops=6 * flop_w, bytes_accessed=20 * field_w.size),
            name="turn",
        )(e, x, cotangent, st, off, we, vec_w[1], c, mom2, vec_n[1])

    def second(block, u, c, st, we, momw, smean, mom2):
        return pl.pallas_call(
            functools.partial(k_second, width, total),
            in_specs=[VM] * 8,
            out_specs=(VM,) * 3,
            out_shape=(field_n, mom_w, stat_n),
            compiler_params=params(24),
            cost_estimate=cst(flops=2 * flop_w, bytes_accessed=12 * c.size),
            name="second",
        )(u, c, st, we, momw, smean, mom2, vec_n[block])

    def expand_grad(block, c, p, we, gw, momw, smean, mom2):
        return pl.pallas_call(
            functools.partial(k_expand_grad, width, total),
            in_specs=[VM] * 8,
            out_specs=VM,
            out_shape=sds((narrow, wide), F32),
            compiler_params=params(24),
            cost_estimate=cst(flops=flop_w, bytes_accessed=8 * c.size),
            name="expand_grad",
        )(c, p, we, gw, momw, smean, mom2, vec_n[block])

    def first_back(block, n, nh, c, ch, st, a, wm, mom1, mom2):
        return pl.pallas_call(
            functools.partial(k_first_back, width, total),
            in_specs=[SM] + [VM] * 21,
            out_specs=(VM,) * 5,
            out_shape=(field_n, field_n, sds((frames + 2, rows + 2, padded, narrow), F32), mom_n,
                       stat_n),
            scratch_shapes=[scr((narrow, narrow), BF16), scr((narrow, narrow), BF16)],
            compiler_params=params(40),
            cost_estimate=cst(flops=6 * flop_w, bytes_accessed=16 * c.size),
            name="first_back",
        )(flags, n, *nh, c, *ch, st, a, wm, taps[block], vec_n[block], mom1, mom2)

    def mix_grads(block, gcp, m, gm, a, mom1):
        return pl.pallas_call(
            functools.partial(k_mix_grads, width),
            in_specs=[SM] + [VM] * 6,
            out_specs=(VM,) * 2,
            out_shape=(sds((32, narrow), F32), sds((narrow, narrow), F32)),
            scratch_shapes=[scr((27, 8, narrow), F32)],
            compiler_params=params(30),
            cost_estimate=cst(flops=6 * flop_w, bytes_accessed=16 * a.size),
            name="mix_grads",
        )(flags, gcp, m, gm, a, vec_n[block], mom1)

    back = [scr(field_n.shape, F32), scr((narrow, wide), BF16), scr((narrow, wide), BF16),
            scr((narrow, wide), F32)]
    full_r = sds((wide, narrow), F32)

    def between(n1, a, st, mom1, wr, x, gz, c, mom2, we, momw, smean):
        return pl.pallas_call(
            functools.partial(k_between, width, total),
            grid=(frames,),
            in_specs=[whole(field_n), whole(field_n), whole(st), whole(mom_n), whole(mom_n),
                      whole(wr), outer(rows, padded), outer(rows, padded), whole(field_n),
                      whole(mom_n), whole(mom_n), whole(we), whole(mom_w), whole(mom_n)],
            out_specs=(outer(rows, padded), whole(field_n), whole(we), whole(full_r), whole(mom_n),
                       whole(stat_w)),
            out_shape=(field_w, field_n, sds((narrow, wide), F32), full_r, mom_n, stat_w),
            scratch_shapes=back + turned + [scr((8, wide), F32)],
            compiler_params=params(56),
            cost_estimate=cst(flops=12 * flop_w, bytes_accessed=12 * field_w.size),
            name="between",
        )(n1, a, st, vec_n[1], mom1, wr, x, gz, c, mom2, vec_n[0], we, momw, smean)

    def last(n1, a, st, mom1, wr, gz):
        return pl.pallas_call(
            functools.partial(k_last, width, total),
            grid=(frames,),
            in_specs=[whole(field_n), whole(field_n), whole(st), whole(mom_n), whole(mom_n),
                      whole(wr), outer(rows, width), outer(rows, padded)],
            out_specs=(outer(rows, width), whole(full_r), whole(mom_n)),
            out_shape=(sds(inputs.shape, F32), full_r, mom_n),
            scratch_shapes=back,
            compiler_params=params(48),
            cost_estimate=cst(flops=6 * flop_w, bytes_accessed=12 * field_w.size),
            name="last",
        )(n1, a, st, vec_n[0], mom1, wr, inputs, gz)

    a0, st = first(inputs, wr0)
    c0, m0, mom10, st = mix(0, a0, halo(a0, shape), exchange(st), mix_w0)
    ch0 = halo(c0, shape)
    e0, mom20, off0, st, we0 = expand(0, c0, exchange(st), exp_w0)
    x1, a1, momw0, smean0, st = join(0, e0, inputs, exchange(st), off0, we0, wr1)
    c1, m1, mom11, st = mix(1, a1, halo(a1, shape), exchange(st), wm1)
    ch1 = halo(c1, shape)
    e1, mom21, off1, st, _ = expand(1, c1, exchange(st), we1)
    out, gz1, u1, p1, momw1, smean1, pool, st = turn(e1, x1, exchange(st), off1, we1, c1, mom21)

    clips = clip_index.shape[0] // 6
    labels = jnp.arange(clips, dtype=jnp.int32)
    hot = (centre[None, :] == labels[:, None]).astype(F32)
    pooled = jnp.dot(hot, pool[:, 0, :], precision=HIGHEST, preferred_element_type=F32)
    if devices <= 64:
        pooled = jnp.sum(lax.all_gather(pooled, AX, axis=0, tiled=False), axis=0)
    else:
        pooled = lax.psum(pooled, AX)
    counts = jnp.sum((clip_index[None, :] == labels[:, None]).astype(F32), axis=1)
    pooled = pooled / (counts * float(rows * shape[1] * width))[:, None]

    n, gw1, st = second(1, u1, c1, exchange(st), we1, momw1, smean1, mom21)
    nh = halo(n, shape)
    st = exchange(st)
    de1 = expand_grad(1, c1, p1, we1, gw1, momw1, smean1, mom21)
    gm, n1, gcp, gd1, st = first_back(1, n, nh, c1, ch1, st, a1, wm1, mom11, mom21)
    st = exchange(st)
    dk1, dm1 = mix_grads(1, gcp, m1, gm, a1, mom11)
    if slotted:
        wr0_full = gather_order(wr0, rank, devices, wide)
    else:
        wr0_full = wr0
    gz0, u0, p0, dr1, gn1, st = between(n1, a1, st, mom11, wr1, x1, gz1, c0, mom20, we0, momw0, smean0)
    n, gw0, st = second(0, u0, c0, exchange(st), we0, momw0, smean0, mom20)
    nh = halo(n, shape)
    st = exchange(st)
    de0 = expand_grad(0, c0, p0, we0, gw0, momw0, smean0, mom20)
    gm, n1, gcp, gd0, st = first_back(0, n, nh, c0, ch0, st, a0, wm0, mom10, mom20)
    st = exchange(st)
    dk0, dm0 = mix_grads(0, gcp, m0, gm, a0, mom10)
    gx, dr0, gn0 = last(n1, a0, st, mom10, wr0_full, gz0)

    own = lambda full: owner_sums(full, devices)
    deltas = [
        jnp.stack([own(dr0), own(dr1)]),
        jnp.stack([own(dm0), own(dm1)]),
        jnp.stack([own(dk0[:27].T), own(dk1[:27].T)]),
        jnp.stack([own(de0), own(de1)]),
    ]

    def mine(vec0, vec1, row):
        share = vec0.shape[1] // devices
        both = jnp.stack([vec0[row], vec1[row]])
        return lax.dynamic_slice_in_dim(both, rank * share, share, axis=1)

    for pair in ((gn0, gn1), (gd0, gd1), (gw0, gw1)):
        deltas.append(mine(pair[0], pair[1], 0))
        deltas.append(mine(pair[0], pair[1], 1))
    velocity = [MOMENTUM * momenta[i] + deltas[i] for i in range(10)]
    updated = [
        weights[i] - LEARN_RATE * (deltas[i] + MOMENTUM * velocity[i]) for i in range(10)
    ]
    return (out, pooled, gx, *deltas, *velocity, *updated)


def k_order(me_ref, slots_ref, out_ref):
    order_rows(slots_ref, out_ref, me_ref[0])


def gather_order(slots, rank, devices, wide):
    return pl.pallas_call(
        k_order,
        in_specs=[SM, VM],
        out_specs=VM,
        out_shape=jax.ShapeDtypeStruct((wide, slots.shape[2]), F32),
        compiler_params=params(12),
        name="order",
    )(rank.astype(jnp.int32)[None], slots)


def solution(mesh):
    field = P("dp", "fsdp", None, None)
    mat = P(None, AX, None)
    vec = P(None, AX)
    group = (mat,) * 4 + (vec,) * 6
    return jax.shard_map(
        body,
        mesh=mesh,
        in_specs=(field, field, P()) + group * 2,
        out_specs=(field, P(), field) + group * 3,
        check_vma=False,
    )
```

```python
import functools

import jax
import jax.numpy as jnp
from jax import lax
from jax.experimental import pallas as pl
from jax.experimental.pallas import tpu as pltpu
from jax.sharding import PartitionSpec as P

EPSILON = 1e-05
MOMENTUM = 0.9
LEARN_RATE = 0.0001
HIGHEST = lax.Precision.HIGHEST
AX = ("dp", "fsdp")
F32 = jnp.float32
BF16 = jnp.bfloat16
MIB = 1 << 20


VM = pl.BlockSpec(memory_space=pltpu.VMEM)
SM = pl.BlockSpec(memory_space=pltpu.SMEM)


def params(mib):
    return pltpu.CompilerParams(vmem_limit_bytes=mib * MIB)


def dot6(left, right):
    return jnp.dot(left, right, precision=HIGHEST, preferred_element_type=F32)


def dot6_rt(left, right):
    return lax.dot_general(
        left, right, (((1,), (1,)), ((), ())), precision=HIGHEST, preferred_element_type=F32
    )


def split2(value):
    high = value.astype(BF16)
    return high, (value - high.astype(F32)).astype(BF16)


def dot3(left, right):
    lh, ll = left
    rh, rl = right
    mm = functools.partial(jnp.dot, preferred_element_type=F32)
    return mm(lh, rh) + (mm(lh, rl) + mm(ll, rh))


def keep_split(value, parts_ref):
    rows = value.shape[0]
    for i in range(parts_ref.shape[0] // rows):
        high = value.astype(BF16)
        parts_ref[i * rows : (i + 1) * rows, :] = high
        value = value - high.astype(F32)


def dot_split(left, parts_ref, count):
    rows = parts_ref.shape[0] // count
    right = [parts_ref[i * rows : (i + 1) * rows, :] for i in range(count)]
    pieces = []
    for i in range(count):
        high = left.astype(BF16)
        pieces.append(high)
        left = left - high.astype(F32)
    mm = functools.partial(jnp.dot, preferred_element_type=F32)
    total = mm(pieces[0], right[1]) + mm(pieces[1], right[0])
    if count == 3:
        low = mm(pieces[1], right[1]) + mm(pieces[0], right[2]) + mm(pieces[2], right[0])
        total = total + low
    return mm(pieces[0], right[0]) + total


def total_rows(value):
    return jnp.sum(value, axis=0, keepdims=True)


def get(ref, start, count):
    return jnp.concatenate([ref[h, pl.ds(start, count), :] for h in range(ref.shape[0])], axis=1)


def put(ref, start, value):
    count = value.shape[0]
    for h in range(ref.shape[0]):
        ref[h, pl.ds(start, count), :] = value[:, h * 128 : h * 128 + 128]


def put_rows(st_ref, first, vec):
    for i in range(vec.shape[1] // 128):
        piece = vec[:, i * 128 : (i + 1) * 128]
        st_ref[:, first + i, :] = jnp.broadcast_to(piece, (st_ref.shape[0], 128))


def take_rows(st_ref, first, channels):
    return jnp.concatenate([st_ref[:, first + i, :] for i in range(channels // 128)], axis=1)


def take_sum(st_ref, first, channels):
    return total_rows(take_rows(st_ref, first, channels))


def narrow_moments(st_ref, channels, local, total):
    sums = take_rows(st_ref, 0, channels)
    squares = take_rows(st_ref, channels // 128, channels)
    mean = total_rows(sums) / total
    off = sums / local - mean
    var = (total_rows(squares) + local * total_rows(off * off)) / total
    return mean, lax.rsqrt(var + EPSILON)


def chunk_loop(voxels, chunk, step, carry):
    def one(i, carry):
        return step(pl.multiple_of(i * chunk, chunk), carry)

    return lax.fori_loop(0, voxels // chunk, one, carry)


def local_moments(ref, chunk):
    halves, voxels, _ = ref.shape
    zero = jnp.zeros((1, halves * 128), F32)
    total = chunk_loop(voxels, chunk, lambda i, acc: acc + total_rows(get(ref, i, chunk)), zero)
    mean = total / float(voxels)

    def squares(i, acc):
        value = get(ref, i, chunk) - mean
        return acc + total_rows(value * value)

    return total, chunk_loop(voxels, chunk, squares, zero)


def put_faces(ref, first, last, frames, start=0):
    halves = ref.shape[0]
    count = (ref.shape[1] - 2 * start) // frames
    for face, frame in ((first, 0), (last, frames - 1)):
        for h in range(halves):
            face[h, 0:count, :] = ref[h, pl.ds(start + frame, count, stride=frames), :]


STAGES = ((3, 4), (1, 2), (0,))


def slot_mask(slot):
    mask = 0
    for bits in STAGES:
        mask |= (slot & ((1 << len(bits)) - 1)) << bits[0]
        slot >>= len(bits)
    return mask


def order_rows(stacks, out_ref, me, first, rows, lanes=slice(None)):
    slot = 0
    for stack in stacks:
        for s in range(stack.shape[0]):
            where = pl.multiple_of(jnp.bitwise_xor(me, slot_mask(slot)) * rows, rows)
            out_ref[pl.ds(where, rows), :] = stack[s, first : first + rows, lanes]
            slot += 1


def k_stack(*refs):
    *parts, out = refs
    at = 0
    for part in parts:
        out[at : at + part.shape[0]] = part[...]
        at += part.shape[0]


def as_column(row):
    n = row.shape[1]
    same = lax.broadcasted_iota(jnp.int32, (n, n), 0) == lax.broadcasted_iota(jnp.int32, (n, n), 1)
    return jnp.sum(jnp.where(same, jnp.broadcast_to(row, (n, n)), 0.0), axis=1, keepdims=True)


def k_pack(wr, wm, dw, we, g1, b1, g2, b2, g3, b3, t1, t2):
    share, narrow = wm.shape[1:]
    share_w = wr.shape[1]
    wide = we.shape[2]
    t1[0, 0:share_w, :] = wr[0]
    t1[0, share_w : share_w + share, :] = wm[0]
    lane = lax.broadcasted_iota(jnp.int32, (share, narrow), 1)
    blocks = []
    for b in range(2):
        block = jnp.concatenate([dw[b], jnp.zeros((share, narrow - 27), F32)], axis=1)
        for i, vec in enumerate((g1, b1, g2, b2)):
            block = jnp.where(lane == 27 + i, as_column(vec[b : b + 1, :]), block)
        blocks.append(block)
    t1[0, share_w + share :, :] = jnp.where(lane < 32, blocks[0], pltpu.roll(blocks[1], 32, 1))
    t2[0:share_w, :] = wr[1]
    t2[share_w : share_w + share, :] = wm[1]
    at = share_w + share
    for b in range(2):
        for q in range(wide // narrow):
            t2[at : at + share, :] = we[b, :, q * narrow : (q + 1) * narrow]
            at += share
    lane = lax.broadcasted_iota(jnp.int32, (share_w, narrow), 1)
    block = jnp.zeros((share_w, narrow), F32)
    for i, (vec, b) in enumerate(((g3, 0), (b3, 0), (g3, 1), (b3, 1))):
        block = jnp.where(lane == i, as_column(vec[b : b + 1, :]), block)
    t2[at : at + share_w, :] = block


def k_open_early(me_ref, mine, theirs, wm, tv, scr):
    narrow = wm.shape[0]
    share = scr.shape[0] // (mine.shape[0] * 2)
    share_w = mine.shape[1] - 2 * share
    order_rows((mine, theirs), wm, me_ref[0], share_w, share)
    order_rows((mine, theirs), scr, me_ref[0], share_w + share, share, slice(0, 128))
    turned = scr[...].T
    tv[0] = turned[0:32]
    tv[1] = turned[32:64]


def k_open_later(later, wr, wm, we0, we1, vw):
    wide, narrow = wr.shape
    devices = later.shape[0]
    share, share_w = narrow // devices, wide // devices
    wr[...] = later[:, 0:share_w, :].reshape(wide, narrow)
    wm[...] = later[:, share_w : share_w + share, :].reshape(narrow, narrow)
    at = share_w + share
    for we in (we0, we1):
        for q in range(wide // narrow):
            piece = later[:, at : at + share, :]
            we[:, q * narrow : (q + 1) * narrow] = piece.reshape(narrow, narrow)
            at += share
    turned = later[:, at : at + share_w, 0:128].reshape(wide, 128).T
    vw[0, 0:2, :] = turned[0:2]
    vw[1, 0:2, :] = turned[2:4]


def run_moments(f, value, acc_ref):
    count = float(value.shape[0])
    total = total_rows(value)
    mean = total / count
    apart = value - mean
    squares = total_rows(apart * apart)

    @pl.when(f == 0)
    def _():
        acc_ref[0:1, :] = total
        acc_ref[1:2, :] = squares

    @pl.when(f > 0)
    def _():
        done = f.astype(F32) * count
        seen = acc_ref[0:1, :]
        delta = mean - seen / done
        acc_ref[1:2, :] = acc_ref[1:2, :] + squares + delta * delta * (done * count / (done + count))
        acc_ref[0:1, :] = seen + total


def put_narrow(f, steps, a, a_ref, face_f, face_l, st_ref, acc_ref, frames):
    put(a_ref, 0, a)
    put_faces(a_ref, face_f, face_l, frames)
    run_moments(f, a, acc_ref)

    @pl.when(f == steps - 1)
    def _():
        put_rows(st_ref, 0, acc_ref[0:1, :])
        put_rows(st_ref, a_ref.shape[0], acc_ref[1:2, :])


def k_first(frames, f, steps, me_ref, x_ref, *refs):
    *w_refs, a_ref, face_f, face_l, st_ref, w_out, w_parts, acc_ref = refs
    wide = x_ref.shape[3]
    chunk = a_ref.shape[1]

    @pl.when(f == 0)
    def _():
        if len(w_refs) == 2:
            order_rows(w_refs, w_out, me_ref[0], 0, wide // (2 * w_refs[0].shape[0]))
        else:
            w_out[...] = w_refs[0][...]
        keep_split(w_out[...], w_parts)

    a = dot_split(x_ref[...].reshape(chunk, wide), w_parts, 3)
    put_narrow(f, steps, a, a_ref, face_f, face_l, st_ref, acc_ref, frames)


def finish_narrow(a_ref, st_ref, line):
    total, squares = local_moments(a_ref, line)
    put_rows(st_ref, 0, total)
    put_rows(st_ref, a_ref.shape[0], squares)


def by_frame(keep_ref, o, frames):
    frame = lax.broadcasted_iota(jnp.int32, (8, 128), 0) % frames
    value = jnp.zeros((8, 128), F32)
    for f in range(frames):
        value = jnp.where(frame == f, keep_ref[o * frames + f], value)
    return value


def make_taps(k_ref, keep_ref, wt_ref, frames, flipped):
    for o in range(3):
        keep = by_frame(keep_ref, o, frames)
        for i in range(9):
            tap = 9 * o + i
            source = 26 - tap if flipped else tap
            for h in range(wt_ref.shape[0]):
                row = k_ref[source : source + 1, h * 128 : h * 128 + 128]
                wt_ref[h, tap] = jnp.broadcast_to(row, (8, 128)) * keep


def shift_frames(field, before, after, line, frames, halos):
    halves, voxels, _ = field.shape

    def step(i, carry):
        for h in range(halves):
            value = field[h, pl.ds(i, line), :].reshape(line // 8, 8, 128)
            before[h, pl.ds(i, line), :] = pltpu.roll(value, 1, 1).reshape(line, 128)
            after[h, pl.ds(i, line), :] = pltpu.roll(value, 7, 1).reshape(line, 128)
        return carry

    chunk_loop(voxels, line, step, 0)
    for target, frame, pieces in ((before, 0, halos[0]), (after, frames - 1, halos[1])):
        start = 0
        for piece in pieces:
            count = piece.shape[0]
            for h in range(halves):
                target[h, pl.ds(start * frames + frame, count, stride=frames), :] = piece[
                    :, h * 128 : h * 128 + 128
                ]
            start += count


def column_views(value, first, last):
    n = value.shape[0] - 2
    upper = lax.broadcasted_iota(jnp.int32, (n, 8, 128), 1) < 4
    turned = pltpu.roll(value, 4, 1)
    left = jnp.where(upper, turned[0:n], turned[1 : n + 1])
    right = jnp.where(upper, turned[1 : n + 1], turned[2:])
    return left, value[1 : n + 1], right


def line_views(ref, h, start, line, part, parts):
    n = line // 8 // parts
    zero = jnp.zeros((1, 8, 128), F32)
    pieces = []
    if part == 0:
        pieces.append(zero)
    low = part * n - (part > 0)
    high = (part + 1) * n + (part < parts - 1)
    body = ref[h, pl.ds(start + low * 8, (high - low) * 8), :]
    pieces.append(body.reshape(high - low, 8, 128))
    if part == parts - 1:
        pieces.append(zero)
    value = jnp.concatenate(pieces, axis=0) if len(pieces) > 1 else pieces[0]
    return column_views(value, part == 0, part == parts - 1)


def stencil_into(fields, wt_ref, out_ref, line):
    halves, voxels, _ = out_ref.shape
    rows = voxels // line
    parts = 2 if (line // 8) % 2 == 0 else 1
    n = line // 8 // parts
    for h in range(halves):
        for part in range(parts):

            def row(j, older, old):
                new = jnp.zeros((n, 8, 128), F32)
                start = pl.multiple_of(j * line, line)
                for o in range(3):
                    views = line_views(fields[o], h, start, line, part, parts)
                    for q in range(3):
                        older = older + views[q] * wt_ref[h, 9 * o + 6 + q][None]
                        old = old + views[q] * wt_ref[h, 9 * o + 3 + q][None]
                        new = new + views[q] * wt_ref[h, 9 * o + q][None]
                return older, old, new

            zero = jnp.zeros((n, 8, 128), F32)

            def step(j, accs):
                done, old, new = row(j, accs[0], accs[1])

                @pl.when(j >= 2)
                def _():
                    where = pl.multiple_of((j - 2) * line, line) + part * n * 8
                    out_ref[h, pl.ds(pl.multiple_of(where, 8), n * 8), :] = done.reshape(n * 8, 128)

                return old, new

            lax.fori_loop(0, rows + 2, step, (zero, zero))


def halo_pieces(i, face, up, down, top, bottom, act):
    edge = up.shape[2]
    return (
        act(get(up.at[i], 0, edge)) * top,
        act(get(face, 0, face.shape[1])),
        act(get(down.at[i], 0, edge)) * bottom,
    )


def k_mix(line, frames, total, keep_ref, a_ref, hp_ref, hn_ref, up_ref, dn_ref, cu_ref, cd_ref,
          st_in, w_ref, tv_ref, c_ref, mp_ref, before, after, mom_ref, st_ref, wt_ref, *, flush):
    halves, voxels, _ = a_ref.shape
    narrow = halves * 128
    top = keep_ref[3 * frames]
    bottom = keep_ref[3 * frames + 1]
    mean, inverse = narrow_moments(st_in, narrow, float(voxels), total)
    mom_ref[0:1, :] = mean
    mom_ref[1:2, :] = inverse
    scale = tv_ref[27:28, :] * inverse
    shift = tv_ref[28:29, :]

    def mixed(value):
        return dot6(jnp.maximum((value - mean) * scale + shift, 0.0), w_ref[...])

    chunk = voxels // 2 if (voxels // 2) % line == 0 else voxels

    def own(i, carry):
        put(mp_ref, pl.multiple_of(line + i, 8), mixed(get(a_ref, i, chunk)))
        return carry

    chunk_loop(voxels, chunk, own, 0)
    put(mp_ref, 0, mixed(get(up_ref, 0, line)) * top)
    put(mp_ref, line + voxels, mixed(get(dn_ref, 0, line)) * bottom)
    make_taps(tv_ref, keep_ref, wt_ref, frames, False)
    halos = [
        halo_pieces(i, face, cu_ref, cd_ref, top, bottom, mixed)
        for i, face in enumerate((hp_ref, hn_ref))
    ]
    shift_frames(mp_ref, before, after, line, frames, halos)
    flush(1, 2, 3)
    stencil_into((before, mp_ref, after), wt_ref, c_ref, line)
    finish_narrow(c_ref, st_ref, line)


def second_act(c, mom, tv):
    return (c - mom[0:1, :]) * (tv[29:30, :] * mom[1:2, :]) + tv[30:31, :]


def k_expand(line, total, c_ref, st_in, w_ref, tv_ref, mom_ref, off_ref, sloc_ref, seen_ref, st_ref,
             s_ref):
    halves, voxels, _ = c_ref.shape
    narrow, wide = w_ref.shape
    local = float(voxels)
    mean, inverse = narrow_moments(st_in, narrow, local, total)
    mom_ref[0:1, :] = mean
    mom_ref[1:2, :] = inverse
    mom = mom_ref[...]

    def act(i, acc):
        s = jnp.maximum(second_act(get(c_ref, i, line), mom, tv_ref), 0.0)
        s_ref[pl.ds(i, line), :] = s
        return acc + total_rows(s)

    sums = chunk_loop(voxels, line, act, jnp.zeros((1, narrow), F32))
    center = sums / local
    sloc_ref[...] = jnp.broadcast_to(center, (8, narrow))
    put_rows(st_ref, 0, sums)
    off_ref[...] = dot6(sloc_ref[...], w_ref[...])
    chunk = voxels // 2 if (voxels // 2) % line == 0 else voxels

    def gram(i, acc):
        s = s_ref[pl.ds(i, chunk), :] - center
        return acc + dot6(s.T, s)

    seen = dot6(chunk_loop(voxels, chunk, gram, jnp.zeros((narrow, narrow), F32)), w_ref[...])
    seen_ref[...] = seen
    put_rows(st_ref, halves, total_rows(seen * w_ref[...]))


def k_widen(f, steps, c_ref, mom_ref, tv_ref, sloc_ref, w_ref, e_ref, w_parts):
    @pl.when(f == 0)
    def _():
        keep_split(w_ref[...], w_parts)

    s = jnp.maximum(second_act(get(c_ref, 0, c_ref.shape[1]), mom_ref[...], tv_ref), 0.0)
    e_ref[...] = dot_split(s - sloc_ref[0:1, :], w_parts, 3)


def third_norm(st_in, w_ref, off_ref, vw_ref, momw_ref, smean_ref, local, total):
    narrow, wide = w_ref.shape
    s_means = take_rows(st_in, 0, narrow) / local
    squares = take_rows(st_in, narrow // 128, wide)
    e_means = dot6(s_means, w_ref[...])
    mean = jnp.mean(e_means, axis=0, keepdims=True)
    away = e_means - mean
    var = (total_rows(squares) + local * total_rows(away * away)) / total
    inverse = lax.rsqrt(var + EPSILON)
    scale = vw_ref[0:1, :] * inverse
    momw_ref[0:1, :] = scale
    momw_ref[1:2, :] = (off_ref[0:1, :] - mean) * scale + vw_ref[1:2, :]
    momw_ref[2:3, :] = inverse
    smean_ref[0:1, :] = jnp.mean(s_means, axis=0, keepdims=True)


def k_join(frames, total, local, f, steps, e_ref, x_ref, st_in, off_ref, w_ref, vw_ref, wr_ref, x_out,
           a_ref, face_f, face_l, momw_ref, smean_ref, st_ref, w_parts, acc_ref):

    @pl.when(f == 0)
    def _():
        third_norm(st_in, w_ref, off_ref, vw_ref, momw_ref, smean_ref, local, total)
        keep_split(wr_ref[...], w_parts)

    x = x_ref[...].reshape(x_out.shape)
    x = jnp.maximum(e_ref[...] * momw_ref[0:1, :] + momw_ref[1:2, :] + x, 0.0)
    x_out[...] = x
    a = dot_split(x, w_parts, 3)
    put_narrow(f, steps, a, a_ref, face_f, face_l, st_ref, acc_ref, frames)


def wide_step(gz, s, f, u_ref, p_ref, bias_acc, w_parts):
    put(u_ref, 0, dot_split(gz, w_parts, 2))
    p = dot3(split2(s.T), split2(gz))
    part = total_rows(gz)

    @pl.when(f == 0)
    def _():
        p_ref[...] = p
        bias_acc[0:1, :] = part

    @pl.when(f > 0)
    def _():
        p_ref[...] = p_ref[...] + p
        bias_acc[0:1, :] = bias_acc[0:1, :] + part


def centred_act(c_ref, mom_ref, tv_ref, smean_ref):
    c = get(c_ref, 0, c_ref.shape[1])
    return jnp.maximum(second_act(c, mom_ref[...], tv_ref), 0.0) - smean_ref[0:1, :]


def wide_finish(p_ref, w_ref, inverse, bias_acc, st_ref):
    wide = w_ref.shape[1]
    gain_sum = total_rows(p_ref[...] * w_ref[...]) * inverse
    put_rows(st_ref, 0, bias_acc[0:1, :])
    put_rows(st_ref, wide // 128, gain_sum)


def k_turn(total, local, f, steps, e_ref, x_ref, cot_ref, c_ref, st_in, off_ref, w_ref, vw_ref, mom_ref,
           tv_ref, out_ref, gz_ref, u_ref, p_ref, momw_ref, smean_ref, pool_ref, st_ref, w_parts,
           bias_acc):
    chunk, wide = x_ref.shape

    @pl.when(f == 0)
    def _():
        third_norm(st_in, w_ref, off_ref, vw_ref, momw_ref, smean_ref, local, total)
        keep_split((w_ref[...] * momw_ref[0:1, :]).T, w_parts)

    z = e_ref[...] * momw_ref[0:1, :] + momw_ref[1:2, :] + x_ref[...]
    out = jnp.maximum(z, 0.0)
    out_ref[...] = out.reshape(out_ref.shape)
    pooled = jnp.sum(out.reshape(chunk // 8, 8, wide), axis=0)

    @pl.when(f == 0)
    def _():
        pool_ref[...] = pooled

    @pl.when(f > 0)
    def _():
        pool_ref[...] = pool_ref[...] + pooled

    gz = jnp.where(z > 0.0, cot_ref[...].reshape(chunk, wide), 0.0)
    gz_ref[...] = gz
    s = centred_act(c_ref, mom_ref, tv_ref, smean_ref)
    wide_step(gz, s, f, u_ref, p_ref, bias_acc, w_parts)

    @pl.when(f == steps - 1)
    def _():
        wide_finish(p_ref, w_ref, momw_ref[2:3, :], bias_acc, st_ref)


def k_second(total, f, steps, u_ref, c_ref, st_in, w_ref, momw_ref, smean_ref, mom_ref, tv_ref, *refs):
    *more, n_ref, gw_ref, st_ref, q_parts, acc_ref = refs
    halves, chunk, _ = u_ref.shape
    narrow, wide = w_ref.shape

    @pl.when(f == 0)
    def _():
        bias_sum = take_sum(st_in, 0, wide)
        gain_sum = take_sum(st_in, wide // 128, wide)
        gw_ref[0:1, :] = gain_sum
        gw_ref[1:2, :] = bias_sum
        alpha = momw_ref[0:1, :]
        w = w_ref[...]
        wt = split2(w.T)
        q = dot3(split2(w * (alpha * momw_ref[2:3, :] * (gain_sum / total))), wt)
        keep_split(q, q_parts)
        acc_ref[0:2, :] = jnp.zeros((2, narrow), F32)
        d = dot3(split2(jnp.broadcast_to(alpha * (bias_sum / total), (8, wide))), wt)
        acc_ref[2:3, :] = d[0:1, :]

    mom = mom_ref[...]
    c = get(c_ref, 0, chunk)
    y = second_act(c, mom, tv_ref)
    corr = dot_split(jnp.maximum(y, 0.0) - smean_ref[0:1, :], q_parts, 2)
    n = jnp.where(y > 0.0, get(u_ref, 0, chunk) - corr - acc_ref[2:3, :], 0.0)
    put(n_ref, 0, n)
    xhat = (c - mom[0:1, :]) * mom[1:2, :]
    acc_ref[0:1, :] = acc_ref[0:1, :] + total_rows(n)
    acc_ref[1:2, :] = acc_ref[1:2, :] + total_rows(n * xhat)

    @pl.when(f == steps - 1)
    def _():
        put_rows(st_ref, 0, acc_ref[0:1, :])
        put_rows(st_ref, halves, acc_ref[1:2, :])
        if more:
            st_ref[:, 2 * halves :, :] = more[0][...]


def expand_grad(local, total, p_ref, w_ref, gw_ref, momw_ref, smean_ref, sloc_ref, seen_ref, dw_ref):
    apart = sloc_ref[...] - smean_ref[0:1, :]
    column = apart.T[:, 0:1] * local
    alpha = momw_ref[0:1, :]
    gamma = gw_ref[0:1, :] / total * momw_ref[2:3, :]
    beta = gw_ref[1:2, :] / total
    seen = seen_ref[...] + column * dot6(apart, w_ref[...])[0:1, :]
    dw_ref[...] = alpha * (p_ref[...] - column * beta - seen * gamma)


def norm_sums(f, st_in, out_ref):
    @pl.when(f == 0)
    def _():
        narrow = out_ref.shape[1]
        out_ref[0:1, :] = take_sum(st_in, narrow // 128, narrow)
        out_ref[1:2, :] = take_sum(st_in, 0, narrow)


def norm_back(n, a, gain, mom_ref, sums_ref, total):
    mom = mom_ref[...]
    xhat = (a - mom[0:1, :]) * mom[1:2, :]
    return gain * mom[1:2, :] * (n - sums_ref[1:2, :] / total - xhat * (sums_ref[0:1, :] / total))


def k_center(frames, total, f, steps, n_ref, c_ref, st_in, tv_ref, mom2_ref, gc_ref, face_f, face_l,
             gd_ref, *more):
    norm_sums(f, st_in, gd_ref)
    if more:
        more[0][...] = jnp.sum(st_in[:, 2 * gc_ref.shape[0] :, :], axis=0)
    chunk = n_ref.shape[1]
    n, c = get(n_ref, 0, chunk), get(c_ref, 0, chunk)
    put(gc_ref, 0, norm_back(n, c, tv_ref[29:30, :], mom2_ref, gd_ref, total))
    put_faces(gc_ref, face_f, face_l, frames)


def k_first_back(line, frames, keep_ref, gc_ref, hp_ref, hn_ref, up_ref, dn_ref, cu_ref, cd_ref,
                 a_ref, w_ref, tv_ref, mom1_ref, *refs, flush):
    *more, gm_ref, n1_ref, st_ref, gcp_ref, before, after, wt_ref = refs
    halves, voxels, _ = gc_ref.shape
    narrow = halves * 128
    top = keep_ref[3 * frames]
    bottom = keep_ref[3 * frames + 1]

    def own(i, carry):
        put(gcp_ref, pl.multiple_of(line + i, 8), get(gc_ref, i, line))
        return carry

    chunk_loop(voxels, line, own, 0)
    put(gcp_ref, 0, get(up_ref, 0, line) * top)
    put(gcp_ref, line + voxels, get(dn_ref, 0, line) * bottom)
    make_taps(tv_ref, keep_ref, wt_ref, frames, True)
    halos = [
        halo_pieces(i, face, cu_ref, cd_ref, top, bottom, lambda v: v)
        for i, face in enumerate((hp_ref, hn_ref))
    ]
    shift_frames(gcp_ref, before, after, line, frames, halos)
    stencil_into((before, gcp_ref, after), wt_ref, gm_ref, line)
    flush(0)
    wt = split2(w_ref[...].T)
    mom1 = mom1_ref[...]
    scale1 = tv_ref[27:28, :] * mom1[1:2, :]
    chunk = voxels // 2 if (voxels // 2) % line == 0 else voxels

    def step(i, accs):
        gr = dot3(split2(get(gm_ref, i, chunk)), wt)
        off = get(a_ref, i, chunk) - mom1[0:1, :]
        n = jnp.where(off * scale1 + tv_ref[28:29, :] > 0.0, gr, 0.0)
        put(n1_ref, i, n)
        return accs[0] + total_rows(n), accs[1] + total_rows(n * (off * mom1[1:2, :]))

    zero = jnp.zeros((1, narrow), F32)
    bias_acc, gain_acc = chunk_loop(voxels, chunk, step, (zero, zero))
    put_rows(st_ref, 0, bias_acc)
    put_rows(st_ref, halves, gain_acc)
    if more:
        rest = st_ref.shape[1] - 2 * halves
        st_ref[:, 2 * halves :, :] = jnp.broadcast_to(more[0][...][None], (st_ref.shape[0], rest, 128))


def k_side_grads(line, frames, total, keep_ref, gc_ref, mp_ref, before, after, p_ref, w_ref, gw_ref,
                 momw_ref, smean_ref, sloc_ref, seen_ref, dk_ref, de_ref):
    expand_grad(float(gc_ref.shape[1]), total, p_ref, w_ref, gw_ref, momw_ref, smean_ref, sloc_ref,
                seen_ref, de_ref)
    halves, voxels, _ = gc_ref.shape
    narrow = halves * 128
    parts = 2 if (line // 8) % 2 == 0 else 1
    n = line // 8 // parts
    for h in range(halves):
        for o, field in enumerate((before, mp_ref, after)):

            def row(r, accs):
                accs = list(accs)
                for part in range(parts):
                    where = pl.multiple_of(r * line, line) + part * n * 8
                    g = gc_ref[h, pl.ds(pl.multiple_of(where, 8), n * 8), :].reshape(n, 8, 128)
                    for p in range(3):
                        start = pl.multiple_of((r + p) * line, line)
                        views = line_views(field, h, start, line, part, parts)
                        for q in range(3):
                            accs[3 * p + q] = accs[3 * p + q] + jnp.sum(g * views[q], axis=0)
                return tuple(accs)

            accs = lax.fori_loop(0, voxels // line, row, (jnp.zeros((8, 128), F32),) * 9)
            keep = by_frame(keep_ref, o, frames)
            for i in range(9):
                tap = 9 * o + i
                dk_ref[tap : tap + 1, h * 128 : h * 128 + 128] = total_rows(accs[i] * keep)
    dk_ref[27:128, :] = jnp.zeros((101, narrow), F32)


def mixing_grad(line, a_ref, gm_ref, tv_ref, mom1_ref):
    halves, voxels, _ = a_ref.shape
    narrow = halves * 128
    mom1 = mom1_ref[...]
    scale1 = tv_ref[27:28, :] * mom1[1:2, :]
    chunk = voxels // 2 if (voxels // 2) % line == 0 else voxels

    def mixing(i, acc):
        y = (get(a_ref, i, chunk) - mom1[0:1, :]) * scale1 + tv_ref[28:29, :]
        turned = jnp.maximum(y, 0.0).T
        return acc + dot3(split2(turned), split2(get(gm_ref, i, chunk)))

    return chunk_loop(voxels, chunk, mixing, jnp.zeros((narrow, narrow), F32))


def k_mix_grad(line, a_ref, gm_ref, tv_ref, mom1_ref, dm_ref):
    dm_ref[...] = mixing_grad(line, a_ref, gm_ref, tv_ref, mom1_ref)


def k_pack_grads(line, me_ref, a, gm, tv, mom1, de, dk, mine, theirs):
    narrow = dk.shape[1]
    lower = me_ref[0] % 2 == 1
    pairs = mine.shape[0]
    share = narrow // (2 * pairs)
    groups = de.shape[1] // narrow

    def store(at, piece):
        piece = piece.reshape(pairs, 2, share, narrow)
        mine[:, at : at + share, :] = jnp.where(lower, piece[:, 1], piece[:, 0])
        theirs[:, at : at + share, :] = jnp.where(lower, piece[:, 0], piece[:, 1])

    for g in range(groups):
        store(g * share, de[:, g * narrow : (g + 1) * narrow])
    store(groups * share, mixing_grad(line, a, gm, tv, mom1))
    turned = jnp.concatenate([dk[...].T, jnp.zeros((narrow, narrow - 128), F32)], axis=1)
    store((groups + 1) * share, turned)


def k_update(*refs):
    me_ref, zero, one, reduce_zero, reduce_one = refs[:5]
    vecs = refs[5:11]
    params, momenta = refs[11:21], refs[21:31]
    grads, velocity, updated = refs[31:41], refs[41:51], refs[51:61]
    me = me_ref[0]
    share = params[1].shape[1]
    narrow = params[1].shape[2]
    groups = params[3].shape[2] // narrow

    def apply(i, b, grad, where=slice(None)):
        v = MOMENTUM * momenta[i][b, :, where] + grad
        grads[i][b, :, where] = grad
        velocity[i][b, :, where] = v
        updated[i][b, :, where] = params[i][b, :, where] - LEARN_RATE * (grad + MOMENTUM * v)

    packs = (jnp.sum(zero[...], axis=0), jnp.sum(one[...], axis=0))
    for b, (pack, reduce) in enumerate(zip(packs, (reduce_zero, reduce_one))):
        for g in range(groups):
            apply(3, b, pack[g * share : (g + 1) * share], slice(g * narrow, (g + 1) * narrow))
        at = groups * share
        apply(1, b, pack[at : at + share])
        at += share
        apply(2, b, pack[at : at + share, 0:27])
        apply(0, b, jnp.sum(reduce[...], axis=0))
    for j in range(3):
        for r in range(2):
            i = 4 + 2 * j + r
            pieces = []
            for b in range(2):
                value = vecs[2 * j + b][...]
                width = params[i].shape[1]
                length = value.shape[1]
                turned = pltpu.roll(value, length - me * width, 1)
                pieces.append(turned[r : r + 1, 0:width])
            grad = jnp.concatenate(pieces, axis=0)
            v = MOMENTUM * momenta[i][...] + grad
            grads[i][...] = grad
            velocity[i][...] = v
            updated[i][...] = params[i][...] - LEARN_RATE * (grad + MOMENTUM * v)


def put_by_core(dw, me_ref, out_refs):
    if len(out_refs) == 1:
        out_refs[0][...] = dw
    else:
        mine, theirs = out_refs
        dw = dw.reshape(mine.shape[0], 2, *mine.shape[1:])
        lower = me_ref[0] % 2 == 1
        mine[...] = jnp.where(lower, dw[:, 1], dw[:, 0])
        theirs[...] = jnp.where(lower, dw[:, 0], dw[:, 1])


def reduce_grad(ga, x, f, dwt):
    dw = dot3(split2(ga.T), split2(x))

    @pl.when(f == 0)
    def _():
        dwt[...] = dw

    @pl.when(f > 0)
    def _():
        dwt[...] = dwt[...] + dw


def k_between(total, f, steps, me_ref, n1_ref, a_ref, c_ref, x_ref, gz_in, st_in, tv_ref, mom1_ref,
              wr_ref, mom2_ref, tv2_ref, w_ref, momw_ref, smean_ref, gz_ref, u_ref, p_ref, gn_ref,
              st_ref, *refs):
    *dw_refs, wr_parts, w_parts, dwt, bias_acc = refs
    chunk, wide = x_ref.shape
    norm_sums(f, st_in, gn_ref)

    @pl.when(f == 0)
    def _():
        keep_split(wr_ref[...].T, wr_parts)
        keep_split((w_ref[...] * momw_ref[0:1, :]).T, w_parts)

    x = x_ref[...]
    n, a = get(n1_ref, 0, chunk), get(a_ref, 0, chunk)
    ga = norm_back(n, a, tv_ref[27:28, :], mom1_ref, gn_ref, total)
    gy = dot_split(ga, wr_parts, 2) + gz_in[...]
    gz = jnp.where(x > 0.0, gy, 0.0)
    gz_ref[...] = gz
    reduce_grad(ga, x, f, dwt)
    s = centred_act(c_ref, mom2_ref, tv2_ref, smean_ref)
    wide_step(gz, s, f, u_ref, p_ref, bias_acc, w_parts)

    @pl.when(f == steps - 1)
    def _():
        wide_finish(p_ref, w_ref, momw_ref[2:3, :], bias_acc, st_ref)
        put_by_core(dwt[...].T, me_ref, dw_refs)


def k_last_weight(total, f, steps, me_ref, n1_ref, a_ref, x_ref, st_in, tv_ref, mom1_ref, ga_ref,
                  gn_ref, *refs):
    *dw_refs, dwt = refs
    chunk = n1_ref.shape[1]
    norm_sums(f, st_in, gn_ref)
    n, a = get(n1_ref, 0, chunk), get(a_ref, 0, chunk)
    ga = norm_back(n, a, tv_ref[27:28, :], mom1_ref, gn_ref, total)
    put(ga_ref, 0, ga)
    reduce_grad(ga, x_ref[...].reshape(chunk, -1), f, dwt)

    @pl.when(f == steps - 1)
    def _():
        put_by_core(dwt[...].T, me_ref, dw_refs)


def k_last(f, steps, ga_ref, gz_in, wr_ref, gx_ref, wr_parts):
    @pl.when(f == 0)
    def _():
        keep_split(wr_ref[...].T, wr_parts)

    gy = dot_split(get(ga_ref, 0, ga_ref.shape[1]), wr_parts, 2) + gz_in[...]
    gx_ref[...] = gy.reshape(gx_ref.shape)


def exchange(rows):
    return lax.all_to_all(rows, AX, 0, 0)


def meet(value, bits, devices):
    parts = [value]
    for step in range(1, 1 << len(bits)):
        mask = step << bits[0]
        parts.append(lax.ppermute(value, AX, [(i, i ^ mask) for i in range(devices)]))
    return parts


def perm(step, shape):
    dp, fs = shape
    pairs = []
    for i in range(dp):
        for j in range(fs):
            a, b = i + step[0], j + step[1]
            if 0 <= a < dp and 0 <= b < fs:
                pairs.append((i * fs + j, a * fs + b))
    return pairs


def halo(field, first, last, line, frames, shape, beside=()):
    voxels = field.shape[1]
    width = line // frames
    count = voxels // frames
    move = lambda value, step: lax.ppermute(value, AX, perm(step, shape))
    before, after = move(last, (1, 0)), move(first, (-1, 0))
    low, high = field[:, :line], field[:, voxels - line :]
    tops = jnp.stack([before[:, :width], after[:, :width]])
    ends = jnp.stack([before[:, count - width :], after[:, count - width :]])
    beside = list(beside)
    if beside:
        tops, ends, *beside = lax.optimization_barrier((tops, ends, *beside))
    if shape[1] == 2:
        upper = lax.axis_index("fsdp") == 0
        pairs = [(i, i ^ 1) for i in range(shape[0] * 2)]
        row = lax.ppermute(jnp.where(upper, high, low), AX, pairs)
        corner = lax.ppermute(jnp.where(upper, ends, tops), AX, pairs)
        return [before, after, row, row, corner, corner], *beside
    rows = [move(high, (0, 1)), move(low, (0, -1))]
    return [before, after, *rows, move(ends, (0, 1)), move(tops, (0, -1))], *beside


def tree_gather(part, devices, name):
    for bits in STAGES[:-1]:
        parts = meet(part, bits, devices)
        dims = (part.shape[0] * len(parts),) + part.shape[1:]
        part = call(k_stack, name, [(dims, HB)], [(piece, HB) for piece in parts], limit=4)[0]
    return meet(part, STAGES[-1], devices)


def core_sums(mine, theirs, shape):
    pairs = [(i, i ^ 1) for i in range(shape[0] * 2)]
    return mine + lax.ppermute(theirs, AX, pairs)


def owner_parts(parts, shape):
    return lax.all_to_all(parts, "dp", 0, 0)


HB = pl.BlockSpec(memory_space=pl.ANY)
FILLER = 1 << 31
HIDER = 1 << 32


def pieces(far, near):
    rows = near.shape[0]
    size = 4
    for dim in near.shape:
        size *= dim
    if size < MIB // 2:
        return [(far, near)]
    if len(near.shape) == 3 and rows <= 4:
        return [(far.at[i], near.at[i]) for i in range(rows)]
    if rows % 16 == 0:
        half = rows // 2
        return [(far.at[pl.ds(i * half, half)], near.at[pl.ds(i * half, half)]) for i in range(2)]
    return [(far, near)]


class Stream:
    def __init__(self, axis):
        self.axis = axis

    def part(self, ref, i, steps):
        size = ref.shape[self.axis] // steps
        where = pl.ds(i * size if isinstance(i, int) else pl.multiple_of(i * size, size), size)
        return ref.at[(slice(None),) * self.axis + (where,)]


WIDE, NARROW = Stream(0), Stream(1)
AHEAD = 2


def call(kernel, name, outs, ins, scratch=(), limit=24, steps=None, flushes=False, cost=1000):
    n_i, n_o, n_s = len(ins), len(outs), len(scratch)
    count = steps or 1
    near_i = [i for i in range(n_i) if ins[i][1] is not SM]
    whole_i = [i for i in near_i if ins[i][1] is HB]
    flow_i = [i for i in near_i if ins[i][1] is not HB]
    whole_o = [i for i in range(n_o) if outs[i][1] is HB]
    flow_o = [i for i in range(n_o) if outs[i][1] is not HB]

    def run(*refs):
        far_in, far_out = refs[:n_i], refs[n_i : n_i + n_o]
        own = refs[n_i + n_o : n_i + n_o + n_s]
        near = refs[n_i + n_o + n_s : -2]
        sem, flow_sem = refs[-2:]
        in_refs, out_refs = list(far_in), list(near[len(near_i) :])
        for i, ref in zip(near_i, near):
            in_refs[i] = ref
        used = 0
        loads, stores = [], {}
        for i in whole_i:
            for src, dst in pieces(far_in[i], in_refs[i]):
                loads.append(pltpu.make_async_copy(src, dst, sem.at[used]))
                used += 1
        for i in whole_o:
            stores[i] = []
            for dst, src in pieces(far_out[i], out_refs[i]):
                stores[i].append(pltpu.make_async_copy(src, dst, sem.at[used]))
                used += 1
        started = set()

        def flush(*which):
            for i in which:
                started.add(i)
                for copy in stores[i]:
                    copy.start()

        def flow_in(i):
            return [
                pltpu.make_async_copy(
                    ins[j][1].part(far_in[j], i, count),
                    ins[j][1].part(in_refs[j], i, count),
                    flow_sem.at[k, i],
                )
                for k, j in enumerate(flow_i)
            ]

        def flow_out(i):
            return [
                pltpu.make_async_copy(
                    outs[j][1].part(out_refs[j], i, count),
                    outs[j][1].part(far_out[j], i, count),
                    flow_sem.at[len(flow_i) + k, i],
                )
                for k, j in enumerate(flow_o)
            ]

        for copy in loads:
            copy.start()
        heavy = any(ins[j][1] is WIDE for j in flow_i)
        ahead = min(AHEAD, count) if heavy else count
        for i in range(ahead):
            for copy in flow_in(i):
                copy.start()
        for copy in loads:
            copy.wait()
        if steps is None:
            kernel(*in_refs, *out_refs, *own, **({"flush": flush} if flushes else {}))
        else:

            def step(i, carry):
                for copy in flow_in(i):
                    copy.wait()
                if count > ahead:

                    @pl.when(i + ahead < count)
                    def _():
                        for copy in flow_in(i + ahead):
                            copy.start()

                views = list(in_refs) + list(out_refs)
                for j in flow_i:
                    views[j] = ins[j][1].part(in_refs[j], i, count)
                for j in flow_o:
                    views[n_i + j] = outs[j][1].part(out_refs[j], i, count)
                kernel(i, count, *views, *own)
                for copy in flow_out(i):
                    copy.start()
                return carry

            lax.fori_loop(0, count, step, 0)
        for i in whole_o:
            if i not in started:
                for copy in stores[i]:
                    copy.start()
        for i in range(count):
            for copy in flow_out(i):
                copy.wait()
        for i in whole_o:
            for copy in stores[i]:
                copy.wait()

    values = [
        value if spec is SM else pltpu.with_memory_space_constraint(value, pltpu.HBM)
        for value, spec in ins
    ]
    whole = 2 * (len(whole_i) + len(whole_o))
    flows = len(flow_i) + len(flow_o)
    return pl.pallas_call(
        run,
        in_specs=[spec if spec is SM else HB for _, spec in ins],
        out_specs=(HB,) * n_o,
        out_shape=tuple(pltpu.HBM(shape, F32) for shape, _ in outs),
        scratch_shapes=[pltpu.VMEM(shape, dtype) for shape, dtype in scratch]
        + [pltpu.VMEM(ins[i][0].shape, F32) for i in near_i]
        + [pltpu.VMEM(shape, F32) for shape, _ in outs]
        + [pltpu.SemaphoreType.DMA((max(whole, 1),)), pltpu.SemaphoreType.DMA((max(flows, 1), count))],
        compiler_params=params(limit),
        cost_estimate=pl.CostEstimate(flops=cost, bytes_accessed=1000, transcendentals=0),
        name=name,
    )(*values)


def body(inputs, cotangent, clip_index, *args):
    weights, momenta = args[:10], args[10:]
    frames, rows, width, wide = inputs.shape
    narrow = weights[0].shape[2]
    halves = narrow // 128
    shape = (lax.axis_size("dp"), lax.axis_size("fsdp"))
    devices = shape[0] * shape[1]
    rank = lax.axis_index(AX)
    voxels = frames * rows * width
    line = width * frames
    total = float(voxels * devices)
    many = 7 if voxels % (7 * 8 * frames) == 0 else 1
    x0 = inputs.transpose(1, 2, 0, 3)
    cot = cotangent.transpose(1, 2, 0, 3)

    edge = jnp.full((1,), -1, jnp.int32)
    window = lax.dynamic_slice_in_dim(
        jnp.concatenate([edge, clip_index, edge]), lax.axis_index("dp") * frames, frames + 2
    )
    centre = window[1:-1]
    flags = jnp.concatenate(
        [
            (window[:-2] == centre).astype(F32),
            jnp.ones((frames,), F32),
            (window[2:] == centre).astype(F32),
            (lax.axis_index("fsdp") > 0).astype(F32)[None],
            (lax.axis_index("fsdp") < shape[1] - 1).astype(F32)[None],
        ]
    )
    me = rank.astype(jnp.int32)[None]

    field_n = (halves, voxels, 128)
    grown_n = (halves, voxels + 2 * line, 128)
    face_n = (halves, voxels // frames, 128)
    field_w = (voxels, wide)
    stat_n = (devices, 2 * halves, 128)
    stat_e = (devices, (narrow + wide) // 128, 128)
    stat_w = (devices, 2 * wide // 128, 128)
    mom_n, mom_w = (8, narrow), (8, wide)
    down_r, down_m, down_e = (wide, narrow), (narrow, narrow), (narrow, wide)
    parts = lambda *values: [(value, NARROW) for value in values]

    near = lambda *values: [(value, HB) for value in values]
    fix = near
    owned = devices == 32
    half = (devices // 2, wide // devices, narrow)
    down_halves = (half, half) if owned else (down_r,)

    def first(wr0):
        return call(
            functools.partial(k_first, frames),
            "first",
            [(field_n, NARROW), (face_n, NARROW), (face_n, NARROW)] + near(stat_n, down_r),
            [(me, SM), (x0, WIDE)] + near(*wr0),
            scratch=[((3 * wide, narrow), BF16), (mom_n, F32)],
            limit=48,
            steps=many,
        )

    if owned:
        share_n, share_w = weights[1].shape[1], weights[0].shape[1]
        early, late = call(
            k_pack,
            "pack",
            near(
                (1, share_w + 2 * share_n, narrow),
                (2 * share_w + share_n * (1 + 2 * (wide // narrow)), narrow),
            ),
            near(*weights),
            limit=4,
        )
        wr0 = slots = tree_gather(early, devices, "stack")
        late = lax.all_gather(late, AX, axis=0, tiled=False)
        a0, *faces, st, wr0 = first(wr0)
        wm0, tv = call(
            k_open_early,
            "open_early",
            near(down_m, (2, 32, narrow)),
            [(me, SM)] + near(*slots),
            scratch=[((narrow, 128), F32)],
            limit=8,
            cost=FILLER,
        )
        wr1, wm1, we0, we1, vw = call(
            k_open_later,
            "open_later",
            near(down_r, down_m, down_e, down_e, (2, 8, wide)),
            near(late),
            limit=16,
            cost=FILLER,
        )
    else:
        gather = lambda part: lax.all_gather(part, AX, axis=0, tiled=True)
        wr0, wr1 = [gather(weights[0][0])], gather(weights[0][1])
        wm0, wm1 = gather(weights[1][0]), gather(weights[1][1])
        we0, we1 = gather(weights[3][0]), gather(weights[3][1])
        small = jnp.concatenate([weights[2]] + [weights[i][..., None] for i in (4, 5, 6, 7)], axis=2)
        small = gather(small.transpose(1, 0, 2))
        tv = jnp.pad(small.transpose(1, 2, 0), ((0, 0), (0, 1), (0, 0)))
        large = gather(jnp.stack([weights[8], weights[9]], axis=2).transpose(1, 0, 2))
        vw = jnp.pad(large.transpose(1, 2, 0), ((0, 0), (0, 6), (0, 0)))

    def mix(block, a, halos, st, wm):
        return call(
            functools.partial(k_mix, line, frames, total),
            "mix",
            near(field_n, grown_n, grown_n, grown_n, mom_n, stat_n),
            [(flags, SM)] + near(a, *halos, st, wm, tv[block]),
            scratch=[((halves, 27, 8, 128), F32)],
            limit=20,
            flushes=True,
        )

    def expand(block, c, st, we):
        return call(
            functools.partial(k_expand, line, total),
            "expand",
            near(mom_n, mom_w, mom_n, down_e, stat_e),
            near(c, st, we, tv[block]),
            scratch=[((voxels, narrow), F32)],
            limit=20,
        )

    def widen(block, c, mom2, sloc, we):
        return call(
            k_widen,
            "widen",
            [(field_w, WIDE)],
            [(c, NARROW)] + near(mom2, tv[block], sloc, we),
            scratch=[((3 * narrow, wide), BF16)],
            limit=48,
            steps=many,
            cost=FILLER,
        )[0]

    def join(e, x, st, off, we, wr):
        return call(
            functools.partial(k_join, frames, total, float(voxels)),
            "join",
            [(field_w, WIDE), (field_n, NARROW), (face_n, NARROW), (face_n, NARROW)]
            + near(mom_w, mom_n, stat_n),
            [(e, WIDE), (x, WIDE)] + near(st, off, we, vw[0], wr),
            scratch=[((3 * wide, narrow), BF16), (mom_n, F32)],
            limit=56,
            steps=many,
        )

    def turn(e, x, c, st, off, we, mom2):
        return call(
            functools.partial(k_turn, total, float(voxels)),
            "turn",
            [((rows, width, frames, wide), WIDE), (field_w, WIDE), (field_n, NARROW)]
            + near(down_e, mom_w, mom_n, mom_w, stat_w),
            [(e, WIDE), (x, WIDE), (cot, WIDE), (c, NARROW)]
            + near(st, off, we, vw[1], mom2, tv[1]),
            scratch=[((2 * wide, narrow), BF16), (mom_w, F32)],
            limit=58,
            steps=many,
        )

    def stat_with(more):
        return (devices, 2 * halves + sum(value.shape[-2] for value in more), 128)

    def second(block, u, c, st, we, momw, smean, mom2, *more):
        return call(
            functools.partial(k_second, total),
            "second",
            parts(field_n) + near(mom_w, stat_with(more)),
            parts(u, c) + near(st, we, momw, smean, mom2, tv[block], *more),
            scratch=[((2 * narrow, narrow), BF16), (mom_n, F32)],
            limit=24,
            steps=many,
        )

    def center(block, n, c, st, mom2):
        return call(
            functools.partial(k_center, frames, total),
            "center",
            [(field_n, NARROW), (face_n, NARROW), (face_n, NARROW)]
            + near(mom_n, *([(st.shape[1] - 2 * halves, 128)] if st.shape[1] > 2 * halves else [])),
            parts(n, c) + near(st, tv[block], mom2),
            limit=24,
            steps=many,
        )

    def first_back(block, gc, halos, a, wm, mom1, *more):
        return call(
            functools.partial(k_first_back, line, frames),
            "first_back",
            near(field_n, field_n, stat_with(more)),
            [(flags, SM)] + near(gc, *halos, a, wm, tv[block], mom1, *more),
            scratch=[(grown_n, F32)] * 3 + [((halves, 27, 8, 128), F32)],
            limit=20,
            flushes=True,
        )

    def side_grads(gc, grown, p, we, gw, momw, smean, sloc, seen):
        return call(
            functools.partial(k_side_grads, line, frames, total),
            "side_grads",
            near((128, narrow), down_e),
            [(flags, SM)] + near(gc, *grown, p, we, gw, momw, smean, sloc, seen),
            limit=24,
            cost=HIDER,
        )

    def pack_grads(block, a, gm, mom1, *grads):
        lines = (narrow // devices) * (wide // narrow + 2)
        return call(
            functools.partial(k_pack_grads, line),
            "pack_grads",
            near(*[(devices // 2, lines, narrow)] * 2),
            [(me, SM)] + near(a, gm, tv[block], mom1, *grads),
            limit=20,
            cost=FILLER,
        )

    def mix_grad(block, a, gm, mom1):
        return call(
            functools.partial(k_mix_grad, line),
            "mix_grad",
            near(down_m),
            near(a, gm, tv[block], mom1),
            limit=12,
        )[0]

    def between(n1, a, st, mom1, wr, x, gz, c, mom2, we, momw, smean):
        return call(
            functools.partial(k_between, total),
            "between",
            [(field_w, WIDE), (field_n, NARROW)] + near(down_e, mom_n, stat_w, *down_halves),
            [(me, SM)]
            + parts(n1, a, c)
            + [(x, WIDE), (gz, WIDE)]
            + near(st, tv[1], mom1, wr, mom2, tv[0], we, momw, smean),
            scratch=[((2 * narrow, wide), BF16), ((2 * wide, narrow), BF16), (down_e, F32),
                     (mom_w, F32)],
            limit=58,
            steps=many,
        )

    def last_weight(n1, a, st, mom1):
        return call(
            functools.partial(k_last_weight, total),
            "last_weight",
            [(field_n, NARROW)] + near(mom_n, *down_halves),
            [(me, SM)] + parts(n1, a) + [(x0, WIDE)] + near(st, tv[0], mom1),
            scratch=[(down_e, F32)],
            limit=48,
            steps=many,
        )

    def last(ga, gz, wr):
        return call(
            k_last,
            "last",
            [((rows, width, frames, wide), WIDE)],
            [(ga, NARROW), (gz, WIDE)] + near(wr),
            scratch=[((2 * narrow, wide), BF16)],
            limit=48,
            steps=many,
            cost=FILLER,
        )[0]

    spread = lambda field, face_f, face_l, *beside: halo(
        field, face_f, face_l, line, frames, shape, beside
    )

    if not owned:
        a0, *faces, st, wr0 = first(wr0)
    c0, *grown0, mom10, st = mix(0, a0, spread(a0, *faces)[0], exchange(st), wm0)
    mom20, off0, sloc0, seen0, st = expand(0, c0, exchange(st), we0)
    e0 = widen(0, c0, mom20, sloc0, we0)
    x1, a1, *faces, momw0, smean0, st = join(e0, x0, exchange(st), off0, we0, wr1)
    c1, *grown1, mom11, st = mix(1, a1, spread(a1, *faces)[0], exchange(st), wm1)
    mom21, off1, sloc1, seen1, st = expand(1, c1, exchange(st), we1)
    e1 = widen(1, c1, mom21, sloc1, we1)
    out, gz1, u1, p1, momw1, smean1, pool, st = turn(
        e1, x1, c1, exchange(st), off1, we1, mom21
    )

    clips = clip_index.shape[0] // 6
    labels = jnp.arange(clips, dtype=jnp.int32)
    hot = (centre[None, :] == labels[:, None]).astype(F32)
    pooled = jnp.dot(
        jnp.concatenate([hot] * (8 // frames), axis=1), pool, precision=HIGHEST,
        preferred_element_type=F32,
    )
    if owned:
        room = -(-clips * share_w // 128) * 128
        pooled = pooled.reshape(clips, devices, share_w).transpose(1, 0, 2).reshape(devices, -1)
        pooled = jnp.pad(pooled, ((0, 0), (0, room - clips * share_w)))
        more = (pooled.reshape(devices, room // 128, 128),)
    else:
        more = ()
        pooled = lax.psum(pooled, AX)
    counts = jnp.sum((clip_index[None, :] == labels[:, None]).astype(F32), axis=1)

    n, gw1, st = second(1, u1, c1, exchange(st), we1, momw1, smean1, mom21, *more)
    gc, face_f, face_l, gd1, *more = center(1, n, c1, exchange(st), mom21)
    faces = (face_f, face_l)
    dk1, de1 = side_grads(gc, grown1, p1, we1, gw1, momw1, smean1, sloc1, seen1)
    halos, de1, dk1 = spread(gc, *faces, de1, dk1)
    gm1, n1, st = first_back(1, gc, halos, a1, wm1, mom11, *more)
    st = exchange(st)
    if owned:
        one = core_sums(*pack_grads(1, a1, gm1, mom11, de1, dk1), shape)
        one, st = lax.optimization_barrier((one, st))
        one = owner_parts(one, shape)
        pooled = st[:, 2 * halves :, :].reshape(devices, -1)[:, : clips * share_w]
        pooled = pooled.reshape(devices, clips, share_w).transpose(1, 0, 2).reshape(clips, wide)
    gz0, u0, p0, gn1, st, *dr1 = between(
        n1, a1, st, mom11, wr1, x1, gz1, c0, mom20, we0, momw0, smean0
    )
    if owned:
        st, one = lax.optimization_barrier((st, one))
    st = exchange(st)
    if owned:
        dr1 = core_sums(*dr1, shape)
        dr1, st = lax.optimization_barrier((dr1, st))
        dr1 = owner_parts(dr1, shape)
    n, gw0, st = second(0, u0, c0, st, we0, momw0, smean0, mom20)
    gc, *faces, gd0 = center(0, n, c0, exchange(st), mom20)
    dk0, de0 = side_grads(gc, grown0, p0, we0, gw0, momw0, smean0, sloc0, seen0)
    halos, de0, dk0 = spread(gc, *faces, de0, dk0)
    gm0, n1, st = first_back(0, gc, halos, a0, wm0, mom10)
    st = exchange(st)
    home = lambda field: field.transpose(2, 0, 1, 3)
    if owned:
        zero = core_sums(*pack_grads(0, a0, gm0, mom10, de0, dk0), shape)
        zero, n1, dr1 = lax.optimization_barrier((zero, n1, dr1))
        zero = owner_parts(zero, shape)
        ga0, gn0, mine, theirs = last_weight(n1, a0, st, mom10)
        tail = owner_parts(core_sums(mine, theirs, shape), shape)
        gx = last(ga0, gz0, wr0)
        pooled = pooled / (counts * float(rows * shape[1] * width))[:, None]
        values = call(
            k_update,
            "update",
            near(*[weights[i].shape for i in range(10)] * 3),
            [(me, SM)]
            + near(zero, one, tail, dr1, gn0, gn1, gd0, gd1, gw0, gw1, *weights, *momenta),
            limit=12,
        )
        return (home(out), pooled, home(gx), *values)

    ga0, gn0, dr0 = last_weight(n1, a0, st, mom10)
    gx = last(ga0, gz0, wr0)
    dm0, dm1 = mix_grad(0, a0, gm0, mom10), mix_grad(1, a1, gm1, mom11)
    pooled = pooled / (counts * float(rows * shape[1] * width))[:, None]

    def own(full):
        parts = full.reshape((devices, full.shape[0] // devices) + full.shape[1:])
        return jnp.sum(lax.all_to_all(parts, AX, 0, 0), axis=0)

    deltas = [
        jnp.stack([own(dr0), own(dr1[0])]),
        jnp.stack([own(dm0), own(dm1)]),
        jnp.stack([own(dk0[:27].T), own(dk1[:27].T)]),
        jnp.stack([own(de0), own(de1)]),
    ]

    def mine(vec0, vec1, row):
        share = vec0.shape[1] // devices
        both = jnp.stack([vec0[row], vec1[row]])
        return lax.dynamic_slice_in_dim(both, rank * share, share, axis=1)

    for first_part, second_part in ((gn0, gn1), (gd0, gd1), (gw0, gw1)):
        deltas.append(mine(first_part, second_part, 0))
        deltas.append(mine(first_part, second_part, 1))
    velocity = [MOMENTUM * momenta[i] + deltas[i] for i in range(10)]
    updated = [
        weights[i] - LEARN_RATE * (deltas[i] + MOMENTUM * velocity[i]) for i in range(10)
    ]
    return (home(out), pooled, home(gx), *deltas, *velocity, *updated)


def solution(mesh):
    field = P("dp", "fsdp", None, None)
    mat = P(None, AX, None)
    vec = P(None, AX)
    group = (mat,) * 4 + (vec,) * 6
    return jax.shard_map(
        body,
        mesh=mesh,
        in_specs=(field, field, P()) + group * 2,
        out_specs=(field, P(), field) + group * 3,
        check_vma=False,
    )
```

```python
import functools

import jax
import jax.numpy as jnp
from jax import lax
from jax.experimental import pallas as pl
from jax.experimental.pallas import tpu as pltpu
from jax.sharding import PartitionSpec as P

EPSILON = 1e-05
MOMENTUM = 0.9
LEARN_RATE = 0.0001
HIGHEST = lax.Precision.HIGHEST
AX = ("dp", "fsdp")
F32 = jnp.float32
BF16 = jnp.bfloat16
MIB = 1 << 20


VM = pl.BlockSpec(memory_space=pltpu.VMEM)
SM = pl.BlockSpec(memory_space=pltpu.SMEM)


def params(mib):
    return pltpu.CompilerParams(vmem_limit_bytes=mib * MIB)


def dot6(left, right):
    return jnp.dot(left, right, precision=HIGHEST, preferred_element_type=F32)


def dot6_rt(left, right):
    return lax.dot_general(
        left, right, (((1,), (1,)), ((), ())), precision=HIGHEST, preferred_element_type=F32
    )


def split2(value):
    high = value.astype(BF16)
    return high, (value - high.astype(F32)).astype(BF16)


def dot3(left, right):
    lh, ll = left
    rh, rl = right
    mm = functools.partial(jnp.dot, preferred_element_type=F32)
    return mm(lh, rh) + (mm(lh, rl) + mm(ll, rh))


def keep_split(value, parts_ref):
    rows = value.shape[0]
    for i in range(parts_ref.shape[0] // rows):
        high = value.astype(BF16)
        parts_ref[i * rows : (i + 1) * rows, :] = high
        value = value - high.astype(F32)


def dot_split(left, parts_ref, count):
    rows = parts_ref.shape[0] // count
    right = [parts_ref[i * rows : (i + 1) * rows, :] for i in range(count)]
    pieces = []
    for i in range(count):
        high = left.astype(BF16)
        pieces.append(high)
        left = left - high.astype(F32)
    mm = functools.partial(jnp.dot, preferred_element_type=F32)
    total = mm(pieces[0], right[1]) + mm(pieces[1], right[0])
    if count == 3:
        low = mm(pieces[1], right[1]) + mm(pieces[0], right[2]) + mm(pieces[2], right[0])
        total = total + low
    return mm(pieces[0], right[0]) + total


def total_rows(value):
    return jnp.sum(value, axis=0, keepdims=True)


def get(ref, start, count):
    return jnp.concatenate([ref[h, pl.ds(start, count), :] for h in range(ref.shape[0])], axis=1)


def put(ref, start, value):
    count = value.shape[0]
    for h in range(ref.shape[0]):
        ref[h, pl.ds(start, count), :] = value[:, h * 128 : h * 128 + 128]


def put_rows(st_ref, first, vec):
    for i in range(vec.shape[1] // 128):
        piece = vec[:, i * 128 : (i + 1) * 128]
        st_ref[:, first + i, :] = jnp.broadcast_to(piece, (st_ref.shape[0], 128))


def take_rows(st_ref, first, channels):
    return jnp.concatenate([st_ref[:, first + i, :] for i in range(channels // 128)], axis=1)


def take_sum(st_ref, first, channels):
    return total_rows(take_rows(st_ref, first, channels))


def narrow_moments(st_ref, channels, local, total):
    sums = take_rows(st_ref, 0, channels)
    squares = take_rows(st_ref, channels // 128, channels)
    mean = total_rows(sums) / total
    off = sums / local - mean
    var = (total_rows(squares) + local * total_rows(off * off)) / total
    return mean, lax.rsqrt(var + EPSILON)


def chunk_loop(voxels, chunk, step, carry):
    def one(i, carry):
        return step(pl.multiple_of(i * chunk, chunk), carry)

    return lax.fori_loop(0, voxels // chunk, one, carry)


def local_moments(ref, chunk):
    halves, voxels, _ = ref.shape
    zero = jnp.zeros((1, halves * 128), F32)
    total = chunk_loop(voxels, chunk, lambda i, acc: acc + total_rows(get(ref, i, chunk)), zero)
    mean = total / float(voxels)

    def squares(i, acc):
        value = get(ref, i, chunk) - mean
        return acc + total_rows(value * value)

    return total, chunk_loop(voxels, chunk, squares, zero)


def put_faces(ref, first, last, frames, start=0):
    halves = ref.shape[0]
    count = (ref.shape[1] - 2 * start) // frames
    for face, frame in ((first, 0), (last, frames - 1)):
        for h in range(halves):
            face[h, 0:count, :] = ref[h, pl.ds(start + frame, count, stride=frames), :]


STAGES = ((3, 4), (1, 2), (0,))


def slot_mask(slot):
    mask = 0
    for bits in STAGES:
        mask |= (slot & ((1 << len(bits)) - 1)) << bits[0]
        slot >>= len(bits)
    return mask


def order_rows(stacks, out_ref, me, first, rows, lanes=slice(None)):
    slot = 0
    for stack in stacks:
        for s in range(stack.shape[0]):
            where = pl.multiple_of(jnp.bitwise_xor(me, slot_mask(slot)) * rows, rows)
            out_ref[pl.ds(where, rows), :] = stack[s, first : first + rows, lanes]
            slot += 1


def k_stack(*refs):
    *parts, out = refs
    at = 0
    for part in parts:
        out[at : at + part.shape[0]] = part[...]
        at += part.shape[0]


def as_column(row):
    n = row.shape[1]
    same = lax.broadcasted_iota(jnp.int32, (n, n), 0) == lax.broadcasted_iota(jnp.int32, (n, n), 1)
    return jnp.sum(jnp.where(same, jnp.broadcast_to(row, (n, n)), 0.0), axis=1, keepdims=True)


def k_pack(wr, wm, dw, we, g1, b1, g2, b2, g3, b3, t1, t2):
    share, narrow = wm.shape[1:]
    share_w = wr.shape[1]
    wide = we.shape[2]
    t1[0, 0:share_w, :] = wr[0]
    t1[0, share_w : share_w + share, :] = wm[0]
    lane = lax.broadcasted_iota(jnp.int32, (share, narrow), 1)
    blocks = []
    for b in range(2):
        block = jnp.concatenate([dw[b], jnp.zeros((share, narrow - 27), F32)], axis=1)
        for i, vec in enumerate((g1, b1, g2, b2)):
            block = jnp.where(lane == 27 + i, as_column(vec[b : b + 1, :]), block)
        blocks.append(block)
    t1[0, share_w + share :, :] = jnp.where(lane < 32, blocks[0], pltpu.roll(blocks[1], 32, 1))
    t2[0:share_w, :] = wr[1]
    t2[share_w : share_w + share, :] = wm[1]
    at = share_w + share
    for b in range(2):
        for q in range(wide // narrow):
            t2[at : at + share, :] = we[b, :, q * narrow : (q + 1) * narrow]
            at += share
    lane = lax.broadcasted_iota(jnp.int32, (share_w, narrow), 1)
    block = jnp.zeros((share_w, narrow), F32)
    for i, (vec, b) in enumerate(((g3, 0), (b3, 0), (g3, 1), (b3, 1))):
        block = jnp.where(lane == i, as_column(vec[b : b + 1, :]), block)
    t2[at : at + share_w, :] = block


def k_open_early(me_ref, mine, theirs, wm, tv, scr):
    narrow = wm.shape[0]
    share = scr.shape[0] // (mine.shape[0] * 2)
    share_w = mine.shape[1] - 2 * share
    order_rows((mine, theirs), wm, me_ref[0], share_w, share)
    order_rows((mine, theirs), scr, me_ref[0], share_w + share, share, slice(0, 128))
    turned = scr[...].T
    tv[0] = turned[0:32]
    tv[1] = turned[32:64]


def k_open_later(later, wr, wm, we0, we1, vw):
    wide, narrow = wr.shape
    devices = later.shape[0]
    share, share_w = narrow // devices, wide // devices
    wr[...] = later[:, 0:share_w, :].reshape(wide, narrow)
    wm[...] = later[:, share_w : share_w + share, :].reshape(narrow, narrow)
    at = share_w + share
    for we in (we0, we1):
        for q in range(wide // narrow):
            piece = later[:, at : at + share, :]
            we[:, q * narrow : (q + 1) * narrow] = piece.reshape(narrow, narrow)
            at += share
    turned = later[:, at : at + share_w, 0:128].reshape(wide, 128).T
    vw[0, 0:2, :] = turned[0:2]
    vw[1, 0:2, :] = turned[2:4]


def run_moments(f, value, acc_ref):
    count = float(value.shape[0])
    total = total_rows(value)
    mean = total / count
    apart = value - mean
    squares = total_rows(apart * apart)

    @pl.when(f == 0)
    def _():
        acc_ref[0:1, :] = total
        acc_ref[1:2, :] = squares

    @pl.when(f > 0)
    def _():
        done = f.astype(F32) * count
        seen = acc_ref[0:1, :]
        delta = mean - seen / done
        acc_ref[1:2, :] = acc_ref[1:2, :] + squares + delta * delta * (done * count / (done + count))
        acc_ref[0:1, :] = seen + total


def put_narrow(f, steps, a, a_ref, face_f, face_l, st_ref, acc_ref, frames):
    put(a_ref, 0, a)
    put_faces(a_ref, face_f, face_l, frames)
    run_moments(f, a, acc_ref)

    @pl.when(f == steps - 1)
    def _():
        put_rows(st_ref, 0, acc_ref[0:1, :])
        put_rows(st_ref, a_ref.shape[0], acc_ref[1:2, :])


def k_first(frames, f, steps, me_ref, x_ref, *refs):
    *w_refs, a_ref, face_f, face_l, st_ref, w_out, w_parts, acc_ref = refs
    wide = x_ref.shape[3]
    chunk = a_ref.shape[1]

    @pl.when(f == 0)
    def _():
        if len(w_refs) == 2:
            order_rows(w_refs, w_out, me_ref[0], 0, wide // (2 * w_refs[0].shape[0]))
        else:
            w_out[...] = w_refs[0][...]
        keep_split(w_out[...], w_parts)

    a = dot_split(x_ref[...].reshape(chunk, wide), w_parts, 3)
    put_narrow(f, steps, a, a_ref, face_f, face_l, st_ref, acc_ref, frames)


def finish_narrow(a_ref, st_ref, line):
    total, squares = local_moments(a_ref, line)
    put_rows(st_ref, 0, total)
    put_rows(st_ref, a_ref.shape[0], squares)


def by_frame(keep_ref, o, frames):
    frame = lax.broadcasted_iota(jnp.int32, (8, 128), 0) % frames
    value = jnp.zeros((8, 128), F32)
    for f in range(frames):
        value = jnp.where(frame == f, keep_ref[o * frames + f], value)
    return value


def make_taps(k_ref, keep_ref, wt_ref, frames, flipped):
    for o in range(3):
        keep = by_frame(keep_ref, o, frames)
        for i in range(9):
            tap = 9 * o + i
            source = 26 - tap if flipped else tap
            for h in range(wt_ref.shape[0]):
                row = k_ref[source : source + 1, h * 128 : h * 128 + 128]
                wt_ref[h, tap] = jnp.broadcast_to(row, (8, 128)) * keep


def frame_of(rows, frames):
    return lax.broadcasted_iota(jnp.int32, (rows // 8, 8, 128), 1) % frames


def shift_frames(field, before, after, line, frames):
    halves, voxels, _ = field.shape
    frame = frame_of(line, frames)

    def step(i, carry):
        for h in range(halves):
            value = field[h, pl.ds(i, line), :].reshape(line // 8, 8, 128)
            earlier = jnp.where(frame == 0, 0.0, pltpu.roll(value, 1, 1))
            later = jnp.where(frame == frames - 1, 0.0, pltpu.roll(value, 7, 1))
            before[h, pl.ds(i, line), :] = earlier.reshape(line, 128)
            after[h, pl.ds(i, line), :] = later.reshape(line, 128)
        return carry

    chunk_loop(voxels, line, step, 0)


def put_frames(target, frame, frames, pieces_):
    start = 0
    for piece in pieces_:
        count = piece.shape[0]
        for h in range(target.shape[0]):
            part = piece[:, h * 128 : h * 128 + 128]
            target[h, pl.ds(start * frames + frame, count, stride=frames), :] = part
        start += count


def place_frames(target, line, frames, halos):
    halves, voxels, _ = target.shape

    def clear(i, carry):
        for h in range(halves):
            target[h, pl.ds(i, line), :] = jnp.zeros((line, 128), F32)
        return carry

    chunk_loop(voxels, line, clear, 0)
    put_frames(target, 0, frames, halos[0])
    put_frames(target, frames - 1, frames, halos[1])


def make_halo_taps(k_ref, keep_ref, wt_ref, frames, flipped):
    frame = lax.broadcasted_iota(jnp.int32, (8, 128), 0) % frames
    for i in range(9):
        for h in range(wt_ref.shape[0]):
            value = jnp.zeros((8, 128), F32)
            for o, place in ((0, 0), (2, frames - 1)):
                tap = 26 - (9 * o + i) if flipped else 9 * o + i
                row = k_ref[tap : tap + 1, h * 128 : h * 128 + 128] * keep_ref[o * frames + place]
                value = jnp.where(frame == place, jnp.broadcast_to(row, (8, 128)), value)
            wt_ref[h, i] = value


def column_views(value, first, last):
    n = value.shape[0] - 2
    upper = lax.broadcasted_iota(jnp.int32, (n, 8, 128), 1) < 4
    turned = pltpu.roll(value, 4, 1)
    left = jnp.where(upper, turned[0:n], turned[1 : n + 1])
    right = jnp.where(upper, turned[1 : n + 1], turned[2:])
    return left, value[1 : n + 1], right


def line_views(ref, h, start, line, part, parts):
    n = line // 8 // parts
    zero = jnp.zeros((1, 8, 128), F32)
    pieces = []
    if part == 0:
        pieces.append(zero)
    low = part * n - (part > 0)
    high = (part + 1) * n + (part < parts - 1)
    body = ref[h, pl.ds(start + low * 8, (high - low) * 8), :]
    pieces.append(body.reshape(high - low, 8, 128))
    if part == parts - 1:
        pieces.append(zero)
    value = jnp.concatenate(pieces, axis=0) if len(pieces) > 1 else pieces[0]
    return column_views(value, part == 0, part == parts - 1)


def stencil_into(fields, wt_ref, out_ref, line, base=None, done_half=None):
    halves, voxels, _ = out_ref.shape
    rows = voxels // line
    parts = 2 if (line // 8) % 2 == 0 else 1
    n = line // 8 // parts
    for h in range(halves):
        for part in range(parts):

            def row(j, older, old):
                new = jnp.zeros((n, 8, 128), F32)
                start = pl.multiple_of(j * line, line)
                for o in range(len(fields)):
                    views = line_views(fields[o], h, start, line, part, parts)
                    for q in range(3):
                        older = older + views[q] * wt_ref[h, 9 * o + 6 + q][None]
                        old = old + views[q] * wt_ref[h, 9 * o + 3 + q][None]
                        new = new + views[q] * wt_ref[h, 9 * o + q][None]
                return older, old, new

            zero = jnp.zeros((n, 8, 128), F32)

            def step(j, accs):
                done, old, new = row(j, accs[0], accs[1])

                @pl.when(j >= 2)
                def _():
                    where = pl.multiple_of((j - 2) * line, line) + part * n * 8
                    where = pl.ds(pl.multiple_of(where, 8), n * 8)
                    value = done.reshape(n * 8, 128)
                    if base is not None:
                        value = value + base[h, where, :]
                    out_ref[h, where, :] = value

                return old, new

            lax.fori_loop(0, rows + 2, step, (zero, zero))
        if done_half is not None:
            done_half(h)


def halo_pieces(i, face, up, down, top, bottom, act):
    edge = up.shape[2]
    above = act(get(up.at[i], 0, edge))
    below = above if down is up else act(get(down.at[i], 0, edge))
    return above * top, act(get(face, 0, face.shape[1])), below * bottom


def both(refs):
    return (refs[0], refs[-1])


def part_of(voxels, line):
    for count in (4, 2):
        if voxels % (count * 8) == 0:
            return voxels // count
    return voxels


def first_act(a, mom_ref, tv_ref):
    scale = tv_ref[27:28, :] * mom_ref[1:2, :]
    return jnp.maximum((a - mom_ref[0:1, :]) * scale + tv_ref[28:29, :], 0.0)


def k_mix_own(line, frames, total, keep_ref, a_ref, *refs, flush, ready):
    c_ref, mp_ref, before, after, mom_ref, wt_ref = refs[-6:]
    *rows, st_in, w_ref, tv_ref = refs[:-6]
    up_ref, dn_ref = both(rows)
    halves, voxels, _ = a_ref.shape
    narrow = halves * 128
    mean, inverse = narrow_moments(st_in, narrow, float(voxels), total)
    mom_ref[0:1, :] = mean
    mom_ref[1:2, :] = inverse

    def mixed(value):
        return dot6(first_act(value, mom_ref, tv_ref), w_ref[...])

    chunk = part_of(voxels, line)

    def own(i, carry):
        put(mp_ref, pl.multiple_of(line + i, 8), mixed(get(a_ref, i, chunk)))
        return carry

    chunk_loop(voxels, chunk, own, 0)
    ready()
    above = mixed(get(up_ref, 0, line))
    below = above if dn_ref is up_ref else mixed(get(dn_ref, 0, line))
    put(mp_ref, 0, above * keep_ref[3 * frames])
    put(mp_ref, line + voxels, below * keep_ref[3 * frames + 1])
    flush(1)
    make_taps(tv_ref, keep_ref, wt_ref, frames, False)
    shift_frames(mp_ref, before, after, line, frames)
    flush(2)
    flush(3)
    stencil_into((before, mp_ref, after), wt_ref, c_ref, line, None, lambda h: flush(0, h))


def k_mix(line, frames, keep_ref, part_ref, hp_ref, hn_ref, *refs, flush, ready):
    c_ref, placed, st_ref, wt_ref = refs[-4:]
    *corners, mom_ref, w_ref, tv_ref = refs[:-4]
    cu_ref, cd_ref = both(corners)
    top = keep_ref[3 * frames]
    bottom = keep_ref[3 * frames + 1]
    halos = [
        halo_pieces(
            i, face, cu_ref, cd_ref, top, bottom,
            lambda value: dot6(first_act(value, mom_ref, tv_ref), w_ref[...]),
        )
        for i, face in enumerate((hp_ref, hn_ref))
    ]
    place_frames(placed, line, frames, halos)
    flush(1)
    make_halo_taps(tv_ref, keep_ref, wt_ref, frames, False)
    ready()
    stencil_into((placed,), wt_ref, c_ref, line, part_ref, lambda h: flush(0, h))
    finish_narrow(c_ref, st_ref, line)


def second_act(c, mom, tv):
    return (c - mom[0:1, :]) * (tv[29:30, :] * mom[1:2, :]) + tv[30:31, :]


def k_expand(line, total, c_ref, st_in, w_ref, tv_ref, mom_ref, off_ref, sloc_ref, seen_ref, st_ref,
             s_ref):
    halves, voxels, _ = c_ref.shape
    narrow, wide = w_ref.shape
    local = float(voxels)
    mean, inverse = narrow_moments(st_in, narrow, local, total)
    mom_ref[0:1, :] = mean
    mom_ref[1:2, :] = inverse
    mom = mom_ref[...]

    def act(i, acc):
        s = jnp.maximum(second_act(get(c_ref, i, line), mom, tv_ref), 0.0)
        s_ref[pl.ds(i, line), :] = s
        return acc + total_rows(s)

    sums = chunk_loop(voxels, line, act, jnp.zeros((1, narrow), F32))
    center = sums / local
    sloc_ref[...] = jnp.broadcast_to(center, (8, narrow))
    put_rows(st_ref, 0, sums)
    chunk = part_of(voxels, line)

    def gram(i, acc):
        s = s_ref[pl.ds(i, chunk), :] - center
        return acc + dot6(s.T, s)

    seen = chunk_loop(voxels, chunk, gram, jnp.zeros((narrow, narrow), F32))
    seen = dot6(jnp.concatenate([seen, sloc_ref[...]], axis=0), w_ref[...])
    off_ref[...] = seen[narrow:]
    seen = seen[0:narrow]
    seen_ref[...] = seen
    put_rows(st_ref, halves, total_rows(seen * w_ref[...]))


def k_widen(f, steps, c_ref, mom_ref, tv_ref, sloc_ref, w_ref, e_ref, w_parts):
    @pl.when(f == 0)
    def _():
        keep_split(w_ref[...], w_parts)

    s = jnp.maximum(second_act(get(c_ref, 0, c_ref.shape[1]), mom_ref[...], tv_ref), 0.0)
    e_ref[...] = dot_split(s - sloc_ref[0:1, :], w_parts, 3)


def third_norm(st_in, w_ref, off_ref, vw_ref, momw_ref, smean_ref, local, total):
    narrow, wide = w_ref.shape
    s_means = take_rows(st_in, 0, narrow) / local
    squares = take_rows(st_in, narrow // 128, wide)
    e_means = dot6(s_means, w_ref[...])
    mean = jnp.mean(e_means, axis=0, keepdims=True)
    away = e_means - mean
    var = (total_rows(squares) + local * total_rows(away * away)) / total
    inverse = lax.rsqrt(var + EPSILON)
    scale = vw_ref[0:1, :] * inverse
    momw_ref[0:1, :] = scale
    momw_ref[1:2, :] = (off_ref[0:1, :] - mean) * scale + vw_ref[1:2, :]
    momw_ref[2:3, :] = inverse
    smean_ref[0:1, :] = jnp.mean(s_means, axis=0, keepdims=True)


def k_join(frames, total, local, f, steps, e_ref, x_ref, st_in, off_ref, w_ref, vw_ref, wr_ref, x_out,
           a_ref, face_f, face_l, momw_ref, smean_ref, st_ref, w_parts, acc_ref):

    @pl.when(f == 0)
    def _():
        third_norm(st_in, w_ref, off_ref, vw_ref, momw_ref, smean_ref, local, total)
        keep_split(wr_ref[...], w_parts)

    x = x_ref[...].reshape(x_out.shape)
    x = jnp.maximum(e_ref[...] * momw_ref[0:1, :] + momw_ref[1:2, :] + x, 0.0)
    x_out[...] = x
    a = dot_split(x, w_parts, 3)
    put_narrow(f, steps, a, a_ref, face_f, face_l, st_ref, acc_ref, frames)


def wide_step(gz, s, f, u_ref, p_ref, bias_acc, w_parts):
    put(u_ref, 0, dot_split(gz, w_parts, 2))
    p = dot3(split2(s.T), split2(gz))
    part = total_rows(gz)

    @pl.when(f == 0)
    def _():
        p_ref[...] = p
        bias_acc[0:1, :] = part

    @pl.when(f > 0)
    def _():
        p_ref[...] = p_ref[...] + p
        bias_acc[0:1, :] = bias_acc[0:1, :] + part


def centred_act(c_ref, mom_ref, tv_ref, smean_ref):
    c = get(c_ref, 0, c_ref.shape[1])
    return jnp.maximum(second_act(c, mom_ref[...], tv_ref), 0.0) - smean_ref[0:1, :]


def wide_finish(p_ref, w_ref, inverse, bias_acc, st_ref):
    wide = w_ref.shape[1]
    gain_sum = total_rows(p_ref[...] * w_ref[...]) * inverse
    put_rows(st_ref, 0, bias_acc[0:1, :])
    put_rows(st_ref, wide // 128, gain_sum)


def k_turn(total, local, f, steps, e_ref, x_ref, cot_ref, c_ref, st_in, off_ref, w_ref, vw_ref, mom_ref,
           tv_ref, out_ref, gz_ref, u_ref, p_ref, momw_ref, smean_ref, pool_ref, st_ref, w_parts,
           bias_acc):
    chunk, wide = x_ref.shape

    @pl.when(f == 0)
    def _():
        third_norm(st_in, w_ref, off_ref, vw_ref, momw_ref, smean_ref, local, total)
        keep_split((w_ref[...] * momw_ref[0:1, :]).T, w_parts)

    z = e_ref[...] * momw_ref[0:1, :] + momw_ref[1:2, :] + x_ref[...]
    out = jnp.maximum(z, 0.0)
    out_ref[...] = out.reshape(out_ref.shape)
    pooled = jnp.sum(out.reshape(chunk // 8, 8, wide), axis=0)

    @pl.when(f == 0)
    def _():
        pool_ref[...] = pooled

    @pl.when(f > 0)
    def _():
        pool_ref[...] = pool_ref[...] + pooled

    gz = jnp.where(z > 0.0, cot_ref[...].reshape(chunk, wide), 0.0)
    gz_ref[...] = gz
    s = centred_act(c_ref, mom_ref, tv_ref, smean_ref)
    wide_step(gz, s, f, u_ref, p_ref, bias_acc, w_parts)

    @pl.when(f == steps - 1)
    def _():
        wide_finish(p_ref, w_ref, momw_ref[2:3, :], bias_acc, st_ref)


def k_second(total, f, steps, u_ref, c_ref, st_in, w_ref, momw_ref, smean_ref, mom_ref, tv_ref, *refs):
    *more, n_ref, gw_ref, st_ref, q_parts, acc_ref = refs
    halves, chunk, _ = u_ref.shape
    narrow, wide = w_ref.shape

    @pl.when(f == 0)
    def _():
        bias_sum = take_sum(st_in, 0, wide)
        gain_sum = take_sum(st_in, wide // 128, wide)
        gw_ref[0:1, :] = gain_sum
        gw_ref[1:2, :] = bias_sum
        alpha = momw_ref[0:1, :]
        w = w_ref[...]
        wt = split2(w.T)
        q = dot3(split2(w * (alpha * momw_ref[2:3, :] * (gain_sum / total))), wt)
        keep_split(q, q_parts)
        acc_ref[0:2, :] = jnp.zeros((2, narrow), F32)
        d = dot3(split2(jnp.broadcast_to(alpha * (bias_sum / total), (8, wide))), wt)
        acc_ref[2:3, :] = d[0:1, :]

    mom = mom_ref[...]
    c = get(c_ref, 0, chunk)
    y = second_act(c, mom, tv_ref)
    corr = dot_split(jnp.maximum(y, 0.0) - smean_ref[0:1, :], q_parts, 2)
    n = jnp.where(y > 0.0, get(u_ref, 0, chunk) - corr - acc_ref[2:3, :], 0.0)
    put(n_ref, 0, n)
    xhat = (c - mom[0:1, :]) * mom[1:2, :]
    acc_ref[0:1, :] = acc_ref[0:1, :] + total_rows(n)
    acc_ref[1:2, :] = acc_ref[1:2, :] + total_rows(n * xhat)

    @pl.when(f == steps - 1)
    def _():
        put_rows(st_ref, 0, acc_ref[0:1, :])
        put_rows(st_ref, halves, acc_ref[1:2, :])
        if more:
            st_ref[:, 2 * halves :, :] = more[0][...]


def expand_grad(local, total, p_ref, w_ref, gw_ref, momw_ref, smean_ref, sloc_ref, seen_ref):
    apart = sloc_ref[...] - smean_ref[0:1, :]
    column = apart.T[:, 0:1] * local
    alpha = momw_ref[0:1, :]
    gamma = gw_ref[0:1, :] / total * momw_ref[2:3, :]
    beta = gw_ref[1:2, :] / total
    seen = seen_ref[...] + column * dot6(apart, w_ref[...])[0:1, :]
    return alpha * (p_ref[...] - column * beta - seen * gamma)


def norm_sums(f, st_in, out_ref):
    @pl.when(f == 0)
    def _():
        narrow = out_ref.shape[1]
        out_ref[0:1, :] = take_sum(st_in, narrow // 128, narrow)
        out_ref[1:2, :] = take_sum(st_in, 0, narrow)


def norm_back(n, a, gain, mom_ref, sums_ref, total):
    mom = mom_ref[...]
    xhat = (a - mom[0:1, :]) * mom[1:2, :]
    return gain * mom[1:2, :] * (n - sums_ref[1:2, :] / total - xhat * (sums_ref[0:1, :] / total))


def k_center(frames, total, f, steps, n_ref, c_ref, st_in, tv_ref, mom2_ref, gc_ref, face_f, face_l,
             gd_ref, *more):
    norm_sums(f, st_in, gd_ref)
    if more:
        more[0][...] = jnp.sum(st_in[:, 2 * gc_ref.shape[0] :, :], axis=0)
    chunk = n_ref.shape[1]
    n, c = get(n_ref, 0, chunk), get(c_ref, 0, chunk)
    put(gc_ref, 0, norm_back(n, c, tv_ref[29:30, :], mom2_ref, gd_ref, total))
    put_faces(gc_ref, face_f, face_l, frames)


def put_halves(piece, at, lower, mine, theirs):
    narrow = piece.shape[1]
    pairs = mine.shape[0]
    share = narrow // (2 * pairs)
    piece = piece.reshape(pairs, 2, share, narrow)
    mine[:, at : at + share, :] = jnp.where(lower, piece[:, 1], piece[:, 0])
    theirs[:, at : at + share, :] = jnp.where(lower, piece[:, 0], piece[:, 1])


def k_first_back(line, frames, more, keep_ref, gc_ref, hp_ref, hn_ref, *refs, flush, ready):
    *refs, gm_ref, gcp_ref, before, after, wt_ref, acc_ref = refs
    dm_refs = refs[-1:] if refs[-1].shape == acc_ref.shape else refs[-2:]
    *refs, n1_ref, st_ref = refs[: -len(dm_refs)]
    *refs, rest_ref = refs if more else (*refs, None)
    *refs, a_ref, w_ref, tv_ref, mom1_ref = refs
    rows, corners = refs[: len(refs) // 2], refs[len(refs) // 2 :]
    (up_ref, dn_ref), (cu_ref, cd_ref) = both(rows), both(corners)
    halves, voxels, _ = gc_ref.shape
    narrow = halves * 128
    top = keep_ref[3 * frames]
    bottom = keep_ref[3 * frames + 1]

    def own(i, carry):
        put(gcp_ref, pl.multiple_of(line + i, 8), get(gc_ref, i, line))
        return carry

    chunk_loop(voxels, line, own, 0)
    put(gcp_ref, 0, get(up_ref, 0, line) * top)
    put(gcp_ref, line + voxels, get(dn_ref, 0, line) * bottom)
    make_taps(tv_ref, keep_ref, wt_ref, frames, True)
    halos = [
        halo_pieces(i, face, cu_ref, cd_ref, top, bottom, lambda v: v)
        for i, face in enumerate((hp_ref, hn_ref))
    ]
    shift_frames(gcp_ref, before, after, line, frames)
    put_frames(before, 0, frames, halos[0])
    put_frames(after, frames - 1, frames, halos[1])
    stencil_into((before, gcp_ref, after), wt_ref, gm_ref, line)
    ready()
    wt = split2(w_ref[...].T)
    mom1 = mom1_ref[...]
    scale1 = tv_ref[27:28, :] * mom1[1:2, :]
    chunk = part_of(voxels, line)

    acc_ref[...] = jnp.zeros(acc_ref.shape, F32)

    def step(i, accs):
        gm = split2(get(gm_ref, i, chunk))
        gr = dot3(gm, wt)
        off = get(a_ref, i, chunk) - mom1[0:1, :]
        y = off * scale1 + tv_ref[28:29, :]
        n = jnp.where(y > 0.0, gr, 0.0)
        put(n1_ref, i, n)
        acc_ref[...] = acc_ref[...] + dot3(split2(jnp.maximum(y, 0.0).T), gm)
        return accs[0] + total_rows(n), accs[1] + total_rows(n * (off * mom1[1:2, :]))

    zero = jnp.zeros((1, narrow), F32)
    bias_acc, gain_acc = chunk_loop(voxels, chunk, step, (zero, zero))
    flush(0)
    put_rows(st_ref, 0, bias_acc)
    put_rows(st_ref, halves, gain_acc)
    if more:
        rest = rest_ref[...][None]
        st_ref[:, 2 * halves :, :] = jnp.broadcast_to(rest, (st_ref.shape[0],) + rest.shape[1:])
    if len(dm_refs) == 1:
        dm_refs[0][...] = acc_ref[...]
    else:
        put_halves(acc_ref[...], 0, top > 0.0, *dm_refs)


def k_side_grads(line, frames, total, keep_ref, gc_ref, mp_ref, before, after, placed, p_ref, w_ref, gw_ref,
                 momw_ref, smean_ref, sloc_ref, seen_ref, *refs):
    *out_refs, dk_ref = refs
    de = expand_grad(float(gc_ref.shape[1]), total, p_ref, w_ref, gw_ref, momw_ref, smean_ref, sloc_ref,
                     seen_ref)
    frame = frame_of(line, frames)

    def merge(i, carry):
        for h in range(gc_ref.shape[0]):
            where = pl.ds(i, line)
            halo_part = placed[h, where, :].reshape(line // 8, 8, 128)
            for target, place in ((before, 0), (after, frames - 1)):
                own = target[h, where, :].reshape(line // 8, 8, 128)
                own = jnp.where(frame == place, halo_part, own)
                target[h, where, :] = own.reshape(line, 128)
        return carry

    chunk_loop(placed.shape[1], line, merge, 0)
    halves, voxels, _ = gc_ref.shape
    narrow = halves * 128
    parts = 2 if (line // 8) % 2 == 0 else 1
    n = line // 8 // parts
    for h in range(halves):
        for o, field in enumerate((before, mp_ref, after)):

            def row(r, accs):
                accs = list(accs)
                for part in range(parts):
                    where = pl.multiple_of(r * line, line) + part * n * 8
                    g = gc_ref[h, pl.ds(pl.multiple_of(where, 8), n * 8), :].reshape(n, 8, 128)
                    for p in range(3):
                        start = pl.multiple_of((r + p) * line, line)
                        views = line_views(field, h, start, line, part, parts)
                        for q in range(3):
                            accs[3 * p + q] = accs[3 * p + q] + jnp.sum(g * views[q], axis=0)
                return tuple(accs)

            accs = lax.fori_loop(0, voxels // line, row, (jnp.zeros((8, 128), F32),) * 9)
            keep = by_frame(keep_ref, o, frames)
            for i in range(9):
                tap = 9 * o + i
                dk_ref[tap : tap + 1, h * 128 : h * 128 + 128] = total_rows(accs[i] * keep)
    dk_ref[27:128, :] = jnp.zeros((101, narrow), F32)
    whole = out_refs[0].shape == w_ref.shape
    if whole:
        out_refs[0][...] = de
        out_refs[1][...] = dk_ref[...]
    else:
        lower = keep_ref[3 * frames] > 0.0
        share = narrow // (2 * out_refs[0].shape[0])
        groups = de.shape[1] // narrow
        for g in range(groups):
            put_halves(de[:, g * narrow : (g + 1) * narrow], g * share, lower, *out_refs)
        turned = jnp.concatenate([dk_ref[...].T, jnp.zeros((narrow, narrow - 128), F32)], axis=1)
        put_halves(turned, groups * share, lower, *out_refs)


def k_add_grads(mine, theirs, mine_late, theirs_late, out):
    rows = mine.shape[1]
    out[:, 0:rows, :] = mine[...] + theirs[...]
    out[:, rows:, :] = mine_late[...] + theirs_late[...]


def k_update(*refs):
    me_ref, zero, one, reduce_zero, reduce_one = refs[:5]
    vecs = refs[5:11]
    params, momenta = refs[11:21], refs[21:31]
    grads, velocity, updated = refs[31:41], refs[41:51], refs[51:61]
    me = me_ref[0]
    share = params[1].shape[1]
    narrow = params[1].shape[2]
    groups = params[3].shape[2] // narrow

    def apply(i, b, grad, where=slice(None)):
        v = MOMENTUM * momenta[i][b, :, where] + grad
        grads[i][b, :, where] = grad
        velocity[i][b, :, where] = v
        updated[i][b, :, where] = params[i][b, :, where] - LEARN_RATE * (grad + MOMENTUM * v)

    packs = (jnp.sum(zero[...], axis=0), jnp.sum(one[...], axis=0))
    for b, (pack, reduce) in enumerate(zip(packs, (reduce_zero, reduce_one))):
        for g in range(groups):
            apply(3, b, pack[g * share : (g + 1) * share], slice(g * narrow, (g + 1) * narrow))
        at = groups * share
        apply(2, b, pack[at : at + share, 0:27])
        at += share
        apply(1, b, pack[at : at + share])
        apply(0, b, jnp.sum(reduce[...], axis=0))
    for j in range(3):
        for r in range(2):
            i = 4 + 2 * j + r
            pieces = []
            for b in range(2):
                value = vecs[2 * j + b][...]
                width = params[i].shape[1]
                length = value.shape[1]
                turned = pltpu.roll(value, length - me * width, 1)
                pieces.append(turned[r : r + 1, 0:width])
            grad = jnp.concatenate(pieces, axis=0)
            v = MOMENTUM * momenta[i][...] + grad
            grads[i][...] = grad
            velocity[i][...] = v
            updated[i][...] = params[i][...] - LEARN_RATE * (grad + MOMENTUM * v)


def put_by_core(dw, me_ref, out_refs):
    if len(out_refs) == 1:
        out_refs[0][...] = dw
    else:
        mine, theirs = out_refs
        dw = dw.reshape(mine.shape[0], 2, *mine.shape[1:])
        lower = me_ref[0] % 2 == 1
        mine[...] = jnp.where(lower, dw[:, 1], dw[:, 0])
        theirs[...] = jnp.where(lower, dw[:, 0], dw[:, 1])


def reduce_grad(ga, x, f, dwt):
    dw = dot3(split2(ga.T), split2(x))

    @pl.when(f == 0)
    def _():
        dwt[...] = dw

    @pl.when(f > 0)
    def _():
        dwt[...] = dwt[...] + dw


def k_between(total, f, steps, me_ref, n1_ref, a_ref, c_ref, x_ref, gz_in, st_in, tv_ref, mom1_ref,
              wr_ref, mom2_ref, tv2_ref, w_ref, momw_ref, smean_ref, gz_ref, u_ref, p_ref, gn_ref,
              st_ref, *refs):
    *dw_refs, wr_parts, w_parts, dwt, bias_acc = refs
    chunk, wide = x_ref.shape
    norm_sums(f, st_in, gn_ref)

    @pl.when(f == 0)
    def _():
        keep_split(wr_ref[...].T, wr_parts)
        keep_split((w_ref[...] * momw_ref[0:1, :]).T, w_parts)

    x = x_ref[...]
    n, a = get(n1_ref, 0, chunk), get(a_ref, 0, chunk)
    ga = norm_back(n, a, tv_ref[27:28, :], mom1_ref, gn_ref, total)
    gy = dot_split(ga, wr_parts, 2) + gz_in[...]
    gz = jnp.where(x > 0.0, gy, 0.0)
    gz_ref[...] = gz
    reduce_grad(ga, x, f, dwt)
    s = centred_act(c_ref, mom2_ref, tv2_ref, smean_ref)
    wide_step(gz, s, f, u_ref, p_ref, bias_acc, w_parts)

    @pl.when(f == steps - 1)
    def _():
        wide_finish(p_ref, w_ref, momw_ref[2:3, :], bias_acc, st_ref)
        put_by_core(dwt[...].T, me_ref, dw_refs)


def k_last_weight(total, f, steps, me_ref, n1_ref, a_ref, x_ref, st_in, tv_ref, mom1_ref, ga_ref,
                  gn_ref, *refs):
    *dw_refs, dwt = refs
    chunk = n1_ref.shape[1]
    norm_sums(f, st_in, gn_ref)
    n, a = get(n1_ref, 0, chunk), get(a_ref, 0, chunk)
    ga = norm_back(n, a, tv_ref[27:28, :], mom1_ref, gn_ref, total)
    put(ga_ref, 0, ga)
    reduce_grad(ga, x_ref[...].reshape(chunk, -1), f, dwt)

    @pl.when(f == steps - 1)
    def _():
        put_by_core(dwt[...].T, me_ref, dw_refs)


def k_last(f, steps, ga_ref, gz_in, wr_ref, gx_ref, wr_parts):
    @pl.when(f == 0)
    def _():
        keep_split(wr_ref[...].T, wr_parts)

    gy = dot_split(get(ga_ref, 0, ga_ref.shape[1]), wr_parts, 2) + gz_in[...]
    gx_ref[...] = gy.reshape(gx_ref.shape)


def exchange(rows):
    return lax.all_to_all(rows, AX, 0, 0)


def meet(value, bits, devices):
    parts = [value]
    for step in range(1, 1 << len(bits)):
        mask = step << bits[0]
        parts.append(lax.ppermute(value, AX, [(i, i ^ mask) for i in range(devices)]))
    return parts


def perm(step, shape):
    dp, fs = shape
    pairs = []
    for i in range(dp):
        for j in range(fs):
            a, b = i + step[0], j + step[1]
            if 0 <= a < dp and 0 <= b < fs:
                pairs.append((i * fs + j, a * fs + b))
    return pairs


def row_halo(field, line, shape):
    low, high = field[:, :line], field[:, field.shape[1] - line :]
    if shape[1] == 2:
        return [swap_cores(jnp.where(lax.axis_index("fsdp") == 0, high, low), shape)]
    move = lambda value, step: lax.ppermute(value, AX, perm(step, shape))
    return [move(high, (0, 1)), move(low, (0, -1))]


def frame_halo(first, last, width, shape, beside):
    count = first.shape[1]
    move = lambda value, step: lax.ppermute(value, AX, perm(step, shape))
    before, after = move(last, (1, 0)), move(first, (-1, 0))
    tops = jnp.stack([before[:, :width], after[:, :width]])
    ends = jnp.stack([before[:, count - width :], after[:, count - width :]])
    tops, ends, *beside = lax.optimization_barrier((tops, ends, *beside))
    if shape[1] == 2:
        corners = [swap_cores(jnp.where(lax.axis_index("fsdp") == 0, ends, tops), shape)]
    else:
        corners = [move(ends, (0, 1)), move(tops, (0, -1))]
    return [before, after, *corners], *beside


def tree_gather(part, devices, name):
    for bits in STAGES[:-1]:
        parts = meet(part, bits, devices)
        dims = (part.shape[0] * len(parts),) + part.shape[1:]
        part = call(k_stack, name, [(dims, HB)], [(piece, VM) for piece in parts], limit=4)[0]
    return meet(part, STAGES[-1], devices)


def core_sums(mine, theirs, shape):
    pairs = [(i, i ^ 1) for i in range(shape[0] * 2)]
    theirs = lax.ppermute(theirs, AX, pairs)
    return call(k_add, "core_add", [(mine.shape, HB)], [(mine, HB), (theirs, VM)], limit=8)[0]


def swap_cores(value, shape):
    return lax.ppermute(value, AX, [(i, i ^ 1) for i in range(shape[0] * 2)])


def k_add(left, right, out):
    out[...] = left[...] + right[...]


def owner_parts(parts, shape):
    return lax.all_to_all(parts, "dp", 0, 0)


HB = pl.BlockSpec(memory_space=pl.ANY)
FILLER = 1 << 31
HIDER = 1 << 32
MINOR = 1 << 27


def pieces(far, near):
    rows = near.shape[0]
    size = 4
    for dim in near.shape:
        size *= dim
    if size < MIB // 2:
        return [(far, near)]
    if len(near.shape) == 3 and rows <= 4:
        return [(far.at[i], near.at[i]) for i in range(rows)]
    if rows % 16 == 0:
        half = rows // 2
        return [(far.at[pl.ds(i * half, half)], near.at[pl.ds(i * half, half)]) for i in range(2)]
    return [(far, near)]


class Stream:
    def __init__(self, axis):
        self.axis = axis

    def part(self, ref, i, steps):
        size = ref.shape[self.axis] // steps
        where = pl.ds(i * size if isinstance(i, int) else pl.multiple_of(i * size, size), size)
        return ref.at[(slice(None),) * self.axis + (where,)]


WIDE, NARROW = Stream(0), Stream(1)
AHEAD = 2


def call(kernel, name, outs, ins, scratch=(), limit=24, steps=None, lazy=None, cost=1000):
    n_i, n_o, n_s = len(ins), len(outs), len(scratch)
    count = steps or 1
    near_i = [i for i in range(n_i) if ins[i][1] not in (SM, VM)]
    whole_i = [i for i in near_i if ins[i][1] is HB]
    flow_i = [i for i in near_i if ins[i][1] is not HB]
    whole_o = [i for i in range(n_o) if outs[i][1] is HB]
    flow_o = [i for i in range(n_o) if outs[i][1] is not HB]

    def run(*refs):
        far_in, far_out = refs[:n_i], refs[n_i : n_i + n_o]
        own = refs[n_i + n_o : n_i + n_o + n_s]
        near = refs[n_i + n_o + n_s : -2]
        sem, flow_sem = refs[-2:]
        in_refs, out_refs = list(far_in), list(near[len(near_i) :])
        for i, ref in zip(near_i, near):
            in_refs[i] = ref
        used = 0
        loads, late, stores = [], [], {}
        for i in whole_i:
            for src, dst in pieces(far_in[i], in_refs[i]):
                copy = pltpu.make_async_copy(src, dst, sem.at[used])
                (late if lazy and i in lazy else loads).append(copy)
                used += 1
        for i in whole_o:
            stores[i] = []
            for dst, src in pieces(far_out[i], out_refs[i]):
                stores[i].append(pltpu.make_async_copy(src, dst, sem.at[used]))
                used += 1
        started = set()

        def flush(i, part=None):
            for k, copy in enumerate(stores[i]):
                if part is None or k == part:
                    started.add((i, k))
                    copy.start()

        def ready():
            for copy in late:
                copy.wait()

        def flow_in(i):
            return [
                pltpu.make_async_copy(
                    ins[j][1].part(far_in[j], i, count),
                    ins[j][1].part(in_refs[j], i, count),
                    flow_sem.at[k, i],
                )
                for k, j in enumerate(flow_i)
            ]

        def flow_out(i):
            return [
                pltpu.make_async_copy(
                    outs[j][1].part(out_refs[j], i, count),
                    outs[j][1].part(far_out[j], i, count),
                    flow_sem.at[len(flow_i) + k, i],
                )
                for k, j in enumerate(flow_o)
            ]

        for copy in loads + late:
            copy.start()
        heavy = any(ins[j][1] is WIDE for j in flow_i)
        ahead = min(AHEAD, count) if heavy else count
        for i in range(ahead):
            for copy in flow_in(i):
                copy.start()
        for copy in loads:
            copy.wait()
        if steps is None:
            kernel(*in_refs, *out_refs, *own, **({} if lazy is None else {"flush": flush, "ready": ready}))
        else:

            def step(i, carry):
                for copy in flow_in(i):
                    copy.wait()
                if count > ahead:

                    @pl.when(i + ahead < count)
                    def _():
                        for copy in flow_in(i + ahead):
                            copy.start()

                views = list(in_refs) + list(out_refs)
                for j in flow_i:
                    views[j] = ins[j][1].part(in_refs[j], i, count)
                for j in flow_o:
                    views[n_i + j] = outs[j][1].part(out_refs[j], i, count)
                kernel(i, count, *views, *own)
                for copy in flow_out(i):
                    copy.start()
                return carry

            lax.fori_loop(0, count, step, 0)
        for i in whole_o:
            for k, copy in enumerate(stores[i]):
                if (i, k) not in started:
                    copy.start()
        for i in range(count):
            for copy in flow_out(i):
                copy.wait()
        for i in whole_o:
            for copy in stores[i]:
                copy.wait()

    values = [
        value if spec in (SM, VM) else pltpu.with_memory_space_constraint(value, pltpu.HBM)
        for value, spec in ins
    ]
    whole = 2 * (len(whole_i) + len(whole_o))
    flows = len(flow_i) + len(flow_o)
    return pl.pallas_call(
        run,
        in_specs=[spec if spec in (SM, VM) else HB for _, spec in ins],
        out_specs=(HB,) * n_o,
        out_shape=tuple(pltpu.HBM(shape, F32) for shape, _ in outs),
        scratch_shapes=[pltpu.VMEM(shape, dtype) for shape, dtype in scratch]
        + [pltpu.VMEM(ins[i][0].shape, F32) for i in near_i]
        + [pltpu.VMEM(shape, F32) for shape, _ in outs]
        + [pltpu.SemaphoreType.DMA((max(whole, 1),)), pltpu.SemaphoreType.DMA((max(flows, 1), count))],
        compiler_params=params(limit),
        cost_estimate=pl.CostEstimate(flops=cost, bytes_accessed=1000, transcendentals=0),
        name=name,
    )(*values)


def body(inputs, cotangent, clip_index, *args):
    weights, momenta = args[:10], args[10:]
    frames, rows, width, wide = inputs.shape
    narrow = weights[0].shape[2]
    halves = narrow // 128
    shape = (lax.axis_size("dp"), lax.axis_size("fsdp"))
    devices = shape[0] * shape[1]
    rank = lax.axis_index(AX)
    voxels = frames * rows * width
    line = width * frames
    total = float(voxels * devices)
    many = 7 if voxels % (7 * 8 * frames) == 0 else 1
    x0 = inputs.transpose(1, 2, 0, 3)
    cot = cotangent.transpose(1, 2, 0, 3)

    edge = jnp.full((1,), -1, jnp.int32)
    window = lax.dynamic_slice_in_dim(
        jnp.concatenate([edge, clip_index, edge]), lax.axis_index("dp") * frames, frames + 2
    )
    centre = window[1:-1]
    flags = jnp.concatenate(
        [
            (window[:-2] == centre).astype(F32),
            jnp.ones((frames,), F32),
            (window[2:] == centre).astype(F32),
            (lax.axis_index("fsdp") > 0).astype(F32)[None],
            (lax.axis_index("fsdp") < shape[1] - 1).astype(F32)[None],
        ]
    )
    me = rank.astype(jnp.int32)[None]

    field_n = (halves, voxels, 128)
    grown_n = (halves, voxels + 2 * line, 128)
    face_n = (halves, voxels // frames, 128)
    field_w = (voxels, wide)
    stat_n = (devices, 2 * halves, 128)
    stat_e = (devices, (narrow + wide) // 128, 128)
    stat_w = (devices, 2 * wide // 128, 128)
    mom_n, mom_w = (8, narrow), (8, wide)
    down_r, down_m, down_e = (wide, narrow), (narrow, narrow), (narrow, wide)
    parts = lambda *values: [(value, NARROW) for value in values]

    near = lambda *values: [(value, HB) for value in values]
    here = lambda *values: [(value, VM) for value in values]
    fix = near
    owned = devices == 32
    half = (devices // 2, wide // devices, narrow)
    down_halves = (half, half) if owned else (down_r,)
    share = narrow // devices
    side = (devices // 2, share * (wide // narrow + 1), narrow)
    side_halves = (side, side) if owned else (down_e, (128, narrow))
    mixed_halves = ((devices // 2, share, narrow),) * 2 if owned else (down_m,)

    def first(wr0):
        return call(
            functools.partial(k_first, frames),
            "first",
            [(field_n, NARROW), (face_n, NARROW), (face_n, NARROW)] + near(stat_n, down_r),
            [(me, SM), (x0, WIDE)] + (here if owned else near)(*wr0),
            scratch=[((3 * wide, narrow), BF16), (mom_n, F32)],
            limit=48,
            steps=many,
        )

    if owned:
        share_n, share_w = weights[1].shape[1], weights[0].shape[1]
        early, late = call(
            k_pack,
            "pack",
            near(
                (1, share_w + 2 * share_n, narrow),
                (2 * share_w + share_n * (1 + 2 * (wide // narrow)), narrow),
            ),
            near(*weights),
            limit=4,
        )
        wr0 = slots = tree_gather(early, devices, "stack")
        late = lax.all_gather(late, AX, axis=0, tiled=False)
        a0, *faces, st, wr0 = first(wr0)
        wm0, tv = call(
            k_open_early,
            "open_early",
            near(down_m, (2, 32, narrow)),
            [(me, SM)] + near(*slots),
            scratch=[((narrow, 128), F32)],
            limit=8,
            cost=FILLER,
        )
        wr1, wm1, we0, we1, vw = call(
            k_open_later,
            "open_later",
            near(down_r, down_m, down_e, down_e, (2, 8, wide)),
            near(late),
            limit=16,
            cost=FILLER,
        )
    else:
        gather = lambda part: lax.all_gather(part, AX, axis=0, tiled=True)
        wr0, wr1 = [gather(weights[0][0])], gather(weights[0][1])
        wm0, wm1 = gather(weights[1][0]), gather(weights[1][1])
        we0, we1 = gather(weights[3][0]), gather(weights[3][1])
        small = jnp.concatenate([weights[2]] + [weights[i][..., None] for i in (4, 5, 6, 7)], axis=2)
        small = gather(small.transpose(1, 0, 2))
        tv = jnp.pad(small.transpose(1, 2, 0), ((0, 0), (0, 1), (0, 0)))
        large = gather(jnp.stack([weights[8], weights[9]], axis=2).transpose(1, 0, 2))
        vw = jnp.pad(large.transpose(1, 2, 0), ((0, 0), (0, 6), (0, 0)))

    def mix_own(block, a, rows, st, wm):
        return call(
            functools.partial(k_mix_own, line, frames, total),
            "mix_own",
            near(field_n, grown_n, grown_n, grown_n, mom_n),
            [(flags, SM)] + near(a) + here(*rows, st) + near(wm, tv[block]),
            scratch=[((halves, 27, 8, 128), F32)],
            limit=20,
            lazy=(),
            cost=MINOR,
        )

    def mix_halo(block, part, halos, mom, wm):
        return call(
            functools.partial(k_mix, line, frames),
            "mix",
            near(field_n, grown_n, stat_n),
            [(flags, SM)]
            + near(part, *halos[:2])
            + here(*halos[2:])
            + near(mom, wm, tv[block]),
            scratch=[((halves, 9, 8, 128), F32)],
            limit=20,
            lazy=(1,),
        )

    def mix(block, a, faces, st, wm):
        own = mix_own(block, a, row_halo(a, line, shape), st, wm)
        halos, part, *grown, mom = frame_halo(*faces, width, shape, own)
        c, placed, st = mix_halo(block, part, halos, mom, wm)
        return c, grown + [placed], mom, st

    def expand(block, c, st, we):
        return call(
            functools.partial(k_expand, line, total),
            "expand",
            near(mom_n, mom_w, mom_n, down_e, stat_e),
            near(c) + here(st) + near(we, tv[block]),
            scratch=[((voxels, narrow), F32)],
            limit=20,
        )

    def widen(block, c, mom2, sloc, we):
        return call(
            k_widen,
            "widen",
            [(field_w, WIDE)],
            [(c, NARROW)] + near(mom2, tv[block], sloc, we),
            scratch=[((3 * narrow, wide), BF16)],
            limit=48,
            steps=many,
            cost=FILLER,
        )[0]

    def join(e, x, st, off, we, wr):
        return call(
            functools.partial(k_join, frames, total, float(voxels)),
            "join",
            [(field_w, WIDE), (field_n, NARROW), (face_n, NARROW), (face_n, NARROW)]
            + near(mom_w, mom_n, stat_n),
            [(e, WIDE), (x, WIDE)] + here(st) + near(off, we, vw[0], wr),
            scratch=[((3 * wide, narrow), BF16), (mom_n, F32)],
            limit=56,
            steps=many,
        )

    def turn(e, x, c, st, off, we, mom2):
        return call(
            functools.partial(k_turn, total, float(voxels)),
            "turn",
            [((rows, width, frames, wide), WIDE), (field_w, WIDE), (field_n, NARROW)]
            + near(down_e, mom_w, mom_n, mom_w, stat_w),
            [(e, WIDE), (x, WIDE), (cot, WIDE), (c, NARROW)]
            + here(st)
            + near(off, we, vw[1], mom2, tv[1]),
            scratch=[((2 * wide, narrow), BF16), (mom_w, F32)],
            limit=58,
            steps=many,
        )

    def stat_with(more):
        return (devices, 2 * halves + sum(value.shape[-2] for value in more), 128)

    def second(block, u, c, st, we, momw, smean, mom2, *more):
        return call(
            functools.partial(k_second, total),
            "second",
            parts(field_n) + near(mom_w, stat_with(more)),
            parts(u, c) + here(st) + near(we, momw, smean, mom2, tv[block], *more),
            scratch=[((2 * narrow, narrow), BF16), (mom_n, F32)],
            limit=24,
            steps=many,
        )

    def center(block, n, c, st, mom2):
        return call(
            functools.partial(k_center, frames, total),
            "center",
            [(field_n, NARROW), (face_n, NARROW), (face_n, NARROW)]
            + near(mom_n, *([(st.shape[1] - 2 * halves, 128)] if st.shape[1] > 2 * halves else [])),
            parts(n, c) + here(st) + near(tv[block], mom2),
            limit=24,
            steps=many,
        )

    def first_back(block, gc, halos, a, wm, mom1, *more):
        return call(
            functools.partial(k_first_back, line, frames, len(more)),
            "first_back",
            near(field_n, stat_with(more), *mixed_halves),
            [(flags, SM)]
            + near(gc, *halos[:2])
            + here(*halos[2:])
            + near(a, wm, tv[block], mom1, *more),
            scratch=[(field_n, F32)] + [(grown_n, F32)] * 3
            + [((halves, 27, 8, 128), F32), (down_m, F32)],
            limit=20,
            lazy=(2 + len(halos), 3 + len(halos), 5 + len(halos)),
        )

    def side_grads(gc, grown, p, we, gw, momw, smean, sloc, seen):
        return call(
            functools.partial(k_side_grads, line, frames, total),
            "side_grads",
            near(*side_halves),
            [(flags, SM)] + near(gc, *grown, p, we, gw, momw, smean, sloc, seen),
            scratch=[((128, narrow), F32)],
            limit=24,
            cost=HIDER,
        )

    def add_grads(mine, theirs, mine_late, theirs_late):
        dims = (mine.shape[0], mine.shape[1] + mine_late.shape[1], narrow)
        return call(
            k_add_grads,
            "add_grads",
            near(dims),
            near(mine) + here(theirs) + near(mine_late) + here(theirs_late),
            limit=12,
        )[0]

    def between(n1, a, st, mom1, wr, x, gz, c, mom2, we, momw, smean):
        return call(
            functools.partial(k_between, total),
            "between",
            [(field_w, WIDE), (field_n, NARROW)] + near(down_e, mom_n, stat_w, *down_halves),
            [(me, SM)]
            + parts(n1, a, c)
            + [(x, WIDE), (gz, WIDE)]
            + here(st)
            + near(tv[1], mom1, wr, mom2, tv[0], we, momw, smean),
            scratch=[((2 * narrow, wide), BF16), ((2 * wide, narrow), BF16), (down_e, F32),
                     (mom_w, F32)],
            limit=58,
            steps=many,
        )

    def last_weight(n1, a, st, mom1):
        return call(
            functools.partial(k_last_weight, total),
            "last_weight",
            [(field_n, NARROW)] + near(mom_n, *down_halves),
            [(me, SM)] + parts(n1, a) + [(x0, WIDE)] + here(st) + near(tv[0], mom1),
            scratch=[(down_e, F32)],
            limit=48,
            steps=many,
        )

    def last(ga, gz, wr):
        return call(
            k_last,
            "last",
            [((rows, width, frames, wide), WIDE)],
            [(ga, NARROW), (gz, WIDE)] + near(wr),
            scratch=[((2 * narrow, wide), BF16)],
            limit=48,
            steps=many,
            cost=FILLER,
        )[0]


    if not owned:
        a0, *faces, st, wr0 = first(wr0)
    c0, grown0, mom10, st = mix(0, a0, faces, exchange(st), wm0)
    mom20, off0, sloc0, seen0, st = expand(0, c0, exchange(st), we0)
    e0 = widen(0, c0, mom20, sloc0, we0)
    x1, a1, *faces, momw0, smean0, st = join(e0, x0, exchange(st), off0, we0, wr1)
    c1, grown1, mom11, st = mix(1, a1, faces, exchange(st), wm1)
    mom21, off1, sloc1, seen1, st = expand(1, c1, exchange(st), we1)
    e1 = widen(1, c1, mom21, sloc1, we1)
    out, gz1, u1, p1, momw1, smean1, pool, st = turn(
        e1, x1, c1, exchange(st), off1, we1, mom21
    )

    clips = clip_index.shape[0] // 6
    labels = jnp.arange(clips, dtype=jnp.int32)
    hot = (centre[None, :] == labels[:, None]).astype(F32)
    pooled = jnp.dot(
        jnp.concatenate([hot] * (8 // frames), axis=1), pool, precision=HIGHEST,
        preferred_element_type=F32,
    )
    if owned:
        room = -(-clips * share_w // 128) * 128
        pooled = pooled.reshape(clips, devices, share_w).transpose(1, 0, 2).reshape(devices, -1)
        pooled = jnp.pad(pooled, ((0, 0), (0, room - clips * share_w)))
        more = (pooled.reshape(devices, room // 128, 128),)
    else:
        more = ()
        pooled = lax.psum(pooled, AX)
    counts = jnp.sum((clip_index[None, :] == labels[:, None]).astype(F32), axis=1)

    n, gw1, st = second(1, u1, c1, exchange(st), we1, momw1, smean1, mom21, *more)
    gc, face_f, face_l, gd1, *more = center(1, n, c1, exchange(st), mom21)
    faces = (face_f, face_l)
    side1 = side_grads(gc, grown1, p1, we1, gw1, momw1, smean1, sloc1, seen1)
    halos, *side1 = frame_halo(*faces, width, shape, side1)
    halos = halos[:2] + row_halo(gc, line, shape) + halos[2:]
    n1, st, *dm1 = first_back(1, gc, halos, a1, wm1, mom11, *more)
    st = exchange(st)
    if owned:
        one = add_grads(
            side1[0], swap_cores(side1[1], shape), dm1[0], swap_cores(dm1[1], shape)
        )
        one, st = lax.optimization_barrier((one, st))
        one = owner_parts(one, shape)
        pooled = st[:, 2 * halves :, :].reshape(devices, -1)[:, : clips * share_w]
        pooled = pooled.reshape(devices, clips, share_w).transpose(1, 0, 2).reshape(clips, wide)
    gz0, u0, p0, gn1, st, *dr1 = between(
        n1, a1, st, mom11, wr1, x1, gz1, c0, mom20, we0, momw0, smean0
    )
    if owned:
        st, one = lax.optimization_barrier((st, one))
    st = exchange(st)
    if owned:
        dr1 = core_sums(*dr1, shape)
        dr1, st = lax.optimization_barrier((dr1, st))
        dr1 = owner_parts(dr1, shape)
    n, gw0, st = second(0, u0, c0, st, we0, momw0, smean0, mom20)
    gc, *faces, gd0 = center(0, n, c0, exchange(st), mom20)
    side0 = side_grads(gc, grown0, p0, we0, gw0, momw0, smean0, sloc0, seen0)
    halos, *side0 = frame_halo(*faces, width, shape, side0)
    halos = halos[:2] + row_halo(gc, line, shape) + halos[2:]
    n1, st, *dm0 = first_back(0, gc, halos, a0, wm0, mom10)
    st = exchange(st)
    home = lambda field: field.transpose(2, 0, 1, 3)
    if owned:
        zero = add_grads(
            side0[0], swap_cores(side0[1], shape), dm0[0], swap_cores(dm0[1], shape)
        )
        zero, n1, dr1 = lax.optimization_barrier((zero, n1, dr1))
        zero = owner_parts(zero, shape)
        ga0, gn0, mine, theirs = last_weight(n1, a0, st, mom10)
        tail = owner_parts(core_sums(mine, theirs, shape), shape)
        gx = last(ga0, gz0, wr0)
        pooled = pooled / (counts * float(rows * shape[1] * width))[:, None]
        values = call(
            k_update,
            "update",
            near(*[weights[i].shape for i in range(10)] * 3),
            [(me, SM)]
            + near(zero, one, tail, dr1, gn0, gn1, gd0, gd1, gw0, gw1, *weights, *momenta),
            limit=12,
        )
        return (home(out), pooled, home(gx), *values)

    ga0, gn0, dr0 = last_weight(n1, a0, st, mom10)
    gx = last(ga0, gz0, wr0)
    (de0, dk0), (de1, dk1), dm0, dm1 = side0, side1, dm0[0], dm1[0]
    pooled = pooled / (counts * float(rows * shape[1] * width))[:, None]

    def own(full):
        parts = full.reshape((devices, full.shape[0] // devices) + full.shape[1:])
        return jnp.sum(lax.all_to_all(parts, AX, 0, 0), axis=0)

    deltas = [
        jnp.stack([own(dr0), own(dr1[0])]),
        jnp.stack([own(dm0), own(dm1)]),
        jnp.stack([own(dk0[:27].T), own(dk1[:27].T)]),
        jnp.stack([own(de0), own(de1)]),
    ]

    def mine(vec0, vec1, row):
        share = vec0.shape[1] // devices
        both = jnp.stack([vec0[row], vec1[row]])
        return lax.dynamic_slice_in_dim(both, rank * share, share, axis=1)

    for first_part, second_part in ((gn0, gn1), (gd0, gd1), (gw0, gw1)):
        deltas.append(mine(first_part, second_part, 0))
        deltas.append(mine(first_part, second_part, 1))
    velocity = [MOMENTUM * momenta[i] + deltas[i] for i in range(10)]
    updated = [
        weights[i] - LEARN_RATE * (deltas[i] + MOMENTUM * velocity[i]) for i in range(10)
    ]
    return (home(out), pooled, home(gx), *deltas, *velocity, *updated)


def solution(mesh):
    field = P("dp", "fsdp", None, None)
    mat = P(None, AX, None)
    vec = P(None, AX)
    group = (mat,) * 4 + (vec,) * 6
    return jax.shard_map(
        body,
        mesh=mesh,
        in_specs=(field, field, P()) + group * 2,
        out_specs=(field, P(), field) + group * 3,
        check_vma=False,
    )
```

```python
import functools

import jax
import jax.numpy as jnp
from jax import lax
from jax.experimental import pallas as pl
from jax.experimental.pallas import tpu as pltpu
from jax.sharding import PartitionSpec as P

EPSILON = 1e-05
MOMENTUM = 0.9
LEARN_RATE = 0.0001
HIGHEST = lax.Precision.HIGHEST
AX = ("dp", "fsdp")
F32 = jnp.float32
BF16 = jnp.bfloat16
MIB = 1 << 20


VM = pl.BlockSpec(memory_space=pltpu.VMEM)
SM = pl.BlockSpec(memory_space=pltpu.SMEM)


def params(mib):
    return pltpu.CompilerParams(vmem_limit_bytes=mib * MIB)


def dot6(left, right):
    return jnp.dot(left, right, precision=HIGHEST, preferred_element_type=F32)


def dot6_rt(left, right):
    return lax.dot_general(
        left, right, (((1,), (1,)), ((), ())), precision=HIGHEST, preferred_element_type=F32
    )


def split2(value):
    high = value.astype(BF16)
    return high, (value - high.astype(F32)).astype(BF16)


def dot3(left, right):
    lh, ll = left
    rh, rl = right
    mm = functools.partial(jnp.dot, preferred_element_type=F32)
    return mm(lh, rh) + (mm(lh, rl) + mm(ll, rh))


def keep_split(value, parts_ref):
    rows = value.shape[0]
    for i in range(parts_ref.shape[0] // rows):
        high = value.astype(BF16)
        parts_ref[i * rows : (i + 1) * rows, :] = high
        value = value - high.astype(F32)


def dot_split(left, parts_ref, count):
    rows = parts_ref.shape[0] // count
    right = [parts_ref[i * rows : (i + 1) * rows, :] for i in range(count)]
    pieces = []
    for i in range(count):
        high = left.astype(BF16)
        pieces.append(high)
        left = left - high.astype(F32)
    mm = functools.partial(jnp.dot, preferred_element_type=F32)
    total = mm(pieces[0], right[1]) + mm(pieces[1], right[0])
    if count == 3:
        low = mm(pieces[1], right[1]) + mm(pieces[0], right[2]) + mm(pieces[2], right[0])
        total = total + low
    return mm(pieces[0], right[0]) + total


def total_rows(value):
    return jnp.sum(value, axis=0, keepdims=True)


def get(ref, start, count):
    return jnp.concatenate([ref[h, pl.ds(start, count), :] for h in range(ref.shape[0])], axis=1)


def put(ref, start, value):
    count = value.shape[0]
    for h in range(ref.shape[0]):
        ref[h, pl.ds(start, count), :] = value[:, h * 128 : h * 128 + 128]


def put_rows(st_ref, first, vec):
    for i in range(vec.shape[1] // 128):
        piece = vec[:, i * 128 : (i + 1) * 128]
        st_ref[:, first + i, :] = jnp.broadcast_to(piece, (st_ref.shape[0], 128))


def take_rows(st_ref, first, channels):
    return jnp.concatenate([st_ref[:, first + i, :] for i in range(channels // 128)], axis=1)


def take_sum(st_ref, first, channels):
    return total_rows(take_rows(st_ref, first, channels))


def narrow_moments(st_ref, channels, local, total):
    sums = take_rows(st_ref, 0, channels)
    squares = take_rows(st_ref, channels // 128, channels)
    mean = total_rows(sums) / total
    off = sums / local - mean
    var = (total_rows(squares) + local * total_rows(off * off)) / total
    return mean, lax.rsqrt(var + EPSILON)


def chunk_loop(voxels, chunk, step, carry):
    def one(i, carry):
        return step(pl.multiple_of(i * chunk, chunk), carry)

    return lax.fori_loop(0, voxels // chunk, one, carry)


def local_moments(ref, chunk):
    halves, voxels, _ = ref.shape
    zero = jnp.zeros((1, halves * 128), F32)
    total = chunk_loop(voxels, chunk, lambda i, acc: acc + total_rows(get(ref, i, chunk)), zero)
    mean = total / float(voxels)

    def squares(i, acc):
        value = get(ref, i, chunk) - mean
        return acc + total_rows(value * value)

    return total, chunk_loop(voxels, chunk, squares, zero)


def put_faces(ref, first, last, frames, start=0):
    halves = ref.shape[0]
    count = (ref.shape[1] - 2 * start) // frames
    for face, frame in ((first, 0), (last, frames - 1)):
        for h in range(halves):
            face[h, 0:count, :] = ref[h, pl.ds(start + frame, count, stride=frames), :]


STAGES = ((3, 4), (1, 2), (0,))


def slot_mask(slot):
    mask = 0
    for bits in STAGES:
        mask |= (slot & ((1 << len(bits)) - 1)) << bits[0]
        slot >>= len(bits)
    return mask


def order_rows(stacks, out_ref, me, first, rows, lanes=slice(None)):
    slot = 0
    for stack in stacks:
        for s in range(stack.shape[0]):
            where = pl.multiple_of(jnp.bitwise_xor(me, slot_mask(slot)) * rows, rows)
            out_ref[pl.ds(where, rows), :] = stack[s, first : first + rows, lanes]
            slot += 1


def k_stack(*refs):
    *parts, out = refs
    at = 0
    for part in parts:
        out[at : at + part.shape[0]] = part[...]
        at += part.shape[0]


def as_column(row):
    n = row.shape[1]
    same = lax.broadcasted_iota(jnp.int32, (n, n), 0) == lax.broadcasted_iota(jnp.int32, (n, n), 1)
    return jnp.sum(jnp.where(same, jnp.broadcast_to(row, (n, n)), 0.0), axis=1, keepdims=True)


def k_pack(wr, wm, dw, we, g1, b1, g2, b2, g3, b3, t1, t2):
    share, narrow = wm.shape[1:]
    share_w = wr.shape[1]
    wide = we.shape[2]
    t1[0, 0:share_w, :] = wr[0]
    t1[0, share_w : share_w + share, :] = wm[0]
    lane = lax.broadcasted_iota(jnp.int32, (share, narrow), 1)
    blocks = []
    for b in range(2):
        block = jnp.concatenate([dw[b], jnp.zeros((share, narrow - 27), F32)], axis=1)
        for i, vec in enumerate((g1, b1, g2, b2)):
            block = jnp.where(lane == 27 + i, as_column(vec[b : b + 1, :]), block)
        blocks.append(block)
    block = jnp.where(lane < 32, blocks[0], pltpu.roll(blocks[1], 32, 1))
    for c, (vec, b) in enumerate(((g3, 0), (b3, 0), (g3, 1), (b3, 1))):
        column = as_column(vec[b : b + 1, :])
        for q in range(share_w // share):
            part = column[q * share : (q + 1) * share]
            block = jnp.where(lane == 64 + 8 * q + c, part, block)
    t1[0, share_w + share :, :] = block
    t2[0:share_w, :] = wr[1]
    t2[share_w : share_w + share, :] = wm[1]
    at = share_w + share
    for b in range(2):
        for q in range(wide // narrow):
            t2[at : at + share, :] = we[b, :, q * narrow : (q + 1) * narrow]
            at += share


def k_open_early(me_ref, mine, theirs, wm, tv, vw, scr):
    narrow = wm.shape[0]
    share = scr.shape[0] // (mine.shape[0] * 2)
    share_w = mine.shape[1] - 2 * share
    order_rows((mine, theirs), wm, me_ref[0], share_w, share)
    order_rows((mine, theirs), scr, me_ref[0], share_w + share, share, slice(0, 128))
    turned = scr[...].T
    tv[0] = turned[0:32]
    tv[1] = turned[32:64]
    groups = share_w // share
    lane = lax.broadcasted_iota(jnp.int32, (8, 128), 1)
    for t in range(vw.shape[2] // 128):
        value = jnp.zeros((8, 128), F32)
        for d in range(128 // share_w):
            for q in range(groups):
                source = (t * (128 // share_w) + d) * share
                target = d * share_w + q * share
                moved = pltpu.roll(turned[64 + 8 * q : 72 + 8 * q], (target - source) % narrow, 1)
                here = jnp.logical_and(lane >= target, lane < target + share)
                value = jnp.where(here, moved[:, 0:128], value)
        vw[0, 0:2, t * 128 : (t + 1) * 128] = value[0:2]
        vw[1, 0:2, t * 128 : (t + 1) * 128] = value[2:4]


def k_open_later(later, wr, wm, we0, we1):
    wide, narrow = wr.shape
    devices = later.shape[0]
    share, share_w = narrow // devices, wide // devices
    wr[...] = later[:, 0:share_w, :].reshape(wide, narrow)
    wm[...] = later[:, share_w : share_w + share, :].reshape(narrow, narrow)
    at = share_w + share
    for we in (we0, we1):
        for q in range(wide // narrow):
            piece = later[:, at : at + share, :]
            we[:, q * narrow : (q + 1) * narrow] = piece.reshape(narrow, narrow)
            at += share


def run_moments(f, value, acc_ref):
    count = float(value.shape[0])
    total = total_rows(value)
    mean = total / count
    apart = value - mean
    squares = total_rows(apart * apart)

    @pl.when(f == 0)
    def _():
        acc_ref[0:1, :] = total
        acc_ref[1:2, :] = squares

    @pl.when(f > 0)
    def _():
        done = f.astype(F32) * count
        seen = acc_ref[0:1, :]
        delta = mean - seen / done
        acc_ref[1:2, :] = acc_ref[1:2, :] + squares + delta * delta * (done * count / (done + count))
        acc_ref[0:1, :] = seen + total


def put_narrow(f, steps, a, a_ref, face_f, face_l, st_ref, acc_ref, frames):
    put(a_ref, 0, a)
    put_faces(a_ref, face_f, face_l, frames)
    run_moments(f, a, acc_ref)

    @pl.when(f == steps - 1)
    def _():
        put_rows(st_ref, 0, acc_ref[0:1, :])
        put_rows(st_ref, a_ref.shape[0], acc_ref[1:2, :])


def k_first(frames, f, steps, me_ref, x_ref, *refs):
    *w_refs, a_ref, face_f, face_l, st_ref, w_out, w_parts, acc_ref = refs
    wide = x_ref.shape[3]
    chunk = a_ref.shape[1]

    @pl.when(f == 0)
    def _():
        if len(w_refs) == 2:
            order_rows(w_refs, w_out, me_ref[0], 0, wide // (2 * w_refs[0].shape[0]))
        else:
            w_out[...] = w_refs[0][...]
        keep_split(w_out[...], w_parts)

    a = dot_split(x_ref[...].reshape(chunk, wide), w_parts, 3)
    put_narrow(f, steps, a, a_ref, face_f, face_l, st_ref, acc_ref, frames)


def finish_narrow(a_ref, st_ref, line):
    total, squares = local_moments(a_ref, line)
    put_rows(st_ref, 0, total)
    put_rows(st_ref, a_ref.shape[0], squares)


def by_frame(keep_ref, o, frames):
    frame = lax.broadcasted_iota(jnp.int32, (8, 128), 0) % frames
    value = jnp.zeros((8, 128), F32)
    for f in range(frames):
        value = jnp.where(frame == f, keep_ref[o * frames + f], value)
    return value


def make_taps(k_ref, keep_ref, wt_ref, frames, flipped):
    for o in range(3):
        keep = by_frame(keep_ref, o, frames)
        for i in range(9):
            tap = 9 * o + i
            source = 26 - tap if flipped else tap
            for h in range(wt_ref.shape[0]):
                row = k_ref[source : source + 1, h * 128 : h * 128 + 128]
                wt_ref[h, tap] = jnp.broadcast_to(row, (8, 128)) * keep


def frame_of(rows, frames):
    return lax.broadcasted_iota(jnp.int32, (rows // 8, 8, 128), 1) % frames


def shift_frames(field, before, after, line, frames):
    halves, voxels, _ = field.shape
    frame = frame_of(line, frames)

    def step(i, carry):
        for h in range(halves):
            value = field[h, pl.ds(i, line), :].reshape(line // 8, 8, 128)
            earlier = jnp.where(frame == 0, 0.0, pltpu.roll(value, 1, 1))
            later = jnp.where(frame == frames - 1, 0.0, pltpu.roll(value, 7, 1))
            before[h, pl.ds(i, line), :] = earlier.reshape(line, 128)
            after[h, pl.ds(i, line), :] = later.reshape(line, 128)
        return carry

    chunk_loop(voxels, line, step, 0)


def put_frames(target, frame, frames, pieces_):
    start = 0
    for piece in pieces_:
        count = piece.shape[0]
        for h in range(target.shape[0]):
            part = piece[:, h * 128 : h * 128 + 128]
            target[h, pl.ds(start * frames + frame, count, stride=frames), :] = part
        start += count


def place_frames(target, line, frames, halos):
    halves, voxels, _ = target.shape

    def clear(i, carry):
        for h in range(halves):
            target[h, pl.ds(i, line), :] = jnp.zeros((line, 128), F32)
        return carry

    chunk_loop(voxels, line, clear, 0)
    put_frames(target, 0, frames, halos[0])
    put_frames(target, frames - 1, frames, halos[1])


def make_halo_taps(k_ref, keep_ref, wt_ref, frames, flipped):
    frame = lax.broadcasted_iota(jnp.int32, (8, 128), 0) % frames
    for i in range(9):
        for h in range(wt_ref.shape[0]):
            value = jnp.zeros((8, 128), F32)
            for o, place in ((0, 0), (2, frames - 1)):
                tap = 26 - (9 * o + i) if flipped else 9 * o + i
                row = k_ref[tap : tap + 1, h * 128 : h * 128 + 128] * keep_ref[o * frames + place]
                value = jnp.where(frame == place, jnp.broadcast_to(row, (8, 128)), value)
            wt_ref[h, i] = value


def column_views(value, first, last):
    n = value.shape[0] - 2
    upper = lax.broadcasted_iota(jnp.int32, (n, 8, 128), 1) < 4
    turned = pltpu.roll(value, 4, 1)
    left = jnp.where(upper, turned[0:n], turned[1 : n + 1])
    right = jnp.where(upper, turned[1 : n + 1], turned[2:])
    return left, value[1 : n + 1], right


def line_views(ref, h, start, line, part, parts):
    n = line // 8 // parts
    zero = jnp.zeros((1, 8, 128), F32)
    pieces = []
    if part == 0:
        pieces.append(zero)
    low = part * n - (part > 0)
    high = (part + 1) * n + (part < parts - 1)
    body = ref[h, pl.ds(start + low * 8, (high - low) * 8), :]
    pieces.append(body.reshape(high - low, 8, 128))
    if part == parts - 1:
        pieces.append(zero)
    value = jnp.concatenate(pieces, axis=0) if len(pieces) > 1 else pieces[0]
    return column_views(value, part == 0, part == parts - 1)


def stencil_into(fields, wt_ref, out_ref, line, base=None, done_half=None):
    halves, voxels, _ = out_ref.shape
    rows = voxels // line
    parts = 2 if (line // 8) % 2 == 0 else 1
    n = line // 8 // parts
    for h in range(halves):
        for part in range(parts):

            def row(j, older, old):
                new = jnp.zeros((n, 8, 128), F32)
                start = pl.multiple_of(j * line, line)
                for o in range(len(fields)):
                    views = line_views(fields[o], h, start, line, part, parts)
                    for q in range(3):
                        older = older + views[q] * wt_ref[h, 9 * o + 6 + q][None]
                        old = old + views[q] * wt_ref[h, 9 * o + 3 + q][None]
                        new = new + views[q] * wt_ref[h, 9 * o + q][None]
                return older, old, new

            zero = jnp.zeros((n, 8, 128), F32)

            def step(j, accs):
                done, old, new = row(j, accs[0], accs[1])

                @pl.when(j >= 2)
                def _():
                    where = pl.multiple_of((j - 2) * line, line) + part * n * 8
                    where = pl.ds(pl.multiple_of(where, 8), n * 8)
                    value = done.reshape(n * 8, 128)
                    if base is not None:
                        value = value + base[h, where, :]
                    out_ref[h, where, :] = value

                return old, new

            lax.fori_loop(0, rows + 2, step, (zero, zero))
        if done_half is not None:
            done_half(h)


def halo_pieces(i, face, up, down, top, bottom, act):
    edge = up.shape[2]
    above = act(get(up.at[i], 0, edge))
    below = above if down is up else act(get(down.at[i], 0, edge))
    return above * top, act(get(face, 0, face.shape[1])), below * bottom


def both(refs):
    return (refs[0], refs[-1])


def part_of(voxels, line):
    for count in (4, 2):
        if voxels % (count * 8) == 0:
            return voxels // count
    return voxels


def first_act(a, mom_ref, tv_ref):
    scale = tv_ref[27:28, :] * mom_ref[1:2, :]
    return jnp.maximum((a - mom_ref[0:1, :]) * scale + tv_ref[28:29, :], 0.0)


def k_mix_own(line, frames, total, keep_ref, a_ref, *refs, flush, ready):
    c_ref, mp_ref, before, after, mom_ref, wt_ref = refs[-6:]
    *rows, st_in, w_ref, tv_ref = refs[:-6]
    up_ref, dn_ref = both(rows)
    halves, voxels, _ = a_ref.shape
    narrow = halves * 128
    mean, inverse = narrow_moments(st_in, narrow, float(voxels), total)
    mom_ref[0:1, :] = mean
    mom_ref[1:2, :] = inverse

    def mixed(value):
        return dot6(first_act(value, mom_ref, tv_ref), w_ref[...])

    chunk = part_of(voxels, line)

    def own(i, carry):
        put(mp_ref, pl.multiple_of(line + i, 8), mixed(get(a_ref, i, chunk)))
        return carry

    chunk_loop(voxels, chunk, own, 0)
    ready()
    above = mixed(get(up_ref, 0, line))
    below = above if dn_ref is up_ref else mixed(get(dn_ref, 0, line))
    put(mp_ref, 0, above * keep_ref[3 * frames])
    put(mp_ref, line + voxels, below * keep_ref[3 * frames + 1])
    flush(1)
    make_taps(tv_ref, keep_ref, wt_ref, frames, False)
    shift_frames(mp_ref, before, after, line, frames)
    flush(2)
    flush(3)
    stencil_into((before, mp_ref, after), wt_ref, c_ref, line, None, lambda h: flush(0, h))


def k_mix(line, frames, keep_ref, part_ref, hp_ref, hn_ref, *refs, flush, ready):
    c_ref, placed, st_ref, wt_ref = refs[-4:]
    *corners, mom_ref, w_ref, tv_ref = refs[:-4]
    cu_ref, cd_ref = both(corners)
    top = keep_ref[3 * frames]
    bottom = keep_ref[3 * frames + 1]
    halos = [
        halo_pieces(
            i, face, cu_ref, cd_ref, top, bottom,
            lambda value: dot6(first_act(value, mom_ref, tv_ref), w_ref[...]),
        )
        for i, face in enumerate((hp_ref, hn_ref))
    ]
    place_frames(placed, line, frames, halos)
    flush(1)
    make_halo_taps(tv_ref, keep_ref, wt_ref, frames, False)
    ready()
    stencil_into((placed,), wt_ref, c_ref, line, part_ref, lambda h: flush(0, h))
    finish_narrow(c_ref, st_ref, line)


def second_act(c, mom, tv):
    return (c - mom[0:1, :]) * (tv[29:30, :] * mom[1:2, :]) + tv[30:31, :]


def k_expand(line, total, c_ref, st_in, w_ref, tv_ref, mom_ref, off_ref, sloc_ref, seen_ref, st_ref,
             s_ref):
    halves, voxels, _ = c_ref.shape
    narrow, wide = w_ref.shape
    local = float(voxels)
    mean, inverse = narrow_moments(st_in, narrow, local, total)
    mom_ref[0:1, :] = mean
    mom_ref[1:2, :] = inverse
    mom = mom_ref[...]

    def act(i, acc):
        s = jnp.maximum(second_act(get(c_ref, i, line), mom, tv_ref), 0.0)
        s_ref[pl.ds(i, line), :] = s
        return acc + total_rows(s)

    sums = chunk_loop(voxels, line, act, jnp.zeros((1, narrow), F32))
    center = sums / local
    sloc_ref[...] = jnp.broadcast_to(center, (8, narrow))
    put_rows(st_ref, 0, sums)
    chunk = part_of(voxels, line)

    def gram(i, acc):
        s = s_ref[pl.ds(i, chunk), :] - center
        return acc + dot6(s.T, s)

    seen = chunk_loop(voxels, chunk, gram, jnp.zeros((narrow, narrow), F32))
    seen = dot6(jnp.concatenate([seen, sloc_ref[...]], axis=0), w_ref[...])
    off_ref[...] = seen[narrow:]
    seen = seen[0:narrow]
    seen_ref[...] = seen
    put_rows(st_ref, halves, total_rows(seen * w_ref[...]))


def k_widen(f, steps, c_ref, mom_ref, tv_ref, sloc_ref, w_ref, e_ref, w_parts):
    @pl.when(f == 0)
    def _():
        keep_split(w_ref[...], w_parts)

    s = jnp.maximum(second_act(get(c_ref, 0, c_ref.shape[1]), mom_ref[...], tv_ref), 0.0)
    e_ref[...] = dot_split(s - sloc_ref[0:1, :], w_parts, 3)


def third_norm(st_in, w_ref, off_ref, vw_ref, momw_ref, smean_ref, local, total):
    narrow, wide = w_ref.shape
    s_means = take_rows(st_in, 0, narrow) / local
    squares = take_rows(st_in, narrow // 128, wide)
    e_means = dot6(s_means, w_ref[...])
    mean = jnp.mean(e_means, axis=0, keepdims=True)
    away = e_means - mean
    var = (total_rows(squares) + local * total_rows(away * away)) / total
    inverse = lax.rsqrt(var + EPSILON)
    scale = vw_ref[0:1, :] * inverse
    momw_ref[0:1, :] = scale
    momw_ref[1:2, :] = (off_ref[0:1, :] - mean) * scale + vw_ref[1:2, :]
    momw_ref[2:3, :] = inverse
    smean_ref[0:1, :] = jnp.mean(s_means, axis=0, keepdims=True)


def k_join(frames, total, local, f, steps, e_ref, x_ref, st_in, off_ref, w_ref, vw_ref, wr_ref, x_out,
           a_ref, face_f, face_l, momw_ref, smean_ref, st_ref, w_parts, acc_ref):

    @pl.when(f == 0)
    def _():
        third_norm(st_in, w_ref, off_ref, vw_ref, momw_ref, smean_ref, local, total)
        keep_split(wr_ref[...], w_parts)

    x = x_ref[...].reshape(x_out.shape)
    x = jnp.maximum(e_ref[...] * momw_ref[0:1, :] + momw_ref[1:2, :] + x, 0.0)
    x_out[...] = x
    a = dot_split(x, w_parts, 3)
    put_narrow(f, steps, a, a_ref, face_f, face_l, st_ref, acc_ref, frames)


def wide_step(gz, s, f, u_ref, p_ref, bias_acc, w_parts):
    put(u_ref, 0, dot_split(gz, w_parts, 2))
    p = dot3(split2(s.T), split2(gz))
    part = total_rows(gz)

    @pl.when(f == 0)
    def _():
        p_ref[...] = p
        bias_acc[0:1, :] = part

    @pl.when(f > 0)
    def _():
        p_ref[...] = p_ref[...] + p
        bias_acc[0:1, :] = bias_acc[0:1, :] + part


def centred_act(c_ref, mom_ref, tv_ref, smean_ref):
    c = get(c_ref, 0, c_ref.shape[1])
    return jnp.maximum(second_act(c, mom_ref[...], tv_ref), 0.0) - smean_ref[0:1, :]


def wide_finish(p_ref, w_ref, inverse, bias_acc, st_ref):
    wide = w_ref.shape[1]
    gain_sum = total_rows(p_ref[...] * w_ref[...]) * inverse
    put_rows(st_ref, 0, bias_acc[0:1, :])
    put_rows(st_ref, wide // 128, gain_sum)


def k_turn(total, local, f, steps, e_ref, x_ref, cot_ref, c_ref, st_in, off_ref, w_ref, vw_ref, mom_ref,
           tv_ref, out_ref, gz_ref, u_ref, p_ref, momw_ref, smean_ref, pool_ref, st_ref, w_parts,
           bias_acc):
    chunk, wide = x_ref.shape

    @pl.when(f == 0)
    def _():
        third_norm(st_in, w_ref, off_ref, vw_ref, momw_ref, smean_ref, local, total)
        keep_split((w_ref[...] * momw_ref[0:1, :]).T, w_parts)

    z = e_ref[...] * momw_ref[0:1, :] + momw_ref[1:2, :] + x_ref[...]
    out = jnp.maximum(z, 0.0)
    out_ref[...] = out.reshape(out_ref.shape)
    pooled = jnp.sum(out.reshape(chunk // 8, 8, wide), axis=0)

    @pl.when(f == 0)
    def _():
        pool_ref[...] = pooled

    @pl.when(f > 0)
    def _():
        pool_ref[...] = pool_ref[...] + pooled

    gz = jnp.where(z > 0.0, cot_ref[...].reshape(chunk, wide), 0.0)
    gz_ref[...] = gz
    s = centred_act(c_ref, mom_ref, tv_ref, smean_ref)
    wide_step(gz, s, f, u_ref, p_ref, bias_acc, w_parts)

    @pl.when(f == steps - 1)
    def _():
        wide_finish(p_ref, w_ref, momw_ref[2:3, :], bias_acc, st_ref)


def k_second(total, f, steps, u_ref, c_ref, st_in, w_ref, momw_ref, smean_ref, mom_ref, tv_ref, *refs):
    *more, n_ref, gw_ref, st_ref, q_parts, acc_ref = refs
    halves, chunk, _ = u_ref.shape
    narrow, wide = w_ref.shape

    @pl.when(f == 0)
    def _():
        bias_sum = take_sum(st_in, 0, wide)
        gain_sum = take_sum(st_in, wide // 128, wide)
        gw_ref[0:1, :] = gain_sum
        gw_ref[1:2, :] = bias_sum
        alpha = momw_ref[0:1, :]
        w = w_ref[...]
        wt = split2(w.T)
        q = dot3(split2(w * (alpha * momw_ref[2:3, :] * (gain_sum / total))), wt)
        keep_split(q, q_parts)
        acc_ref[0:2, :] = jnp.zeros((2, narrow), F32)
        d = dot3(split2(jnp.broadcast_to(alpha * (bias_sum / total), (8, wide))), wt)
        acc_ref[2:3, :] = d[0:1, :]

    mom = mom_ref[...]
    c = get(c_ref, 0, chunk)
    y = second_act(c, mom, tv_ref)
    corr = dot_split(jnp.maximum(y, 0.0) - smean_ref[0:1, :], q_parts, 2)
    n = jnp.where(y > 0.0, get(u_ref, 0, chunk) - corr - acc_ref[2:3, :], 0.0)
    put(n_ref, 0, n)
    xhat = (c - mom[0:1, :]) * mom[1:2, :]
    acc_ref[0:1, :] = acc_ref[0:1, :] + total_rows(n)
    acc_ref[1:2, :] = acc_ref[1:2, :] + total_rows(n * xhat)

    @pl.when(f == steps - 1)
    def _():
        put_rows(st_ref, 0, acc_ref[0:1, :])
        put_rows(st_ref, halves, acc_ref[1:2, :])
        if more:
            st_ref[:, 2 * halves :, :] = more[0][...]


def expand_grad(local, total, p_ref, w_ref, gw_ref, momw_ref, smean_ref, sloc_ref, seen_ref):
    apart = sloc_ref[...] - smean_ref[0:1, :]
    column = apart.T[:, 0:1] * local
    alpha = momw_ref[0:1, :]
    gamma = gw_ref[0:1, :] / total * momw_ref[2:3, :]
    beta = gw_ref[1:2, :] / total
    seen = seen_ref[...] + column * dot6(apart, w_ref[...])[0:1, :]
    return alpha * (p_ref[...] - column * beta - seen * gamma)


def norm_sums(f, st_in, out_ref):
    @pl.when(f == 0)
    def _():
        narrow = out_ref.shape[1]
        out_ref[0:1, :] = take_sum(st_in, narrow // 128, narrow)
        out_ref[1:2, :] = take_sum(st_in, 0, narrow)


def norm_back(n, a, gain, mom_ref, sums_ref, total):
    mom = mom_ref[...]
    xhat = (a - mom[0:1, :]) * mom[1:2, :]
    return gain * mom[1:2, :] * (n - sums_ref[1:2, :] / total - xhat * (sums_ref[0:1, :] / total))


def k_center(frames, total, f, steps, n_ref, c_ref, st_in, tv_ref, mom2_ref, gc_ref, face_f, face_l,
             gd_ref, *more):
    norm_sums(f, st_in, gd_ref)
    if more:
        more[0][...] = jnp.sum(st_in[:, 2 * gc_ref.shape[0] :, :], axis=0)
    chunk = n_ref.shape[1]
    n, c = get(n_ref, 0, chunk), get(c_ref, 0, chunk)
    put(gc_ref, 0, norm_back(n, c, tv_ref[29:30, :], mom2_ref, gd_ref, total))
    put_faces(gc_ref, face_f, face_l, frames)


def put_halves(piece, at, lower, mine, theirs):
    narrow = piece.shape[1]
    pairs = mine.shape[0]
    share = narrow // (2 * pairs)
    piece = piece.reshape(pairs, 2, share, narrow)
    mine[:, at : at + share, :] = jnp.where(lower, piece[:, 1], piece[:, 0])
    theirs[:, at : at + share, :] = jnp.where(lower, piece[:, 0], piece[:, 1])


def k_first_back(line, frames, more, keep_ref, gc_ref, hp_ref, hn_ref, *refs, flush, ready):
    *refs, gm_ref, gcp_ref, before, after, wt_ref, acc_ref = refs
    dm_refs = refs[-1:] if refs[-1].shape == acc_ref.shape else refs[-2:]
    *refs, n1_ref, st_ref = refs[: -len(dm_refs)]
    *refs, rest_ref = refs if more else (*refs, None)
    *refs, a_ref, w_ref, tv_ref, mom1_ref = refs
    rows, corners = refs[: len(refs) // 2], refs[len(refs) // 2 :]
    (up_ref, dn_ref), (cu_ref, cd_ref) = both(rows), both(corners)
    halves, voxels, _ = gc_ref.shape
    narrow = halves * 128
    top = keep_ref[3 * frames]
    bottom = keep_ref[3 * frames + 1]

    def own(i, carry):
        put(gcp_ref, pl.multiple_of(line + i, 8), get(gc_ref, i, line))
        return carry

    chunk_loop(voxels, line, own, 0)
    put(gcp_ref, 0, get(up_ref, 0, line) * top)
    put(gcp_ref, line + voxels, get(dn_ref, 0, line) * bottom)
    make_taps(tv_ref, keep_ref, wt_ref, frames, True)
    halos = [
        halo_pieces(i, face, cu_ref, cd_ref, top, bottom, lambda v: v)
        for i, face in enumerate((hp_ref, hn_ref))
    ]
    shift_frames(gcp_ref, before, after, line, frames)
    put_frames(before, 0, frames, halos[0])
    put_frames(after, frames - 1, frames, halos[1])
    stencil_into((before, gcp_ref, after), wt_ref, gm_ref, line)
    ready()
    wt = split2(w_ref[...].T)
    mom1 = mom1_ref[...]
    scale1 = tv_ref[27:28, :] * mom1[1:2, :]
    chunk = part_of(voxels, line)

    acc_ref[...] = jnp.zeros(acc_ref.shape, F32)

    def step(i, accs):
        gm = split2(get(gm_ref, i, chunk))
        gr = dot3(gm, wt)
        off = get(a_ref, i, chunk) - mom1[0:1, :]
        y = off * scale1 + tv_ref[28:29, :]
        n = jnp.where(y > 0.0, gr, 0.0)
        put(n1_ref, i, n)
        acc_ref[...] = acc_ref[...] + dot3(split2(jnp.maximum(y, 0.0).T), gm)
        return accs[0] + total_rows(n), accs[1] + total_rows(n * (off * mom1[1:2, :]))

    zero = jnp.zeros((1, narrow), F32)
    bias_acc, gain_acc = chunk_loop(voxels, chunk, step, (zero, zero))
    flush(0)
    put_rows(st_ref, 0, bias_acc)
    put_rows(st_ref, halves, gain_acc)
    if more:
        rest = rest_ref[...][None]
        st_ref[:, 2 * halves :, :] = jnp.broadcast_to(rest, (st_ref.shape[0],) + rest.shape[1:])
    if len(dm_refs) == 1:
        dm_refs[0][...] = acc_ref[...]
    else:
        put_halves(acc_ref[...], 0, top > 0.0, *dm_refs)


def k_side_grads(line, frames, total, keep_ref, gc_ref, mp_ref, before, after, placed, p_ref, w_ref, gw_ref,
                 momw_ref, smean_ref, sloc_ref, seen_ref, *refs):
    *out_refs, dk_ref = refs
    de = expand_grad(float(gc_ref.shape[1]), total, p_ref, w_ref, gw_ref, momw_ref, smean_ref, sloc_ref,
                     seen_ref)
    frame = frame_of(line, frames)

    def merge(i, carry):
        for h in range(gc_ref.shape[0]):
            where = pl.ds(i, line)
            halo_part = placed[h, where, :].reshape(line // 8, 8, 128)
            for target, place in ((before, 0), (after, frames - 1)):
                own = target[h, where, :].reshape(line // 8, 8, 128)
                own = jnp.where(frame == place, halo_part, own)
                target[h, where, :] = own.reshape(line, 128)
        return carry

    chunk_loop(placed.shape[1], line, merge, 0)
    halves, voxels, _ = gc_ref.shape
    narrow = halves * 128
    parts = 2 if (line // 8) % 2 == 0 else 1
    n = line // 8 // parts
    for h in range(halves):
        for o, field in enumerate((before, mp_ref, after)):

            def row(r, accs):
                accs = list(accs)
                for part in range(parts):
                    where = pl.multiple_of(r * line, line) + part * n * 8
                    g = gc_ref[h, pl.ds(pl.multiple_of(where, 8), n * 8), :].reshape(n, 8, 128)
                    for p in range(3):
                        start = pl.multiple_of((r + p) * line, line)
                        views = line_views(field, h, start, line, part, parts)
                        for q in range(3):
                            accs[3 * p + q] = accs[3 * p + q] + jnp.sum(g * views[q], axis=0)
                return tuple(accs)

            accs = lax.fori_loop(0, voxels // line, row, (jnp.zeros((8, 128), F32),) * 9)
            keep = by_frame(keep_ref, o, frames)
            for i in range(9):
                tap = 9 * o + i
                dk_ref[tap : tap + 1, h * 128 : h * 128 + 128] = total_rows(accs[i] * keep)
    dk_ref[27:128, :] = jnp.zeros((101, narrow), F32)
    whole = out_refs[0].shape == w_ref.shape
    if whole:
        out_refs[0][...] = de
        out_refs[1][...] = dk_ref[...]
    else:
        lower = keep_ref[3 * frames] > 0.0
        share = narrow // (2 * out_refs[0].shape[0])
        groups = de.shape[1] // narrow
        for g in range(groups):
            put_halves(de[:, g * narrow : (g + 1) * narrow], g * share, lower, *out_refs)
        turned = jnp.concatenate([dk_ref[...].T, jnp.zeros((narrow, narrow - 128), F32)], axis=1)
        put_halves(turned, groups * share, lower, *out_refs)


def k_add_grads(mine, theirs, mine_late, theirs_late, out):
    rows = mine.shape[1]
    out[:, 0:rows, :] = mine[...] + theirs[...]
    out[:, rows:, :] = mine_late[...] + theirs_late[...]


def k_update(*refs):
    me_ref, zero, one, reduce_zero, reduce_one = refs[:5]
    vecs = refs[5:11]
    params, momenta = refs[11:21], refs[21:31]
    grads, velocity, updated = refs[31:41], refs[41:51], refs[51:61]
    me = me_ref[0]
    share = params[1].shape[1]
    narrow = params[1].shape[2]
    groups = params[3].shape[2] // narrow

    def apply(i, b, grad, where=slice(None)):
        v = MOMENTUM * momenta[i][b, :, where] + grad
        grads[i][b, :, where] = grad
        velocity[i][b, :, where] = v
        updated[i][b, :, where] = params[i][b, :, where] - LEARN_RATE * (grad + MOMENTUM * v)

    packs = (jnp.sum(zero[...], axis=0), jnp.sum(one[...], axis=0))
    for b, (pack, reduce) in enumerate(zip(packs, (reduce_zero, reduce_one))):
        for g in range(groups):
            apply(3, b, pack[g * share : (g + 1) * share], slice(g * narrow, (g + 1) * narrow))
        at = groups * share
        apply(2, b, pack[at : at + share, 0:27])
        at += share
        apply(1, b, pack[at : at + share])
        apply(0, b, jnp.sum(reduce[...], axis=0))
    for j in range(3):
        for r in range(2):
            i = 4 + 2 * j + r
            pieces = []
            for b in range(2):
                value = vecs[2 * j + b][...]
                width = params[i].shape[1]
                length = value.shape[1]
                turned = pltpu.roll(value, length - me * width, 1)
                pieces.append(turned[r : r + 1, 0:width])
            grad = jnp.concatenate(pieces, axis=0)
            v = MOMENTUM * momenta[i][...] + grad
            grads[i][...] = grad
            velocity[i][...] = v
            updated[i][...] = params[i][...] - LEARN_RATE * (grad + MOMENTUM * v)


def put_by_core(dw, me_ref, out_refs):
    if len(out_refs) == 1:
        out_refs[0][...] = dw
    else:
        mine, theirs = out_refs
        dw = dw.reshape(mine.shape[0], 2, *mine.shape[1:])
        lower = me_ref[0] % 2 == 1
        mine[...] = jnp.where(lower, dw[:, 1], dw[:, 0])
        theirs[...] = jnp.where(lower, dw[:, 0], dw[:, 1])


def reduce_grad(ga, x, f, dwt):
    dw = dot3(split2(ga.T), split2(x))

    @pl.when(f == 0)
    def _():
        dwt[...] = dw

    @pl.when(f > 0)
    def _():
        dwt[...] = dwt[...] + dw


def k_between(total, f, steps, me_ref, n1_ref, a_ref, c_ref, x_ref, gz_in, st_in, tv_ref, mom1_ref,
              wr_ref, mom2_ref, tv2_ref, w_ref, momw_ref, smean_ref, gz_ref, u_ref, p_ref, gn_ref,
              st_ref, *refs):
    *dw_refs, wr_parts, w_parts, dwt, bias_acc = refs
    chunk, wide = x_ref.shape
    norm_sums(f, st_in, gn_ref)

    @pl.when(f == 0)
    def _():
        keep_split(wr_ref[...].T, wr_parts)
        keep_split((w_ref[...] * momw_ref[0:1, :]).T, w_parts)

    x = x_ref[...]
    n, a = get(n1_ref, 0, chunk), get(a_ref, 0, chunk)
    ga = norm_back(n, a, tv_ref[27:28, :], mom1_ref, gn_ref, total)
    gy = dot_split(ga, wr_parts, 2) + gz_in[...]
    gz = jnp.where(x > 0.0, gy, 0.0)
    gz_ref[...] = gz
    reduce_grad(ga, x, f, dwt)
    s = centred_act(c_ref, mom2_ref, tv2_ref, smean_ref)
    wide_step(gz, s, f, u_ref, p_ref, bias_acc, w_parts)

    @pl.when(f == steps - 1)
    def _():
        wide_finish(p_ref, w_ref, momw_ref[2:3, :], bias_acc, st_ref)
        put_by_core(dwt[...].T, me_ref, dw_refs)


def k_last_weight(total, f, steps, me_ref, n1_ref, a_ref, x_ref, st_in, tv_ref, mom1_ref, ga_ref,
                  gn_ref, *refs):
    *dw_refs, dwt = refs
    chunk = n1_ref.shape[1]
    norm_sums(f, st_in, gn_ref)
    n, a = get(n1_ref, 0, chunk), get(a_ref, 0, chunk)
    ga = norm_back(n, a, tv_ref[27:28, :], mom1_ref, gn_ref, total)
    put(ga_ref, 0, ga)
    reduce_grad(ga, x_ref[...].reshape(chunk, -1), f, dwt)

    @pl.when(f == steps - 1)
    def _():
        put_by_core(dwt[...].T, me_ref, dw_refs)


def k_last(f, steps, ga_ref, gz_in, wr_ref, gx_ref, wr_parts):
    @pl.when(f == 0)
    def _():
        keep_split(wr_ref[...].T, wr_parts)

    gy = dot_split(get(ga_ref, 0, ga_ref.shape[1]), wr_parts, 2) + gz_in[...]
    gx_ref[...] = gy.reshape(gx_ref.shape)


def exchange(rows):
    return lax.all_to_all(rows, AX, 0, 0)


def meet(value, bits, devices):
    parts = [value]
    for step in range(1, 1 << len(bits)):
        mask = step << bits[0]
        parts.append(lax.ppermute(value, AX, [(i, i ^ mask) for i in range(devices)]))
    return parts


def perm(step, shape):
    dp, fs = shape
    pairs = []
    for i in range(dp):
        for j in range(fs):
            a, b = i + step[0], j + step[1]
            if 0 <= a < dp and 0 <= b < fs:
                pairs.append((i * fs + j, a * fs + b))
    return pairs


def row_halo(field, line, shape):
    low, high = field[:, :line], field[:, field.shape[1] - line :]
    if shape[1] == 2:
        return [swap_cores(jnp.where(lax.axis_index("fsdp") == 0, high, low), shape)]
    move = lambda value, step: lax.ppermute(value, AX, perm(step, shape))
    return [move(high, (0, 1)), move(low, (0, -1))]


def frame_halo(first, last, width, shape, beside):
    count = first.shape[1]
    move = lambda value, step: lax.ppermute(value, AX, perm(step, shape))
    before, after = move(last, (1, 0)), move(first, (-1, 0))
    tops = jnp.stack([before[:, :width], after[:, :width]])
    ends = jnp.stack([before[:, count - width :], after[:, count - width :]])
    tops, ends, *beside = lax.optimization_barrier((tops, ends, *beside))
    if shape[1] == 2:
        corners = [swap_cores(jnp.where(lax.axis_index("fsdp") == 0, ends, tops), shape)]
    else:
        corners = [move(ends, (0, 1)), move(tops, (0, -1))]
    return [before, after, *corners], *beside


def tree_gather(part, devices, name):
    for bits in STAGES[:-1]:
        parts = meet(part, bits, devices)
        dims = (part.shape[0] * len(parts),) + part.shape[1:]
        part = call(k_stack, name, [(dims, HB)], [(piece, VM) for piece in parts], limit=4)[0]
    return meet(part, STAGES[-1], devices)


def core_sums(mine, theirs, shape):
    pairs = [(i, i ^ 1) for i in range(shape[0] * 2)]
    theirs = lax.ppermute(theirs, AX, pairs)
    return call(k_add, "core_add", [(mine.shape, HB)], [(mine, HB), (theirs, VM)], limit=8)[0]


def swap_cores(value, shape):
    return lax.ppermute(value, AX, [(i, i ^ 1) for i in range(shape[0] * 2)])


def k_add(left, right, out):
    out[...] = left[...] + right[...]


def owner_parts(parts, shape):
    return lax.all_to_all(parts, "dp", 0, 0)


HB = pl.BlockSpec(memory_space=pl.ANY)
FILLER = 1 << 31
HIDER = 1 << 32
MINOR = 1 << 27


def pieces(far, near):
    rows = near.shape[0]
    size = 4
    for dim in near.shape:
        size *= dim
    if size < MIB // 2:
        return [(far, near)]
    if len(near.shape) == 3 and rows <= 4:
        return [(far.at[i], near.at[i]) for i in range(rows)]
    if rows % 16 == 0:
        half = rows // 2
        return [(far.at[pl.ds(i * half, half)], near.at[pl.ds(i * half, half)]) for i in range(2)]
    return [(far, near)]


class Stream:
    def __init__(self, axis):
        self.axis = axis

    def part(self, ref, i, steps):
        size = ref.shape[self.axis] // steps
        where = pl.ds(i * size if isinstance(i, int) else pl.multiple_of(i * size, size), size)
        return ref.at[(slice(None),) * self.axis + (where,)]


WIDE, NARROW = Stream(0), Stream(1)
AHEAD = 2


def call(kernel, name, outs, ins, scratch=(), limit=24, steps=None, lazy=None, cost=1000):
    n_i, n_o, n_s = len(ins), len(outs), len(scratch)
    count = steps or 1
    near_i = [i for i in range(n_i) if ins[i][1] not in (SM, VM)]
    whole_i = [i for i in near_i if ins[i][1] is HB]
    flow_i = [i for i in near_i if ins[i][1] is not HB]
    whole_o = [i for i in range(n_o) if outs[i][1] is HB]
    flow_o = [i for i in range(n_o) if outs[i][1] is not HB]

    def run(*refs):
        far_in, far_out = refs[:n_i], refs[n_i : n_i + n_o]
        own = refs[n_i + n_o : n_i + n_o + n_s]
        near = refs[n_i + n_o + n_s : -2]
        sem, flow_sem = refs[-2:]
        in_refs, out_refs = list(far_in), list(near[len(near_i) :])
        for i, ref in zip(near_i, near):
            in_refs[i] = ref
        used = 0
        loads, late, stores = [], [], {}
        for i in whole_i:
            for src, dst in pieces(far_in[i], in_refs[i]):
                copy = pltpu.make_async_copy(src, dst, sem.at[used])
                (late if lazy and i in lazy else loads).append(copy)
                used += 1
        for i in whole_o:
            stores[i] = []
            for dst, src in pieces(far_out[i], out_refs[i]):
                stores[i].append(pltpu.make_async_copy(src, dst, sem.at[used]))
                used += 1
        started = set()

        def flush(i, part=None):
            for k, copy in enumerate(stores[i]):
                if part is None or k == part:
                    started.add((i, k))
                    copy.start()

        def ready():
            for copy in late:
                copy.wait()

        def flow_in(i):
            return [
                pltpu.make_async_copy(
                    ins[j][1].part(far_in[j], i, count),
                    ins[j][1].part(in_refs[j], i, count),
                    flow_sem.at[k, i],
                )
                for k, j in enumerate(flow_i)
            ]

        def flow_out(i):
            return [
                pltpu.make_async_copy(
                    outs[j][1].part(out_refs[j], i, count),
                    outs[j][1].part(far_out[j], i, count),
                    flow_sem.at[len(flow_i) + k, i],
                )
                for k, j in enumerate(flow_o)
            ]

        for copy in loads + late:
            copy.start()
        heavy = any(ins[j][1] is WIDE for j in flow_i)
        ahead = min(AHEAD, count) if heavy else count
        for i in range(ahead):
            for copy in flow_in(i):
                copy.start()
        for copy in loads:
            copy.wait()
        if steps is None:
            kernel(*in_refs, *out_refs, *own, **({} if lazy is None else {"flush": flush, "ready": ready}))
        else:

            def step(i, carry):
                for copy in flow_in(i):
                    copy.wait()
                if count > ahead:

                    @pl.when(i + ahead < count)
                    def _():
                        for copy in flow_in(i + ahead):
                            copy.start()

                views = list(in_refs) + list(out_refs)
                for j in flow_i:
                    views[j] = ins[j][1].part(in_refs[j], i, count)
                for j in flow_o:
                    views[n_i + j] = outs[j][1].part(out_refs[j], i, count)
                kernel(i, count, *views, *own)
                for copy in flow_out(i):
                    copy.start()
                return carry

            lax.fori_loop(0, count, step, 0)
        for i in whole_o:
            for k, copy in enumerate(stores[i]):
                if (i, k) not in started:
                    copy.start()
        for i in range(count):
            for copy in flow_out(i):
                copy.wait()
        for i in whole_o:
            for copy in stores[i]:
                copy.wait()

    values = [
        value if spec in (SM, VM) else pltpu.with_memory_space_constraint(value, pltpu.HBM)
        for value, spec in ins
    ]
    whole = 2 * (len(whole_i) + len(whole_o))
    flows = len(flow_i) + len(flow_o)
    return pl.pallas_call(
        run,
        in_specs=[spec if spec in (SM, VM) else HB for _, spec in ins],
        out_specs=(HB,) * n_o,
        out_shape=tuple(pltpu.HBM(shape, F32) for shape, _ in outs),
        scratch_shapes=[pltpu.VMEM(shape, dtype) for shape, dtype in scratch]
        + [pltpu.VMEM(ins[i][0].shape, F32) for i in near_i]
        + [pltpu.VMEM(shape, F32) for shape, _ in outs]
        + [pltpu.SemaphoreType.DMA((max(whole, 1),)), pltpu.SemaphoreType.DMA((max(flows, 1), count))],
        compiler_params=params(limit),
        cost_estimate=pl.CostEstimate(flops=cost, bytes_accessed=1000, transcendentals=0),
        name=name,
    )(*values)


def body(inputs, cotangent, clip_index, *args):
    weights, momenta = args[:10], args[10:]
    frames, rows, width, wide = inputs.shape
    narrow = weights[0].shape[2]
    halves = narrow // 128
    shape = (lax.axis_size("dp"), lax.axis_size("fsdp"))
    devices = shape[0] * shape[1]
    rank = lax.axis_index(AX)
    voxels = frames * rows * width
    line = width * frames
    total = float(voxels * devices)
    many = 7 if voxels % (7 * 8 * frames) == 0 else 1
    x0 = inputs.transpose(1, 2, 0, 3)
    cot = cotangent.transpose(1, 2, 0, 3)

    edge = jnp.full((1,), -1, jnp.int32)
    window = lax.dynamic_slice_in_dim(
        jnp.concatenate([edge, clip_index, edge]), lax.axis_index("dp") * frames, frames + 2
    )
    centre = window[1:-1]
    flags = jnp.concatenate(
        [
            (window[:-2] == centre).astype(F32),
            jnp.ones((frames,), F32),
            (window[2:] == centre).astype(F32),
            (lax.axis_index("fsdp") > 0).astype(F32)[None],
            (lax.axis_index("fsdp") < shape[1] - 1).astype(F32)[None],
        ]
    )
    me = rank.astype(jnp.int32)[None]

    field_n = (halves, voxels, 128)
    grown_n = (halves, voxels + 2 * line, 128)
    face_n = (halves, voxels // frames, 128)
    field_w = (voxels, wide)
    stat_n = (devices, 2 * halves, 128)
    stat_e = (devices, (narrow + wide) // 128, 128)
    stat_w = (devices, 2 * wide // 128, 128)
    mom_n, mom_w = (8, narrow), (8, wide)
    down_r, down_m, down_e = (wide, narrow), (narrow, narrow), (narrow, wide)
    parts = lambda *values: [(value, NARROW) for value in values]

    near = lambda *values: [(value, HB) for value in values]
    here = lambda *values: [(value, VM) for value in values]
    fix = near
    owned = devices == 32
    half = (devices // 2, wide // devices, narrow)
    down_halves = (half, half) if owned else (down_r,)
    share = narrow // devices
    side = (devices // 2, share * (wide // narrow + 1), narrow)
    side_halves = (side, side) if owned else (down_e, (128, narrow))
    mixed_halves = ((devices // 2, share, narrow),) * 2 if owned else (down_m,)

    def first(wr0):
        return call(
            functools.partial(k_first, frames),
            "first",
            [(field_n, NARROW), (face_n, NARROW), (face_n, NARROW)] + near(stat_n, down_r),
            [(me, SM), (x0, WIDE)] + (here if owned else near)(*wr0),
            scratch=[((3 * wide, narrow), BF16), (mom_n, F32)],
            limit=48,
            steps=many,
        )

    if owned:
        share_n, share_w = weights[1].shape[1], weights[0].shape[1]
        early, late = call(
            k_pack,
            "pack",
            near(
                (1, share_w + 2 * share_n, narrow),
                (share_w + share_n * (1 + 2 * (wide // narrow)), narrow),
            ),
            near(*weights),
            limit=4,
        )
        wr0 = slots = tree_gather(early, devices, "stack")
        late = lax.all_gather(late, AX, axis=0, tiled=False)
        a0, *faces, st, wr0 = first(wr0)
        wm0, tv, vw = call(
            k_open_early,
            "open_early",
            near(down_m, (2, 32, narrow), (2, 8, wide)),
            [(me, SM)] + near(*slots),
            scratch=[((narrow, 128), F32)],
            limit=8,
            cost=FILLER,
        )
        wr1, wm1, we0, we1 = call(
            k_open_later,
            "open_later",
            near(down_r, down_m, down_e, down_e),
            near(late),
            limit=16,
            cost=FILLER,
        )
    else:
        gather = lambda part: lax.all_gather(part, AX, axis=0, tiled=True)
        wr0, wr1 = [gather(weights[0][0])], gather(weights[0][1])
        wm0, wm1 = gather(weights[1][0]), gather(weights[1][1])
        we0, we1 = gather(weights[3][0]), gather(weights[3][1])
        small = jnp.concatenate([weights[2]] + [weights[i][..., None] for i in (4, 5, 6, 7)], axis=2)
        small = gather(small.transpose(1, 0, 2))
        tv = jnp.pad(small.transpose(1, 2, 0), ((0, 0), (0, 1), (0, 0)))
        large = gather(jnp.stack([weights[8], weights[9]], axis=2).transpose(1, 0, 2))
        vw = jnp.pad(large.transpose(1, 2, 0), ((0, 0), (0, 6), (0, 0)))

    def mix_own(block, a, rows, st, wm):
        return call(
            functools.partial(k_mix_own, line, frames, total),
            "mix_own",
            near(field_n, grown_n, grown_n, grown_n, mom_n),
            [(flags, SM)] + near(a) + here(*rows, st) + near(wm, tv[block]),
            scratch=[((halves, 27, 8, 128), F32)],
            limit=20,
            lazy=(),
            cost=MINOR,
        )

    def mix_halo(block, part, halos, mom, wm):
        return call(
            functools.partial(k_mix, line, frames),
            "mix",
            near(field_n, grown_n, stat_n),
            [(flags, SM)]
            + near(part, *halos[:2])
            + here(*halos[2:])
            + near(mom, wm, tv[block]),
            scratch=[((halves, 9, 8, 128), F32)],
            limit=20,
            lazy=(1,),
        )

    def mix(block, a, faces, st, wm):
        own = mix_own(block, a, row_halo(a, line, shape), st, wm)
        halos, part, *grown, mom = frame_halo(*faces, width, shape, own)
        c, placed, st = mix_halo(block, part, halos, mom, wm)
        return c, grown + [placed], mom, st

    def expand(block, c, st, we):
        return call(
            functools.partial(k_expand, line, total),
            "expand",
            near(mom_n, mom_w, mom_n, down_e, stat_e),
            near(c) + here(st) + near(we, tv[block]),
            scratch=[((voxels, narrow), F32)],
            limit=20,
        )

    def widen(block, c, mom2, sloc, we):
        return call(
            k_widen,
            "widen",
            [(field_w, WIDE)],
            [(c, NARROW)] + near(mom2, tv[block], sloc, we),
            scratch=[((3 * narrow, wide), BF16)],
            limit=48,
            steps=many,
            cost=FILLER,
        )[0]

    def join(e, x, st, off, we, wr):
        return call(
            functools.partial(k_join, frames, total, float(voxels)),
            "join",
            [(field_w, WIDE), (field_n, NARROW), (face_n, NARROW), (face_n, NARROW)]
            + near(mom_w, mom_n, stat_n),
            [(e, WIDE), (x, WIDE)] + here(st) + near(off, we, vw[0], wr),
            scratch=[((3 * wide, narrow), BF16), (mom_n, F32)],
            limit=56,
            steps=many,
        )

    def turn(e, x, c, st, off, we, mom2):
        return call(
            functools.partial(k_turn, total, float(voxels)),
            "turn",
            [((rows, width, frames, wide), WIDE), (field_w, WIDE), (field_n, NARROW)]
            + near(down_e, mom_w, mom_n, mom_w, stat_w),
            [(e, WIDE), (x, WIDE), (cot, WIDE), (c, NARROW)]
            + here(st)
            + near(off, we, vw[1], mom2, tv[1]),
            scratch=[((2 * wide, narrow), BF16), (mom_w, F32)],
            limit=58,
            steps=many,
        )

    def stat_with(more):
        return (devices, 2 * halves + sum(value.shape[-2] for value in more), 128)

    def second(block, u, c, st, we, momw, smean, mom2, *more):
        return call(
            functools.partial(k_second, total),
            "second",
            parts(field_n) + near(mom_w, stat_with(more)),
            parts(u, c) + here(st) + near(we, momw, smean, mom2, tv[block], *more),
            scratch=[((2 * narrow, narrow), BF16), (mom_n, F32)],
            limit=24,
            steps=many,
        )

    def center(block, n, c, st, mom2):
        return call(
            functools.partial(k_center, frames, total),
            "center",
            [(field_n, NARROW), (face_n, NARROW), (face_n, NARROW)]
            + near(mom_n, *([(st.shape[1] - 2 * halves, 128)] if st.shape[1] > 2 * halves else [])),
            parts(n, c) + here(st) + near(tv[block], mom2),
            limit=24,
            steps=many,
        )

    def first_back(block, gc, halos, a, wm, mom1, *more):
        return call(
            functools.partial(k_first_back, line, frames, len(more)),
            "first_back",
            near(field_n, stat_with(more), *mixed_halves),
            [(flags, SM)]
            + near(gc, *halos[:2])
            + here(*halos[2:])
            + near(a, wm, tv[block], mom1, *more),
            scratch=[(field_n, F32)] + [(grown_n, F32)] * 3
            + [((halves, 27, 8, 128), F32), (down_m, F32)],
            limit=20,
            lazy=(2 + len(halos), 3 + len(halos), 5 + len(halos)),
        )

    def side_grads(gc, grown, p, we, gw, momw, smean, sloc, seen):
        return call(
            functools.partial(k_side_grads, line, frames, total),
            "side_grads",
            near(*side_halves),
            [(flags, SM)] + near(gc, *grown, p, we, gw, momw, smean, sloc, seen),
            scratch=[((128, narrow), F32)],
            limit=24,
            cost=HIDER,
        )

    def add_grads(mine, theirs, mine_late, theirs_late):
        dims = (mine.shape[0], mine.shape[1] + mine_late.shape[1], narrow)
        return call(
            k_add_grads,
            "add_grads",
            near(dims),
            near(mine) + here(theirs) + near(mine_late) + here(theirs_late),
            limit=12,
        )[0]

    def between(n1, a, st, mom1, wr, x, gz, c, mom2, we, momw, smean):
        return call(
            functools.partial(k_between, total),
            "between",
            [(field_w, WIDE), (field_n, NARROW)] + near(down_e, mom_n, stat_w, *down_halves),
            [(me, SM)]
            + parts(n1, a, c)
            + [(x, WIDE), (gz, WIDE)]
            + here(st)
            + near(tv[1], mom1, wr, mom2, tv[0], we, momw, smean),
            scratch=[((2 * narrow, wide), BF16), ((2 * wide, narrow), BF16), (down_e, F32),
                     (mom_w, F32)],
            limit=58,
            steps=many,
        )

    def last_weight(n1, a, st, mom1):
        return call(
            functools.partial(k_last_weight, total),
            "last_weight",
            [(field_n, NARROW)] + near(mom_n, *down_halves),
            [(me, SM)] + parts(n1, a) + [(x0, WIDE)] + here(st) + near(tv[0], mom1),
            scratch=[(down_e, F32)],
            limit=48,
            steps=many,
        )

    def last(ga, gz, wr):
        return call(
            k_last,
            "last",
            [((rows, width, frames, wide), WIDE)],
            [(ga, NARROW), (gz, WIDE)] + near(wr),
            scratch=[((2 * narrow, wide), BF16)],
            limit=48,
            steps=many,
            cost=FILLER,
        )[0]


    if not owned:
        a0, *faces, st, wr0 = first(wr0)
    c0, grown0, mom10, st = mix(0, a0, faces, exchange(st), wm0)
    mom20, off0, sloc0, seen0, st = expand(0, c0, exchange(st), we0)
    e0 = widen(0, c0, mom20, sloc0, we0)
    x1, a1, *faces, momw0, smean0, st = join(e0, x0, exchange(st), off0, we0, wr1)
    c1, grown1, mom11, st = mix(1, a1, faces, exchange(st), wm1)
    mom21, off1, sloc1, seen1, st = expand(1, c1, exchange(st), we1)
    e1 = widen(1, c1, mom21, sloc1, we1)
    out, gz1, u1, p1, momw1, smean1, pool, st = turn(
        e1, x1, c1, exchange(st), off1, we1, mom21
    )

    clips = clip_index.shape[0] // 6
    labels = jnp.arange(clips, dtype=jnp.int32)
    hot = (centre[None, :] == labels[:, None]).astype(F32)
    pooled = jnp.dot(
        jnp.concatenate([hot] * (8 // frames), axis=1), pool, precision=HIGHEST,
        preferred_element_type=F32,
    )
    if owned:
        room = -(-clips * share_w // 128) * 128
        pooled = pooled.reshape(clips, devices, share_w).transpose(1, 0, 2).reshape(devices, -1)
        pooled = jnp.pad(pooled, ((0, 0), (0, room - clips * share_w)))
        more = (pooled.reshape(devices, room // 128, 128),)
    else:
        more = ()
        pooled = lax.psum(pooled, AX)
    counts = jnp.sum((clip_index[None, :] == labels[:, None]).astype(F32), axis=1)

    n, gw1, st = second(1, u1, c1, exchange(st), we1, momw1, smean1, mom21, *more)
    gc, face_f, face_l, gd1, *more = center(1, n, c1, exchange(st), mom21)
    faces = (face_f, face_l)
    side1 = side_grads(gc, grown1, p1, we1, gw1, momw1, smean1, sloc1, seen1)
    halos, *side1 = frame_halo(*faces, width, shape, side1)
    halos = halos[:2] + row_halo(gc, line, shape) + halos[2:]
    n1, st, *dm1 = first_back(1, gc, halos, a1, wm1, mom11, *more)
    st = exchange(st)
    if owned:
        one = add_grads(
            side1[0], swap_cores(side1[1], shape), dm1[0], swap_cores(dm1[1], shape)
        )
        one, st = lax.optimization_barrier((one, st))
        one = owner_parts(one, shape)
        pooled = st[:, 2 * halves :, :].reshape(devices, -1)[:, : clips * share_w]
        pooled = pooled.reshape(devices, clips, share_w).transpose(1, 0, 2).reshape(clips, wide)
    gz0, u0, p0, gn1, st, *dr1 = between(
        n1, a1, st, mom11, wr1, x1, gz1, c0, mom20, we0, momw0, smean0
    )
    if owned:
        st, one = lax.optimization_barrier((st, one))
    st = exchange(st)
    if owned:
        dr1 = core_sums(*dr1, shape)
        dr1, st = lax.optimization_barrier((dr1, st))
        dr1 = owner_parts(dr1, shape)
    n, gw0, st = second(0, u0, c0, st, we0, momw0, smean0, mom20)
    gc, *faces, gd0 = center(0, n, c0, exchange(st), mom20)
    side0 = side_grads(gc, grown0, p0, we0, gw0, momw0, smean0, sloc0, seen0)
    halos, *side0 = frame_halo(*faces, width, shape, side0)
    halos = halos[:2] + row_halo(gc, line, shape) + halos[2:]
    n1, st, *dm0 = first_back(0, gc, halos, a0, wm0, mom10)
    st = exchange(st)
    home = lambda field: field.transpose(2, 0, 1, 3)
    if owned:
        zero = add_grads(
            side0[0], swap_cores(side0[1], shape), dm0[0], swap_cores(dm0[1], shape)
        )
        zero, n1, dr1 = lax.optimization_barrier((zero, n1, dr1))
        zero = owner_parts(zero, shape)
        ga0, gn0, mine, theirs = last_weight(n1, a0, st, mom10)
        tail = owner_parts(core_sums(mine, theirs, shape), shape)
        gx = last(ga0, gz0, wr0)
        pooled = pooled / (counts * float(rows * shape[1] * width))[:, None]
        values = call(
            k_update,
            "update",
            near(*[weights[i].shape for i in range(10)] * 3),
            [(me, SM)]
            + near(zero, one, tail, dr1, gn0, gn1, gd0, gd1, gw0, gw1, *weights, *momenta),
            limit=12,
        )
        return (home(out), pooled, home(gx), *values)

    ga0, gn0, dr0 = last_weight(n1, a0, st, mom10)
    gx = last(ga0, gz0, wr0)
    (de0, dk0), (de1, dk1), dm0, dm1 = side0, side1, dm0[0], dm1[0]
    pooled = pooled / (counts * float(rows * shape[1] * width))[:, None]

    def own(full):
        parts = full.reshape((devices, full.shape[0] // devices) + full.shape[1:])
        return jnp.sum(lax.all_to_all(parts, AX, 0, 0), axis=0)

    deltas = [
        jnp.stack([own(dr0), own(dr1[0])]),
        jnp.stack([own(dm0), own(dm1)]),
        jnp.stack([own(dk0[:27].T), own(dk1[:27].T)]),
        jnp.stack([own(de0), own(de1)]),
    ]

    def mine(vec0, vec1, row):
        share = vec0.shape[1] // devices
        both = jnp.stack([vec0[row], vec1[row]])
        return lax.dynamic_slice_in_dim(both, rank * share, share, axis=1)

    for first_part, second_part in ((gn0, gn1), (gd0, gd1), (gw0, gw1)):
        deltas.append(mine(first_part, second_part, 0))
        deltas.append(mine(first_part, second_part, 1))
    velocity = [MOMENTUM * momenta[i] + deltas[i] for i in range(10)]
    updated = [
        weights[i] - LEARN_RATE * (deltas[i] + MOMENTUM * velocity[i]) for i in range(10)
    ]
    return (home(out), pooled, home(gx), *deltas, *velocity, *updated)


def solution(mesh):
    field = P("dp", "fsdp", None, None)
    mat = P(None, AX, None)
    vec = P(None, AX)
    group = (mat,) * 4 + (vec,) * 6
    return jax.shard_map(
        body,
        mesh=mesh,
        in_specs=(field, field, P()) + group * 2,
        out_specs=(field, P(), field) + group * 3,
        check_vma=False,
    )
```

```python
import functools

import jax
import jax.numpy as jnp
from jax import lax
from jax.experimental import pallas as pl
from jax.experimental.pallas import tpu as pltpu
from jax.sharding import PartitionSpec as P

EPSILON = 1e-05
MOMENTUM = 0.9
LEARN_RATE = 0.0001
HIGHEST = lax.Precision.HIGHEST
AX = ("dp", "fsdp")
F32 = jnp.float32
BF16 = jnp.bfloat16
MIB = 1 << 20


VM = pl.BlockSpec(memory_space=pltpu.VMEM)
SM = pl.BlockSpec(memory_space=pltpu.SMEM)


def params(mib):
    return pltpu.CompilerParams(vmem_limit_bytes=mib * MIB)


def dot6(left, right):
    return jnp.dot(left, right, precision=HIGHEST, preferred_element_type=F32)


def dot6_rt(left, right):
    return lax.dot_general(
        left, right, (((1,), (1,)), ((), ())), precision=HIGHEST, preferred_element_type=F32
    )


def split2(value):
    high = value.astype(BF16)
    return high, (value - high.astype(F32)).astype(BF16)


def dot3(left, right):
    lh, ll = left
    rh, rl = right
    mm = functools.partial(jnp.dot, preferred_element_type=F32)
    return mm(lh, rh) + (mm(lh, rl) + mm(ll, rh))


def keep_split(value, parts_ref):
    rows = value.shape[0]
    for i in range(parts_ref.shape[0] // rows):
        high = value.astype(BF16)
        parts_ref[i * rows : (i + 1) * rows, :] = high
        value = value - high.astype(F32)


def dot_split(left, parts_ref, count):
    rows = parts_ref.shape[0] // count
    right = [parts_ref[i * rows : (i + 1) * rows, :] for i in range(count)]
    pieces = []
    for i in range(count):
        high = left.astype(BF16)
        pieces.append(high)
        left = left - high.astype(F32)
    mm = functools.partial(jnp.dot, preferred_element_type=F32)
    total = mm(pieces[0], right[1]) + mm(pieces[1], right[0])
    if count == 3:
        low = mm(pieces[1], right[1]) + mm(pieces[0], right[2]) + mm(pieces[2], right[0])
        total = total + low
    return mm(pieces[0], right[0]) + total


def total_rows(value):
    return jnp.sum(value, axis=0, keepdims=True)


def get(ref, start, count):
    return jnp.concatenate([ref[h, pl.ds(start, count), :] for h in range(ref.shape[0])], axis=1)


def put(ref, start, value):
    count = value.shape[0]
    for h in range(ref.shape[0]):
        ref[h, pl.ds(start, count), :] = value[:, h * 128 : h * 128 + 128]


def put_rows(st_ref, first, vec):
    for i in range(vec.shape[1] // 128):
        piece = vec[:, i * 128 : (i + 1) * 128]
        st_ref[:, first + i, :] = jnp.broadcast_to(piece, (st_ref.shape[0], 128))


def take_rows(st_ref, first, channels):
    return jnp.concatenate([st_ref[:, first + i, :] for i in range(channels // 128)], axis=1)


def take_sum(st_ref, first, channels):
    return total_rows(take_rows(st_ref, first, channels))


def narrow_moments(st_ref, channels, local, total):
    sums = take_rows(st_ref, 0, channels)
    squares = take_rows(st_ref, channels // 128, channels)
    mean = total_rows(sums) / total
    off = sums / local - mean
    var = (total_rows(squares) + local * total_rows(off * off)) / total
    return mean, lax.rsqrt(var + EPSILON)


def chunk_loop(voxels, chunk, step, carry):
    def one(i, carry):
        return step(pl.multiple_of(i * chunk, chunk), carry)

    return lax.fori_loop(0, voxels // chunk, one, carry)


def local_moments(ref, chunk):
    halves, voxels, _ = ref.shape
    zero = jnp.zeros((1, halves * 128), F32)
    total = chunk_loop(voxels, chunk, lambda i, acc: acc + total_rows(get(ref, i, chunk)), zero)
    mean = total / float(voxels)

    def squares(i, acc):
        value = get(ref, i, chunk) - mean
        return acc + total_rows(value * value)

    return total, chunk_loop(voxels, chunk, squares, zero)


def put_faces(ref, first, last, frames, start=0):
    halves = ref.shape[0]
    count = (ref.shape[1] - 2 * start) // frames
    for face, frame in ((first, 0), (last, frames - 1)):
        for h in range(halves):
            face[h, 0:count, :] = ref[h, pl.ds(start + frame, count, stride=frames), :]


STAGES = ((3, 4), (1, 2), (0,))


def slot_mask(slot):
    mask = 0
    for bits in STAGES:
        mask |= (slot & ((1 << len(bits)) - 1)) << bits[0]
        slot >>= len(bits)
    return mask


def order_rows(stacks, out_ref, me, first, rows, lanes=slice(None)):
    slot = 0
    for stack in stacks:
        for s in range(stack.shape[0]):
            where = pl.multiple_of(jnp.bitwise_xor(me, slot_mask(slot)) * rows, rows)
            out_ref[pl.ds(where, rows), :] = stack[s, first : first + rows, lanes]
            slot += 1


def k_stack(*refs):
    *parts, out = refs
    at = 0
    for part in parts:
        out[at : at + part.shape[0]] = part[...]
        at += part.shape[0]


def as_column(row):
    n = row.shape[1]
    same = lax.broadcasted_iota(jnp.int32, (n, n), 0) == lax.broadcasted_iota(jnp.int32, (n, n), 1)
    return jnp.sum(jnp.where(same, jnp.broadcast_to(row, (n, n)), 0.0), axis=1, keepdims=True)


def k_pack(wr, wm, dw, we, g1, b1, g2, b2, g3, b3, t1, t2):
    share, narrow = wm.shape[1:]
    share_w = wr.shape[1]
    wide = we.shape[2]
    t1[0, 0:share_w, :] = wr[0]
    t1[0, share_w : share_w + share, :] = wm[0]
    lane = lax.broadcasted_iota(jnp.int32, (share, narrow), 1)
    blocks = []
    for b in range(2):
        block = jnp.concatenate([dw[b], jnp.zeros((share, narrow - 27), F32)], axis=1)
        for i, vec in enumerate((g1, b1, g2, b2)):
            block = jnp.where(lane == 27 + i, as_column(vec[b : b + 1, :]), block)
        blocks.append(block)
    block = jnp.where(lane < 32, blocks[0], pltpu.roll(blocks[1], 32, 1))
    for c, (vec, b) in enumerate(((g3, 0), (b3, 0), (g3, 1), (b3, 1))):
        column = as_column(vec[b : b + 1, :])
        for q in range(share_w // share):
            part = column[q * share : (q + 1) * share]
            block = jnp.where(lane == 64 + 8 * q + c, part, block)
    t1[0, share_w + share :, :] = block
    t2[0:share_w, :] = wr[1]
    t2[share_w : share_w + share, :] = wm[1]
    at = share_w + share
    for b in range(2):
        for q in range(wide // narrow):
            t2[at : at + share, :] = we[b, :, q * narrow : (q + 1) * narrow]
            at += share


def k_open_early(me_ref, mine, theirs, wm, tv, vw, scr):
    narrow = wm.shape[0]
    share = scr.shape[0] // (mine.shape[0] * 2)
    share_w = mine.shape[1] - 2 * share
    order_rows((mine, theirs), wm, me_ref[0], share_w, share)
    order_rows((mine, theirs), scr, me_ref[0], share_w + share, share, slice(0, 128))
    turned = scr[...].T
    tv[0] = turned[0:32]
    tv[1] = turned[32:64]
    groups = share_w // share
    lane = lax.broadcasted_iota(jnp.int32, (8, 128), 1)
    for t in range(vw.shape[2] // 128):
        value = jnp.zeros((8, 128), F32)
        for d in range(128 // share_w):
            for q in range(groups):
                source = (t * (128 // share_w) + d) * share
                target = d * share_w + q * share
                moved = pltpu.roll(turned[64 + 8 * q : 72 + 8 * q], (target - source) % narrow, 1)
                here = jnp.logical_and(lane >= target, lane < target + share)
                value = jnp.where(here, moved[:, 0:128], value)
        vw[0, 0:2, t * 128 : (t + 1) * 128] = value[0:2]
        vw[1, 0:2, t * 128 : (t + 1) * 128] = value[2:4]


def k_open_later(later, wr, wm, we0, we1):
    wide, narrow = wr.shape
    devices = later.shape[0]
    share, share_w = narrow // devices, wide // devices
    wr[...] = later[:, 0:share_w, :].reshape(wide, narrow)
    wm[...] = later[:, share_w : share_w + share, :].reshape(narrow, narrow)
    at = share_w + share
    for we in (we0, we1):
        for q in range(wide // narrow):
            piece = later[:, at : at + share, :]
            we[:, q * narrow : (q + 1) * narrow] = piece.reshape(narrow, narrow)
            at += share


def run_moments(f, value, acc_ref):
    count = float(value.shape[0])
    total = total_rows(value)
    mean = total / count
    apart = value - mean
    squares = total_rows(apart * apart)

    @pl.when(f == 0)
    def _():
        acc_ref[0:1, :] = total
        acc_ref[1:2, :] = squares

    @pl.when(f > 0)
    def _():
        done = f.astype(F32) * count
        seen = acc_ref[0:1, :]
        delta = mean - seen / done
        acc_ref[1:2, :] = acc_ref[1:2, :] + squares + delta * delta * (done * count / (done + count))
        acc_ref[0:1, :] = seen + total


def put_narrow(f, steps, a, a_ref, face_f, face_l, st_ref, acc_ref, frames):
    put(a_ref, 0, a)
    put_faces(a_ref, face_f, face_l, frames)
    run_moments(f, a, acc_ref)

    @pl.when(f == steps - 1)
    def _():
        put_rows(st_ref, 0, acc_ref[0:1, :])
        put_rows(st_ref, a_ref.shape[0], acc_ref[1:2, :])


def k_first(frames, f, steps, me_ref, x_ref, *refs):
    *w_refs, a_ref, face_f, face_l, st_ref, w_out, w_parts, acc_ref = refs
    wide = x_ref.shape[3]
    chunk = a_ref.shape[1]

    @pl.when(f == 0)
    def _():
        if len(w_refs) == 2:
            order_rows(w_refs, w_out, me_ref[0], 0, wide // (2 * w_refs[0].shape[0]))
        else:
            w_out[...] = w_refs[0][...]
        keep_split(w_out[...], w_parts)

    a = dot_split(x_ref[...].reshape(chunk, wide), w_parts, 3)
    put_narrow(f, steps, a, a_ref, face_f, face_l, st_ref, acc_ref, frames)


def finish_narrow(a_ref, st_ref, line):
    total, squares = local_moments(a_ref, line)
    put_rows(st_ref, 0, total)
    put_rows(st_ref, a_ref.shape[0], squares)


def by_frame(keep_ref, o, frames):
    frame = lax.broadcasted_iota(jnp.int32, (8, 128), 0) % frames
    value = jnp.zeros((8, 128), F32)
    for f in range(frames):
        value = jnp.where(frame == f, keep_ref[o * frames + f], value)
    return value


def make_taps(k_ref, keep_ref, wt_ref, frames, flipped):
    for o in range(3):
        keep = by_frame(keep_ref, o, frames)
        for i in range(9):
            tap = 9 * o + i
            source = 26 - tap if flipped else tap
            for h in range(wt_ref.shape[0]):
                row = k_ref[source : source + 1, h * 128 : h * 128 + 128]
                wt_ref[h, tap] = jnp.broadcast_to(row, (8, 128)) * keep


def frame_of(rows, frames):
    return lax.broadcasted_iota(jnp.int32, (rows // 8, 8, 128), 1) % frames


def shift_frames(field, before, after, line, frames):
    halves, voxels, _ = field.shape
    frame = frame_of(line, frames)

    def step(i, carry):
        for h in range(halves):
            value = field[h, pl.ds(i, line), :].reshape(line // 8, 8, 128)
            earlier = jnp.where(frame == 0, 0.0, pltpu.roll(value, 1, 1))
            later = jnp.where(frame == frames - 1, 0.0, pltpu.roll(value, 7, 1))
            before[h, pl.ds(i, line), :] = earlier.reshape(line, 128)
            after[h, pl.ds(i, line), :] = later.reshape(line, 128)
        return carry

    chunk_loop(voxels, line, step, 0)


def put_frames(target, frame, frames, pieces_):
    start = 0
    for piece in pieces_:
        count = piece.shape[0]
        for h in range(target.shape[0]):
            part = piece[:, h * 128 : h * 128 + 128]
            target[h, pl.ds(start * frames + frame, count, stride=frames), :] = part
        start += count


def place_frames(target, line, frames, halos):
    halves, voxels, _ = target.shape

    def clear(i, carry):
        for h in range(halves):
            target[h, pl.ds(i, line), :] = jnp.zeros((line, 128), F32)
        return carry

    chunk_loop(voxels, line, clear, 0)
    put_frames(target, 0, frames, halos[0])
    put_frames(target, frames - 1, frames, halos[1])


def make_halo_taps(k_ref, keep_ref, wt_ref, frames, flipped):
    frame = lax.broadcasted_iota(jnp.int32, (8, 128), 0) % frames
    for i in range(9):
        for h in range(wt_ref.shape[0]):
            value = jnp.zeros((8, 128), F32)
            for o, place in ((0, 0), (2, frames - 1)):
                tap = 26 - (9 * o + i) if flipped else 9 * o + i
                row = k_ref[tap : tap + 1, h * 128 : h * 128 + 128] * keep_ref[o * frames + place]
                value = jnp.where(frame == place, jnp.broadcast_to(row, (8, 128)), value)
            wt_ref[h, i] = value


def column_views(value, first, last):
    n = value.shape[0] - 2
    upper = lax.broadcasted_iota(jnp.int32, (n, 8, 128), 1) < 4
    turned = pltpu.roll(value, 4, 1)
    left = jnp.where(upper, turned[0:n], turned[1 : n + 1])
    right = jnp.where(upper, turned[1 : n + 1], turned[2:])
    return left, value[1 : n + 1], right


def line_views(ref, h, start, line, part, parts):
    n = line // 8 // parts
    zero = jnp.zeros((1, 8, 128), F32)
    pieces = []
    if part == 0:
        pieces.append(zero)
    low = part * n - (part > 0)
    high = (part + 1) * n + (part < parts - 1)
    body = ref[h, pl.ds(start + low * 8, (high - low) * 8), :]
    pieces.append(body.reshape(high - low, 8, 128))
    if part == parts - 1:
        pieces.append(zero)
    value = jnp.concatenate(pieces, axis=0) if len(pieces) > 1 else pieces[0]
    return column_views(value, part == 0, part == parts - 1)


def stencil_into(fields, wt_ref, out_ref, line, base=None, done_half=None):
    halves, voxels, _ = out_ref.shape
    rows = voxels // line
    parts = 2 if (line // 8) % 2 == 0 else 1
    n = line // 8 // parts
    for h in range(halves):
        for part in range(parts):

            def row(j, older, old):
                new = jnp.zeros((n, 8, 128), F32)
                start = pl.multiple_of(j * line, line)
                for o in range(len(fields)):
                    views = line_views(fields[o], h, start, line, part, parts)
                    for q in range(3):
                        older = older + views[q] * wt_ref[h, 9 * o + 6 + q][None]
                        old = old + views[q] * wt_ref[h, 9 * o + 3 + q][None]
                        new = new + views[q] * wt_ref[h, 9 * o + q][None]
                return older, old, new

            zero = jnp.zeros((n, 8, 128), F32)

            def step(j, accs):
                done, old, new = row(j, accs[0], accs[1])

                @pl.when(j >= 2)
                def _():
                    where = pl.multiple_of((j - 2) * line, line) + part * n * 8
                    where = pl.ds(pl.multiple_of(where, 8), n * 8)
                    value = done.reshape(n * 8, 128)
                    if base is not None:
                        value = value + base[h, where, :]
                    out_ref[h, where, :] = value

                return old, new

            lax.fori_loop(0, rows + 2, step, (zero, zero))
        if done_half is not None:
            done_half(h)


def halo_pieces(i, face, up, down, top, bottom, act):
    edge = up.shape[2]
    above = act(get(up.at[i], 0, edge))
    below = above if down is up else act(get(down.at[i], 0, edge))
    return above * top, act(get(face, 0, face.shape[1])), below * bottom


def both(refs):
    return (refs[0], refs[-1])


def part_of(voxels, line):
    for count in (4, 2):
        if voxels % (count * 8) == 0:
            return voxels // count
    return voxels


def first_act(a, mom_ref, tv_ref):
    scale = tv_ref[27:28, :] * mom_ref[1:2, :]
    return jnp.maximum((a - mom_ref[0:1, :]) * scale + tv_ref[28:29, :], 0.0)


def k_mix_own(line, frames, total, keep_ref, a_ref, *refs, flush, ready):
    c_ref, mp_ref, before, after, mom_ref, wt_ref = refs[-6:]
    *rows, st_in, w_ref, tv_ref = refs[:-6]
    up_ref, dn_ref = both(rows)
    halves, voxels, _ = a_ref.shape
    narrow = halves * 128
    mean, inverse = narrow_moments(st_in, narrow, float(voxels), total)
    mom_ref[0:1, :] = mean
    mom_ref[1:2, :] = inverse

    def mixed(value):
        return dot6(first_act(value, mom_ref, tv_ref), w_ref[...])

    chunk = part_of(voxels, line)

    def own(i, carry):
        put(mp_ref, pl.multiple_of(line + i, 8), mixed(get(a_ref, i, chunk)))
        return carry

    chunk_loop(voxels, chunk, own, 0)
    ready()
    above = mixed(get(up_ref, 0, line))
    below = above if dn_ref is up_ref else mixed(get(dn_ref, 0, line))
    put(mp_ref, 0, above * keep_ref[3 * frames])
    put(mp_ref, line + voxels, below * keep_ref[3 * frames + 1])
    flush(1)
    make_taps(tv_ref, keep_ref, wt_ref, frames, False)
    shift_frames(mp_ref, before, after, line, frames)
    flush(2)
    flush(3)
    stencil_into((before, mp_ref, after), wt_ref, c_ref, line, None, lambda h: flush(0, h))


def k_mix(line, frames, keep_ref, part_ref, hp_ref, hn_ref, *refs, flush, ready):
    c_ref, placed, st_ref, wt_ref = refs[-4:]
    *corners, mom_ref, w_ref, tv_ref = refs[:-4]
    cu_ref, cd_ref = both(corners)
    top = keep_ref[3 * frames]
    bottom = keep_ref[3 * frames + 1]
    halos = [
        halo_pieces(
            i, face, cu_ref, cd_ref, top, bottom,
            lambda value: dot6(first_act(value, mom_ref, tv_ref), w_ref[...]),
        )
        for i, face in enumerate((hp_ref, hn_ref))
    ]
    place_frames(placed, line, frames, halos)
    flush(1)
    make_halo_taps(tv_ref, keep_ref, wt_ref, frames, False)
    ready()
    stencil_into((placed,), wt_ref, c_ref, line, part_ref, lambda h: flush(0, h))
    finish_narrow(c_ref, st_ref, line)


def second_act(c, mom, tv):
    return (c - mom[0:1, :]) * (tv[29:30, :] * mom[1:2, :]) + tv[30:31, :]


def k_expand(line, total, c_ref, st_in, w_ref, tv_ref, mom_ref, off_ref, sloc_ref, seen_ref, st_ref,
             s_ref):
    halves, voxels, _ = c_ref.shape
    narrow, wide = w_ref.shape
    local = float(voxels)
    mean, inverse = narrow_moments(st_in, narrow, local, total)
    mom_ref[0:1, :] = mean
    mom_ref[1:2, :] = inverse
    mom = mom_ref[...]

    def act(i, acc):
        s = jnp.maximum(second_act(get(c_ref, i, line), mom, tv_ref), 0.0)
        s_ref[pl.ds(i, line), :] = s
        return acc + total_rows(s)

    sums = chunk_loop(voxels, line, act, jnp.zeros((1, narrow), F32))
    center = sums / local
    sloc_ref[...] = jnp.broadcast_to(center, (8, narrow))
    put_rows(st_ref, 0, sums)
    chunk = part_of(voxels, line)

    def gram(i, acc):
        s = s_ref[pl.ds(i, chunk), :] - center
        return acc + dot6(s.T, s)

    seen = chunk_loop(voxels, chunk, gram, jnp.zeros((narrow, narrow), F32))
    seen = dot6(jnp.concatenate([seen, sloc_ref[...]], axis=0), w_ref[...])
    off_ref[...] = seen[narrow:]
    seen = seen[0:narrow]
    seen_ref[...] = seen
    put_rows(st_ref, halves, total_rows(seen * w_ref[...]))


def k_widen(f, steps, c_ref, mom_ref, tv_ref, sloc_ref, w_ref, e_ref, w_parts):
    @pl.when(f == 0)
    def _():
        keep_split(w_ref[...], w_parts)

    s = jnp.maximum(second_act(get(c_ref, 0, c_ref.shape[1]), mom_ref[...], tv_ref), 0.0)
    e_ref[...] = dot_split(s - sloc_ref[0:1, :], w_parts, 3)


def third_norm(st_in, w_ref, off_ref, vw_ref, momw_ref, smean_ref, local, total):
    narrow, wide = w_ref.shape
    s_means = take_rows(st_in, 0, narrow) / local
    squares = take_rows(st_in, narrow // 128, wide)
    e_means = dot6(s_means, w_ref[...])
    mean = jnp.mean(e_means, axis=0, keepdims=True)
    away = e_means - mean
    var = (total_rows(squares) + local * total_rows(away * away)) / total
    inverse = lax.rsqrt(var + EPSILON)
    scale = vw_ref[0:1, :] * inverse
    momw_ref[0:1, :] = scale
    momw_ref[1:2, :] = (off_ref[0:1, :] - mean) * scale + vw_ref[1:2, :]
    momw_ref[2:3, :] = inverse
    smean_ref[0:1, :] = jnp.mean(s_means, axis=0, keepdims=True)


def k_join(frames, total, local, f, steps, e_ref, x_ref, st_in, off_ref, w_ref, vw_ref, wr_ref, x_out,
           a_ref, face_f, face_l, momw_ref, smean_ref, st_ref, w_parts, acc_ref):

    @pl.when(f == 0)
    def _():
        third_norm(st_in, w_ref, off_ref, vw_ref, momw_ref, smean_ref, local, total)
        keep_split(wr_ref[...], w_parts)

    x = x_ref[...].reshape(x_out.shape)
    x = jnp.maximum(e_ref[...] * momw_ref[0:1, :] + momw_ref[1:2, :] + x, 0.0)
    x_out[...] = x
    a = dot_split(x, w_parts, 3)
    put_narrow(f, steps, a, a_ref, face_f, face_l, st_ref, acc_ref, frames)


def wide_step(gz, s, f, u_ref, p_ref, bias_acc, w_parts):
    put(u_ref, 0, dot_split(gz, w_parts, 2))
    p = dot3(split2(s.T), split2(gz))
    part = total_rows(gz)

    @pl.when(f == 0)
    def _():
        p_ref[...] = p
        bias_acc[0:1, :] = part

    @pl.when(f > 0)
    def _():
        p_ref[...] = p_ref[...] + p
        bias_acc[0:1, :] = bias_acc[0:1, :] + part


def centred_act(c_ref, mom_ref, tv_ref, smean_ref):
    c = get(c_ref, 0, c_ref.shape[1])
    return jnp.maximum(second_act(c, mom_ref[...], tv_ref), 0.0) - smean_ref[0:1, :]


def wide_finish(p_ref, w_ref, inverse, bias_acc, st_ref):
    wide = w_ref.shape[1]
    gain_sum = total_rows(p_ref[...] * w_ref[...]) * inverse
    put_rows(st_ref, 0, bias_acc[0:1, :])
    put_rows(st_ref, wide // 128, gain_sum)


def k_turn(total, local, f, steps, e_ref, x_ref, cot_ref, c_ref, st_in, off_ref, w_ref, vw_ref, mom_ref,
           tv_ref, out_ref, gz_ref, u_ref, p_ref, momw_ref, smean_ref, pool_ref, st_ref, w_parts,
           bias_acc):
    chunk, wide = x_ref.shape

    @pl.when(f == 0)
    def _():
        third_norm(st_in, w_ref, off_ref, vw_ref, momw_ref, smean_ref, local, total)
        keep_split((w_ref[...] * momw_ref[0:1, :]).T, w_parts)

    z = e_ref[...] * momw_ref[0:1, :] + momw_ref[1:2, :] + x_ref[...]
    out = jnp.maximum(z, 0.0)
    out_ref[...] = out.reshape(out_ref.shape)
    pooled = jnp.sum(out.reshape(chunk // 8, 8, wide), axis=0)

    @pl.when(f == 0)
    def _():
        pool_ref[...] = pooled

    @pl.when(f > 0)
    def _():
        pool_ref[...] = pool_ref[...] + pooled

    gz = jnp.where(z > 0.0, cot_ref[...].reshape(chunk, wide), 0.0)
    gz_ref[...] = gz
    s = centred_act(c_ref, mom_ref, tv_ref, smean_ref)
    wide_step(gz, s, f, u_ref, p_ref, bias_acc, w_parts)

    @pl.when(f == steps - 1)
    def _():
        wide_finish(p_ref, w_ref, momw_ref[2:3, :], bias_acc, st_ref)


def k_second(total, f, steps, u_ref, c_ref, st_in, w_ref, momw_ref, smean_ref, mom_ref, tv_ref, *refs):
    *more, n_ref, gw_ref, st_ref, q_parts, acc_ref = refs
    halves, chunk, _ = u_ref.shape
    narrow, wide = w_ref.shape

    @pl.when(f == 0)
    def _():
        bias_sum = take_sum(st_in, 0, wide)
        gain_sum = take_sum(st_in, wide // 128, wide)
        gw_ref[0:1, :] = gain_sum
        gw_ref[1:2, :] = bias_sum
        alpha = momw_ref[0:1, :]
        w = w_ref[...]
        wt = split2(w.T)
        q = dot3(split2(w * (alpha * momw_ref[2:3, :] * (gain_sum / total))), wt)
        keep_split(q, q_parts)
        acc_ref[0:2, :] = jnp.zeros((2, narrow), F32)
        d = dot3(split2(jnp.broadcast_to(alpha * (bias_sum / total), (8, wide))), wt)
        acc_ref[2:3, :] = d[0:1, :]

    mom = mom_ref[...]
    c = get(c_ref, 0, chunk)
    y = second_act(c, mom, tv_ref)
    corr = dot_split(jnp.maximum(y, 0.0) - smean_ref[0:1, :], q_parts, 2)
    n = jnp.where(y > 0.0, get(u_ref, 0, chunk) - corr - acc_ref[2:3, :], 0.0)
    put(n_ref, 0, n)
    xhat = (c - mom[0:1, :]) * mom[1:2, :]
    acc_ref[0:1, :] = acc_ref[0:1, :] + total_rows(n)
    acc_ref[1:2, :] = acc_ref[1:2, :] + total_rows(n * xhat)

    @pl.when(f == steps - 1)
    def _():
        put_rows(st_ref, 0, acc_ref[0:1, :])
        put_rows(st_ref, halves, acc_ref[1:2, :])
        if more:
            st_ref[:, 2 * halves :, :] = more[0][...]


def expand_grad(local, total, p_ref, w_ref, gw_ref, momw_ref, smean_ref, sloc_ref, seen_ref):
    apart = sloc_ref[...] - smean_ref[0:1, :]
    column = apart.T[:, 0:1] * local
    alpha = momw_ref[0:1, :]
    gamma = gw_ref[0:1, :] / total * momw_ref[2:3, :]
    beta = gw_ref[1:2, :] / total
    seen = seen_ref[...] + column * dot6(apart, w_ref[...])[0:1, :]
    return alpha * (p_ref[...] - column * beta - seen * gamma)


def norm_sums(f, st_in, out_ref):
    @pl.when(f == 0)
    def _():
        narrow = out_ref.shape[1]
        out_ref[0:1, :] = take_sum(st_in, narrow // 128, narrow)
        out_ref[1:2, :] = take_sum(st_in, 0, narrow)


def norm_back(n, a, gain, mom_ref, sums_ref, total):
    mom = mom_ref[...]
    xhat = (a - mom[0:1, :]) * mom[1:2, :]
    return gain * mom[1:2, :] * (n - sums_ref[1:2, :] / total - xhat * (sums_ref[0:1, :] / total))


def k_center(frames, total, f, steps, n_ref, c_ref, st_in, tv_ref, mom2_ref, gc_ref, face_f, face_l,
             gd_ref, *more):
    norm_sums(f, st_in, gd_ref)
    if more:
        more[0][...] = jnp.sum(st_in[:, 2 * gc_ref.shape[0] :, :], axis=0)
    chunk = n_ref.shape[1]
    n, c = get(n_ref, 0, chunk), get(c_ref, 0, chunk)
    put(gc_ref, 0, norm_back(n, c, tv_ref[29:30, :], mom2_ref, gd_ref, total))
    put_faces(gc_ref, face_f, face_l, frames)


def put_halves(piece, at, lower, mine, theirs):
    narrow = piece.shape[1]
    pairs = mine.shape[0]
    share = narrow // (2 * pairs)
    piece = piece.reshape(pairs, 2, share, narrow)
    mine[:, at : at + share, :] = jnp.where(lower, piece[:, 1], piece[:, 0])
    theirs[:, at : at + share, :] = jnp.where(lower, piece[:, 0], piece[:, 1])


def k_first_back(line, frames, more, keep_ref, gc_ref, hp_ref, hn_ref, *refs, flush, ready):
    *refs, gm_ref, gcp_ref, before, after, wt_ref, acc_ref = refs
    dm_refs = refs[-1:] if refs[-1].shape == acc_ref.shape else refs[-2:]
    *refs, n1_ref, st_ref = refs[: -len(dm_refs)]
    *refs, rest_ref = refs if more else (*refs, None)
    *refs, a_ref, w_ref, tv_ref, mom1_ref = refs
    rows, corners = refs[: len(refs) // 2], refs[len(refs) // 2 :]
    (up_ref, dn_ref), (cu_ref, cd_ref) = both(rows), both(corners)
    halves, voxels, _ = gc_ref.shape
    narrow = halves * 128
    top = keep_ref[3 * frames]
    bottom = keep_ref[3 * frames + 1]

    def own(i, carry):
        put(gcp_ref, pl.multiple_of(line + i, 8), get(gc_ref, i, line))
        return carry

    chunk_loop(voxels, line, own, 0)
    put(gcp_ref, 0, get(up_ref, 0, line) * top)
    put(gcp_ref, line + voxels, get(dn_ref, 0, line) * bottom)
    make_taps(tv_ref, keep_ref, wt_ref, frames, True)
    halos = [
        halo_pieces(i, face, cu_ref, cd_ref, top, bottom, lambda v: v)
        for i, face in enumerate((hp_ref, hn_ref))
    ]
    shift_frames(gcp_ref, before, after, line, frames)
    put_frames(before, 0, frames, halos[0])
    put_frames(after, frames - 1, frames, halos[1])
    stencil_into((before, gcp_ref, after), wt_ref, gm_ref, line)
    ready()
    wt = split2(w_ref[...].T)
    mom1 = mom1_ref[...]
    scale1 = tv_ref[27:28, :] * mom1[1:2, :]
    chunk = part_of(voxels, line)

    acc_ref[...] = jnp.zeros(acc_ref.shape, F32)

    def step(i, accs):
        gm = split2(get(gm_ref, i, chunk))
        gr = dot3(gm, wt)
        off = get(a_ref, i, chunk) - mom1[0:1, :]
        y = off * scale1 + tv_ref[28:29, :]
        n = jnp.where(y > 0.0, gr, 0.0)
        put(n1_ref, i, n)
        acc_ref[...] = acc_ref[...] + dot3(split2(jnp.maximum(y, 0.0).T), gm)
        return accs[0] + total_rows(n), accs[1] + total_rows(n * (off * mom1[1:2, :]))

    zero = jnp.zeros((1, narrow), F32)
    bias_acc, gain_acc = chunk_loop(voxels, chunk, step, (zero, zero))
    flush(0)
    put_rows(st_ref, 0, bias_acc)
    put_rows(st_ref, halves, gain_acc)
    if more:
        rest = rest_ref[...][None]
        st_ref[:, 2 * halves :, :] = jnp.broadcast_to(rest, (st_ref.shape[0],) + rest.shape[1:])
    if len(dm_refs) == 1:
        dm_refs[0][...] = acc_ref[...]
    else:
        put_halves(acc_ref[...], 0, top > 0.0, *dm_refs)


def k_side_grads(line, frames, total, keep_ref, gc_ref, mp_ref, before, after, placed, p_ref, w_ref, gw_ref,
                 momw_ref, smean_ref, sloc_ref, seen_ref, *refs):
    *out_refs, dk_ref = refs
    de = expand_grad(float(gc_ref.shape[1]), total, p_ref, w_ref, gw_ref, momw_ref, smean_ref, sloc_ref,
                     seen_ref)
    frame = frame_of(line, frames)

    def merge(i, carry):
        for h in range(gc_ref.shape[0]):
            where = pl.ds(i, line)
            halo_part = placed[h, where, :].reshape(line // 8, 8, 128)
            for target, place in ((before, 0), (after, frames - 1)):
                own = target[h, where, :].reshape(line // 8, 8, 128)
                own = jnp.where(frame == place, halo_part, own)
                target[h, where, :] = own.reshape(line, 128)
        return carry

    chunk_loop(placed.shape[1], line, merge, 0)
    halves, voxels, _ = gc_ref.shape
    narrow = halves * 128
    parts = 2 if (line // 8) % 2 == 0 else 1
    n = line // 8 // parts
    for h in range(halves):
        for o, field in enumerate((before, mp_ref, after)):

            def row(r, accs):
                accs = list(accs)
                for part in range(parts):
                    where = pl.multiple_of(r * line, line) + part * n * 8
                    g = gc_ref[h, pl.ds(pl.multiple_of(where, 8), n * 8), :].reshape(n, 8, 128)
                    for p in range(3):
                        start = pl.multiple_of((r + p) * line, line)
                        views = line_views(field, h, start, line, part, parts)
                        for q in range(3):
                            accs[3 * p + q] = accs[3 * p + q] + jnp.sum(g * views[q], axis=0)
                return tuple(accs)

            accs = lax.fori_loop(0, voxels // line, row, (jnp.zeros((8, 128), F32),) * 9)
            keep = by_frame(keep_ref, o, frames)
            for i in range(9):
                tap = 9 * o + i
                dk_ref[tap : tap + 1, h * 128 : h * 128 + 128] = total_rows(accs[i] * keep)
    dk_ref[27:128, :] = jnp.zeros((101, narrow), F32)
    whole = out_refs[0].shape == w_ref.shape
    if whole:
        out_refs[0][...] = de
        out_refs[1][...] = dk_ref[...]
    else:
        lower = keep_ref[3 * frames] > 0.0
        share = narrow // (2 * out_refs[0].shape[0])
        groups = de.shape[1] // narrow
        for g in range(groups):
            put_halves(de[:, g * narrow : (g + 1) * narrow], g * share, lower, *out_refs)
        turned = jnp.concatenate([dk_ref[...].T, jnp.zeros((narrow, narrow - 128), F32)], axis=1)
        put_halves(turned, groups * share, lower, *out_refs)


def k_add_grads(mine, theirs, mine_late, theirs_late, out):
    rows = mine.shape[1]
    out[:, 0:rows, :] = mine[...] + theirs[...]
    out[:, rows:, :] = mine_late[...] + theirs_late[...]


def k_update(*refs):
    me_ref, zero, one, reduce_zero, reduce_one = refs[:5]
    vecs = refs[5:11]
    params, momenta = refs[11:21], refs[21:31]
    grads, velocity, updated = refs[31:41], refs[41:51], refs[51:61]
    me = me_ref[0]
    share = params[1].shape[1]
    narrow = params[1].shape[2]
    groups = params[3].shape[2] // narrow

    def apply(i, b, grad, where=slice(None)):
        v = MOMENTUM * momenta[i][b, :, where] + grad
        grads[i][b, :, where] = grad
        velocity[i][b, :, where] = v
        updated[i][b, :, where] = params[i][b, :, where] - LEARN_RATE * (grad + MOMENTUM * v)

    packs = (jnp.sum(zero[...], axis=0), jnp.sum(one[...], axis=0))
    for b, (pack, reduce) in enumerate(zip(packs, (reduce_zero, reduce_one))):
        for g in range(groups):
            apply(3, b, pack[g * share : (g + 1) * share], slice(g * narrow, (g + 1) * narrow))
        at = groups * share
        apply(2, b, pack[at : at + share, 0:27])
        at += share
        apply(1, b, pack[at : at + share])
        apply(0, b, jnp.sum(reduce[...], axis=0))
    for j in range(3):
        for r in range(2):
            i = 4 + 2 * j + r
            pieces = []
            for b in range(2):
                value = vecs[2 * j + b][...]
                width = params[i].shape[1]
                length = value.shape[1]
                turned = pltpu.roll(value, length - me * width, 1)
                pieces.append(turned[r : r + 1, 0:width])
            grad = jnp.concatenate(pieces, axis=0)
            v = MOMENTUM * momenta[i][...] + grad
            grads[i][...] = grad
            velocity[i][...] = v
            updated[i][...] = params[i][...] - LEARN_RATE * (grad + MOMENTUM * v)


def put_by_core(dw, me_ref, out_refs):
    if len(out_refs) == 1:
        out_refs[0][...] = dw
    else:
        mine, theirs = out_refs
        dw = dw.reshape(mine.shape[0], 2, *mine.shape[1:])
        lower = me_ref[0] % 2 == 1
        mine[...] = jnp.where(lower, dw[:, 1], dw[:, 0])
        theirs[...] = jnp.where(lower, dw[:, 0], dw[:, 1])


def reduce_grad(ga, x, f, dwt):
    dw = dot3(split2(ga.T), split2(x))

    @pl.when(f == 0)
    def _():
        dwt[...] = dw

    @pl.when(f > 0)
    def _():
        dwt[...] = dwt[...] + dw


def k_between(total, f, steps, me_ref, n1_ref, a_ref, c_ref, x_ref, gz_in, st_in, tv_ref, mom1_ref,
              wr_ref, mom2_ref, tv2_ref, w_ref, momw_ref, smean_ref, gz_ref, u_ref, p_ref, gn_ref,
              st_ref, *refs):
    *dw_refs, wr_parts, w_parts, dwt, bias_acc = refs
    chunk, wide = x_ref.shape
    norm_sums(f, st_in, gn_ref)

    @pl.when(f == 0)
    def _():
        keep_split(wr_ref[...].T, wr_parts)
        keep_split((w_ref[...] * momw_ref[0:1, :]).T, w_parts)

    x = x_ref[...]
    n, a = get(n1_ref, 0, chunk), get(a_ref, 0, chunk)
    ga = norm_back(n, a, tv_ref[27:28, :], mom1_ref, gn_ref, total)
    gy = dot_split(ga, wr_parts, 2) + gz_in[...]
    gz = jnp.where(x > 0.0, gy, 0.0)
    gz_ref[...] = gz
    reduce_grad(ga, x, f, dwt)
    s = centred_act(c_ref, mom2_ref, tv2_ref, smean_ref)
    wide_step(gz, s, f, u_ref, p_ref, bias_acc, w_parts)

    @pl.when(f == steps - 1)
    def _():
        wide_finish(p_ref, w_ref, momw_ref[2:3, :], bias_acc, st_ref)
        put_by_core(dwt[...].T, me_ref, dw_refs)


def k_last_weight(total, f, steps, me_ref, n1_ref, a_ref, x_ref, st_in, tv_ref, mom1_ref, ga_ref,
                  gn_ref, *refs):
    *dw_refs, dwt = refs
    chunk = n1_ref.shape[1]
    norm_sums(f, st_in, gn_ref)
    n, a = get(n1_ref, 0, chunk), get(a_ref, 0, chunk)
    ga = norm_back(n, a, tv_ref[27:28, :], mom1_ref, gn_ref, total)
    put(ga_ref, 0, ga)
    reduce_grad(ga, x_ref[...].reshape(chunk, -1), f, dwt)

    @pl.when(f == steps - 1)
    def _():
        put_by_core(dwt[...].T, me_ref, dw_refs)


def k_last(f, steps, ga_ref, gz_in, wr_ref, gx_ref, wr_parts):
    @pl.when(f == 0)
    def _():
        keep_split(wr_ref[...].T, wr_parts)

    gy = dot_split(get(ga_ref, 0, ga_ref.shape[1]), wr_parts, 2) + gz_in[...]
    gx_ref[...] = gy.reshape(gx_ref.shape)


def exchange(rows):
    return lax.all_to_all(rows, AX, 0, 0)


def meet(value, bits, devices):
    parts = [value]
    for step in range(1, 1 << len(bits)):
        mask = step << bits[0]
        parts.append(lax.ppermute(value, AX, [(i, i ^ mask) for i in range(devices)]))
    return parts


def perm(step, shape):
    dp, fs = shape
    pairs = []
    for i in range(dp):
        for j in range(fs):
            a, b = i + step[0], j + step[1]
            if 0 <= a < dp and 0 <= b < fs:
                pairs.append((i * fs + j, a * fs + b))
    return pairs


def row_halo(field, line, shape):
    low, high = field[:, :line], field[:, field.shape[1] - line :]
    if shape[1] == 2:
        return [swap_cores(jnp.where(lax.axis_index("fsdp") == 0, high, low), shape)]
    move = lambda value, step: lax.ppermute(value, AX, perm(step, shape))
    return [move(high, (0, 1)), move(low, (0, -1))]


def frame_halo(first, last, width, shape, beside):
    count = first.shape[1]
    move = lambda value, step: lax.ppermute(value, AX, perm(step, shape))
    before, after = move(last, (1, 0)), move(first, (-1, 0))
    tops = jnp.stack([before[:, :width], after[:, :width]])
    ends = jnp.stack([before[:, count - width :], after[:, count - width :]])
    tops, ends, *beside = lax.optimization_barrier((tops, ends, *beside))
    if shape[1] == 2:
        corners = [swap_cores(jnp.where(lax.axis_index("fsdp") == 0, ends, tops), shape)]
    else:
        corners = [move(ends, (0, 1)), move(tops, (0, -1))]
    return [before, after, *corners], *beside


def tree_gather(part, devices, name):
    for bits in STAGES[:-1]:
        parts = meet(part, bits, devices)
        dims = (part.shape[0] * len(parts),) + part.shape[1:]
        part = call(k_stack, name, [(dims, HB)], [(piece, VM) for piece in parts], limit=4)[0]
    return meet(part, STAGES[-1], devices)


def core_sums(mine, theirs, shape):
    pairs = [(i, i ^ 1) for i in range(shape[0] * 2)]
    theirs = lax.ppermute(theirs, AX, pairs)
    return call(k_add, "core_add", [(mine.shape, HB)], [(mine, HB), (theirs, VM)], limit=8)[0]


def swap_cores(value, shape):
    return lax.ppermute(value, AX, [(i, i ^ 1) for i in range(shape[0] * 2)])


def k_add(left, right, out):
    out[...] = left[...] + right[...]


def owner_parts(parts, shape):
    return lax.all_to_all(parts, "dp", 0, 0)


HB = pl.BlockSpec(memory_space=pl.ANY)
FILLER = 1 << 31
HIDER = 1 << 32
MINOR = 1 << 27


def pieces(far, near):
    rows = near.shape[0]
    size = 4
    for dim in near.shape:
        size *= dim
    if size < MIB // 2:
        return [(far, near)]
    if len(near.shape) == 3 and rows <= 4:
        return [(far.at[i], near.at[i]) for i in range(rows)]
    if rows % 16 == 0:
        half = rows // 2
        return [(far.at[pl.ds(i * half, half)], near.at[pl.ds(i * half, half)]) for i in range(2)]
    return [(far, near)]


class Stream:
    def __init__(self, axis):
        self.axis = axis

    def part(self, ref, i, steps):
        size = ref.shape[self.axis] // steps
        where = pl.ds(i * size if isinstance(i, int) else pl.multiple_of(i * size, size), size)
        return ref.at[(slice(None),) * self.axis + (where,)]


WIDE, NARROW = Stream(0), Stream(1)
AHEAD = 2


def call(kernel, name, outs, ins, scratch=(), limit=24, steps=None, lazy=None, cost=1000):
    n_i, n_o, n_s = len(ins), len(outs), len(scratch)
    count = steps or 1
    near_i = [i for i in range(n_i) if ins[i][1] not in (SM, VM)]
    whole_i = [i for i in near_i if ins[i][1] is HB]
    flow_i = [i for i in near_i if ins[i][1] is not HB]
    whole_o = [i for i in range(n_o) if outs[i][1] is HB]
    flow_o = [i for i in range(n_o) if outs[i][1] is not HB]

    def run(*refs):
        far_in, far_out = refs[:n_i], refs[n_i : n_i + n_o]
        own = refs[n_i + n_o : n_i + n_o + n_s]
        near = refs[n_i + n_o + n_s : -2]
        sem, flow_sem = refs[-2:]
        in_refs, out_refs = list(far_in), list(near[len(near_i) :])
        for i, ref in zip(near_i, near):
            in_refs[i] = ref
        used = 0
        loads, late, stores = [], [], {}
        for i in whole_i:
            for src, dst in pieces(far_in[i], in_refs[i]):
                copy = pltpu.make_async_copy(src, dst, sem.at[used])
                (late if lazy and i in lazy else loads).append(copy)
                used += 1
        for i in whole_o:
            stores[i] = []
            for dst, src in pieces(far_out[i], out_refs[i]):
                stores[i].append(pltpu.make_async_copy(src, dst, sem.at[used]))
                used += 1
        started = set()

        def flush(i, part=None):
            for k, copy in enumerate(stores[i]):
                if part is None or k == part:
                    started.add((i, k))
                    copy.start()

        def ready():
            for copy in late:
                copy.wait()

        def flow_in(i):
            return [
                pltpu.make_async_copy(
                    ins[j][1].part(far_in[j], i, count),
                    ins[j][1].part(in_refs[j], i, count),
                    flow_sem.at[k, i],
                )
                for k, j in enumerate(flow_i)
            ]

        def flow_out(i):
            return [
                pltpu.make_async_copy(
                    outs[j][1].part(out_refs[j], i, count),
                    outs[j][1].part(far_out[j], i, count),
                    flow_sem.at[len(flow_i) + k, i],
                )
                for k, j in enumerate(flow_o)
            ]

        for copy in loads + late:
            copy.start()
        heavy = any(ins[j][1] is WIDE for j in flow_i)
        ahead = min(AHEAD, count) if heavy else count
        for i in range(ahead):
            for copy in flow_in(i):
                copy.start()
        for copy in loads:
            copy.wait()
        if steps is None:
            kernel(*in_refs, *out_refs, *own, **({} if lazy is None else {"flush": flush, "ready": ready}))
        else:

            def step(i, carry):
                for copy in flow_in(i):
                    copy.wait()
                if count > ahead:

                    @pl.when(i + ahead < count)
                    def _():
                        for copy in flow_in(i + ahead):
                            copy.start()

                views = list(in_refs) + list(out_refs)
                for j in flow_i:
                    views[j] = ins[j][1].part(in_refs[j], i, count)
                for j in flow_o:
                    views[n_i + j] = outs[j][1].part(out_refs[j], i, count)
                kernel(i, count, *views, *own)
                for copy in flow_out(i):
                    copy.start()
                return carry

            lax.fori_loop(0, count, step, 0)
        for i in whole_o:
            for k, copy in enumerate(stores[i]):
                if (i, k) not in started:
                    copy.start()
        for i in range(count):
            for copy in flow_out(i):
                copy.wait()
        for i in whole_o:
            for copy in stores[i]:
                copy.wait()

    values = [
        value if spec in (SM, VM) else pltpu.with_memory_space_constraint(value, pltpu.HBM)
        for value, spec in ins
    ]
    whole = 2 * (len(whole_i) + len(whole_o))
    flows = len(flow_i) + len(flow_o)
    return pl.pallas_call(
        run,
        in_specs=[spec if spec in (SM, VM) else HB for _, spec in ins],
        out_specs=(HB,) * n_o,
        out_shape=tuple(pltpu.HBM(shape, F32) for shape, _ in outs),
        scratch_shapes=[pltpu.VMEM(shape, dtype) for shape, dtype in scratch]
        + [pltpu.VMEM(ins[i][0].shape, F32) for i in near_i]
        + [pltpu.VMEM(shape, F32) for shape, _ in outs]
        + [pltpu.SemaphoreType.DMA((max(whole, 1),)), pltpu.SemaphoreType.DMA((max(flows, 1), count))],
        compiler_params=params(limit),
        cost_estimate=pl.CostEstimate(flops=cost, bytes_accessed=1000, transcendentals=0),
        name=name,
    )(*values)


def body(inputs, cotangent, clip_index, *args):
    weights, momenta = args[:10], args[10:]
    frames, rows, width, wide = inputs.shape
    narrow = weights[0].shape[2]
    halves = narrow // 128
    shape = (lax.axis_size("dp"), lax.axis_size("fsdp"))
    devices = shape[0] * shape[1]
    rank = lax.axis_index(AX)
    voxels = frames * rows * width
    line = width * frames
    total = float(voxels * devices)
    few = 2 if voxels % (2 * 8 * frames) == 0 else 1
    many = 7 if voxels % (7 * 8 * frames) == 0 else 1
    x0 = inputs.transpose(1, 2, 0, 3)
    cot = cotangent.transpose(1, 2, 0, 3)

    edge = jnp.full((1,), -1, jnp.int32)
    window = lax.dynamic_slice_in_dim(
        jnp.concatenate([edge, clip_index, edge]), lax.axis_index("dp") * frames, frames + 2
    )
    centre = window[1:-1]
    flags = jnp.concatenate(
        [
            (window[:-2] == centre).astype(F32),
            jnp.ones((frames,), F32),
            (window[2:] == centre).astype(F32),
            (lax.axis_index("fsdp") > 0).astype(F32)[None],
            (lax.axis_index("fsdp") < shape[1] - 1).astype(F32)[None],
        ]
    )
    me = rank.astype(jnp.int32)[None]

    field_n = (halves, voxels, 128)
    grown_n = (halves, voxels + 2 * line, 128)
    face_n = (halves, voxels // frames, 128)
    field_w = (voxels, wide)
    stat_n = (devices, 2 * halves, 128)
    stat_e = (devices, (narrow + wide) // 128, 128)
    stat_w = (devices, 2 * wide // 128, 128)
    mom_n, mom_w = (8, narrow), (8, wide)
    down_r, down_m, down_e = (wide, narrow), (narrow, narrow), (narrow, wide)
    parts = lambda *values: [(value, NARROW) for value in values]

    near = lambda *values: [(value, HB) for value in values]
    here = lambda *values: [(value, VM) for value in values]
    fix = near
    owned = devices == 32
    half = (devices // 2, wide // devices, narrow)
    down_halves = (half, half) if owned else (down_r,)
    share = narrow // devices
    side = (devices // 2, share * (wide // narrow + 1), narrow)
    side_halves = (side, side) if owned else (down_e, (128, narrow))
    mixed_halves = ((devices // 2, share, narrow),) * 2 if owned else (down_m,)

    def first(wr0):
        return call(
            functools.partial(k_first, frames),
            "first",
            [(field_n, NARROW), (face_n, NARROW), (face_n, NARROW)] + near(stat_n, down_r),
            [(me, SM), (x0, WIDE)] + (here if owned else near)(*wr0),
            scratch=[((3 * wide, narrow), BF16), (mom_n, F32)],
            limit=48,
            steps=many,
        )

    if owned:
        share_n, share_w = weights[1].shape[1], weights[0].shape[1]
        early, late = call(
            k_pack,
            "pack",
            near(
                (1, share_w + 2 * share_n, narrow),
                (share_w + share_n * (1 + 2 * (wide // narrow)), narrow),
            ),
            near(*weights),
            limit=4,
        )
        wr0 = slots = tree_gather(early, devices, "stack")
        late = lax.all_gather(late, AX, axis=0, tiled=False)
        a0, *faces, st, wr0 = first(wr0)
        wm0, tv, vw = call(
            k_open_early,
            "open_early",
            near(down_m, (2, 32, narrow), (2, 8, wide)),
            [(me, SM)] + near(*slots),
            scratch=[((narrow, 128), F32)],
            limit=8,
            cost=FILLER,
        )
        wr1, wm1, we0, we1 = call(
            k_open_later,
            "open_later",
            near(down_r, down_m, down_e, down_e),
            near(late),
            limit=16,
            cost=FILLER,
        )
    else:
        gather = lambda part: lax.all_gather(part, AX, axis=0, tiled=True)
        wr0, wr1 = [gather(weights[0][0])], gather(weights[0][1])
        wm0, wm1 = gather(weights[1][0]), gather(weights[1][1])
        we0, we1 = gather(weights[3][0]), gather(weights[3][1])
        small = jnp.concatenate([weights[2]] + [weights[i][..., None] for i in (4, 5, 6, 7)], axis=2)
        small = gather(small.transpose(1, 0, 2))
        tv = jnp.pad(small.transpose(1, 2, 0), ((0, 0), (0, 1), (0, 0)))
        large = gather(jnp.stack([weights[8], weights[9]], axis=2).transpose(1, 0, 2))
        vw = jnp.pad(large.transpose(1, 2, 0), ((0, 0), (0, 6), (0, 0)))

    def mix_own(block, a, rows, st, wm):
        return call(
            functools.partial(k_mix_own, line, frames, total),
            "mix_own",
            near(field_n, grown_n, grown_n, grown_n, mom_n),
            [(flags, SM)] + near(a) + here(*rows, st) + near(wm, tv[block]),
            scratch=[((halves, 27, 8, 128), F32)],
            limit=20,
            lazy=(),
            cost=MINOR,
        )

    def mix_halo(block, part, halos, mom, wm):
        return call(
            functools.partial(k_mix, line, frames),
            "mix",
            near(field_n, grown_n, stat_n),
            [(flags, SM)]
            + near(part, *halos[:2])
            + here(*halos[2:])
            + near(mom, wm, tv[block]),
            scratch=[((halves, 9, 8, 128), F32)],
            limit=20,
            lazy=(1,),
        )

    def mix(block, a, faces, st, wm):
        own = mix_own(block, a, row_halo(a, line, shape), st, wm)
        halos, part, *grown, mom = frame_halo(*faces, width, shape, own)
        c, placed, st = mix_halo(block, part, halos, mom, wm)
        return c, grown + [placed], mom, st

    def expand(block, c, st, we):
        return call(
            functools.partial(k_expand, line, total),
            "expand",
            near(mom_n, mom_w, mom_n, down_e, stat_e),
            near(c) + here(st, we) + near(tv[block]),
            scratch=[((voxels, narrow), F32)],
            limit=20,
        )

    def widen(block, c, mom2, sloc, we):
        return call(
            k_widen,
            "widen",
            [(field_w, WIDE)],
            [(c, NARROW)] + near(mom2, tv[block], sloc, we),
            scratch=[((3 * narrow, wide), BF16)],
            limit=48,
            steps=many,
            cost=FILLER,
        )[0]

    def join(e, x, st, off, we, wr):
        return call(
            functools.partial(k_join, frames, total, float(voxels)),
            "join",
            [(field_w, WIDE), (field_n, NARROW), (face_n, NARROW), (face_n, NARROW)]
            + near(mom_w, mom_n, stat_n),
            [(e, WIDE), (x, WIDE)] + here(st) + near(off, we, vw[0], wr),
            scratch=[((3 * wide, narrow), BF16), (mom_n, F32)],
            limit=56,
            steps=many,
        )

    def turn(e, x, c, st, off, we, mom2):
        return call(
            functools.partial(k_turn, total, float(voxels)),
            "turn",
            [((rows, width, frames, wide), WIDE), (field_w, WIDE), (field_n, NARROW)]
            + near(down_e, mom_w, mom_n, mom_w, stat_w),
            [(e, WIDE), (x, WIDE), (cot, WIDE), (c, NARROW)]
            + here(st)
            + near(off, we, vw[1], mom2, tv[1]),
            scratch=[((2 * wide, narrow), BF16), (mom_w, F32)],
            limit=58,
            steps=many,
        )

    def stat_with(more):
        return (devices, 2 * halves + sum(value.shape[-2] for value in more), 128)

    def second(block, u, c, st, we, momw, smean, mom2, *more):
        return call(
            functools.partial(k_second, total),
            "second",
            parts(field_n) + near(mom_w, stat_with(more)),
            parts(u, c) + here(st, we) + near(momw, smean, mom2, tv[block], *more),
            scratch=[((2 * narrow, narrow), BF16), (mom_n, F32)],
            limit=24,
            steps=few,
        )

    def center(block, n, c, st, mom2):
        return call(
            functools.partial(k_center, frames, total),
            "center",
            [(field_n, NARROW), (face_n, NARROW), (face_n, NARROW)]
            + near(mom_n, *([(st.shape[1] - 2 * halves, 128)] if st.shape[1] > 2 * halves else [])),
            parts(n, c) + here(st) + near(tv[block], mom2),
            limit=24,
            steps=many,
        )

    def first_back(block, gc, halos, a, wm, mom1, *more):
        return call(
            functools.partial(k_first_back, line, frames, len(more)),
            "first_back",
            near(field_n, stat_with(more), *mixed_halves),
            [(flags, SM)]
            + near(gc, *halos[:2])
            + here(*halos[2:])
            + near(a, wm, tv[block], mom1, *more),
            scratch=[(field_n, F32)] + [(grown_n, F32)] * 3
            + [((halves, 27, 8, 128), F32), (down_m, F32)],
            limit=20,
            lazy=(2 + len(halos), 3 + len(halos), 5 + len(halos)),
        )

    def side_grads(gc, grown, p, we, gw, momw, smean, sloc, seen):
        return call(
            functools.partial(k_side_grads, line, frames, total),
            "side_grads",
            near(*side_halves),
            [(flags, SM)] + near(gc, *grown, p, we, gw, momw, smean, sloc, seen),
            scratch=[((128, narrow), F32)],
            limit=24,
            cost=HIDER,
        )

    def add_grads(mine, theirs, mine_late, theirs_late):
        dims = (mine.shape[0], mine.shape[1] + mine_late.shape[1], narrow)
        return call(
            k_add_grads,
            "add_grads",
            near(dims),
            near(mine) + here(theirs) + near(mine_late) + here(theirs_late),
            limit=12,
        )[0]

    def between(n1, a, st, mom1, wr, x, gz, c, mom2, we, momw, smean):
        return call(
            functools.partial(k_between, total),
            "between",
            [(field_w, WIDE), (field_n, NARROW)] + near(down_e, mom_n, stat_w, *down_halves),
            [(me, SM)]
            + parts(n1, a, c)
            + [(x, WIDE), (gz, WIDE)]
            + here(st)
            + near(tv[1], mom1, wr, mom2, tv[0], we, momw, smean),
            scratch=[((2 * narrow, wide), BF16), ((2 * wide, narrow), BF16), (down_e, F32),
                     (mom_w, F32)],
            limit=58,
            steps=many,
        )

    def last_weight(n1, a, st, mom1):
        return call(
            functools.partial(k_last_weight, total),
            "last_weight",
            [(field_n, NARROW)] + near(mom_n, *down_halves),
            [(me, SM)] + parts(n1, a) + [(x0, WIDE)] + here(st) + near(tv[0], mom1),
            scratch=[(down_e, F32)],
            limit=48,
            steps=many,
        )

    def last(ga, gz, wr):
        return call(
            k_last,
            "last",
            [((rows, width, frames, wide), WIDE)],
            [(ga, NARROW), (gz, WIDE)] + near(wr),
            scratch=[((2 * narrow, wide), BF16)],
            limit=48,
            steps=many,
            cost=FILLER,
        )[0]


    if not owned:
        a0, *faces, st, wr0 = first(wr0)
    c0, grown0, mom10, st = mix(0, a0, faces, exchange(st), wm0)
    mom20, off0, sloc0, seen0, st = expand(0, c0, exchange(st), we0)
    e0 = widen(0, c0, mom20, sloc0, we0)
    x1, a1, *faces, momw0, smean0, st = join(e0, x0, exchange(st), off0, we0, wr1)
    c1, grown1, mom11, st = mix(1, a1, faces, exchange(st), wm1)
    mom21, off1, sloc1, seen1, st = expand(1, c1, exchange(st), we1)
    e1 = widen(1, c1, mom21, sloc1, we1)
    out, gz1, u1, p1, momw1, smean1, pool, st = turn(
        e1, x1, c1, exchange(st), off1, we1, mom21
    )

    clips = clip_index.shape[0] // 6
    labels = jnp.arange(clips, dtype=jnp.int32)
    hot = (centre[None, :] == labels[:, None]).astype(F32)
    pooled = jnp.dot(
        jnp.concatenate([hot] * (8 // frames), axis=1), pool, precision=HIGHEST,
        preferred_element_type=F32,
    )
    if owned:
        room = -(-clips * share_w // 128) * 128
        pooled = pooled.reshape(clips, devices, share_w).transpose(1, 0, 2).reshape(devices, -1)
        pooled = jnp.pad(pooled, ((0, 0), (0, room - clips * share_w)))
        more = (pooled.reshape(devices, room // 128, 128),)
    else:
        more = ()
        pooled = lax.psum(pooled, AX)
    counts = jnp.sum((clip_index[None, :] == labels[:, None]).astype(F32), axis=1)

    n, gw1, st = second(1, u1, c1, exchange(st), we1, momw1, smean1, mom21, *more)
    gc, face_f, face_l, gd1, *more = center(1, n, c1, exchange(st), mom21)
    faces = (face_f, face_l)
    side1 = side_grads(gc, grown1, p1, we1, gw1, momw1, smean1, sloc1, seen1)
    halos, *side1 = frame_halo(*faces, width, shape, side1)
    halos = halos[:2] + row_halo(gc, line, shape) + halos[2:]
    n1, st, *dm1 = first_back(1, gc, halos, a1, wm1, mom11, *more)
    st = exchange(st)
    if owned:
        one = add_grads(
            side1[0], swap_cores(side1[1], shape), dm1[0], swap_cores(dm1[1], shape)
        )
        one, st = lax.optimization_barrier((one, st))
        one = owner_parts(one, shape)
        pooled = st[:, 2 * halves :, :].reshape(devices, -1)[:, : clips * share_w]
        pooled = pooled.reshape(devices, clips, share_w).transpose(1, 0, 2).reshape(clips, wide)
    gz0, u0, p0, gn1, st, *dr1 = between(
        n1, a1, st, mom11, wr1, x1, gz1, c0, mom20, we0, momw0, smean0
    )
    if owned:
        st, one = lax.optimization_barrier((st, one))
    st = exchange(st)
    if owned:
        dr1 = core_sums(*dr1, shape)
        dr1, st = lax.optimization_barrier((dr1, st))
        dr1 = owner_parts(dr1, shape)
    n, gw0, st = second(0, u0, c0, st, we0, momw0, smean0, mom20)
    gc, *faces, gd0 = center(0, n, c0, exchange(st), mom20)
    side0 = side_grads(gc, grown0, p0, we0, gw0, momw0, smean0, sloc0, seen0)
    halos, *side0 = frame_halo(*faces, width, shape, side0)
    halos = halos[:2] + row_halo(gc, line, shape) + halos[2:]
    n1, st, *dm0 = first_back(0, gc, halos, a0, wm0, mom10)
    st = exchange(st)
    home = lambda field: field.transpose(2, 0, 1, 3)
    if owned:
        zero = add_grads(
            side0[0], swap_cores(side0[1], shape), dm0[0], swap_cores(dm0[1], shape)
        )
        zero, n1, dr1 = lax.optimization_barrier((zero, n1, dr1))
        zero = owner_parts(zero, shape)
        ga0, gn0, mine, theirs = last_weight(n1, a0, st, mom10)
        tail = owner_parts(core_sums(mine, theirs, shape), shape)
        gx = last(ga0, gz0, wr0)
        pooled = pooled / (counts * float(rows * shape[1] * width))[:, None]
        values = call(
            k_update,
            "update",
            near(*[weights[i].shape for i in range(10)] * 3),
            [(me, SM)]
            + near(zero, one, tail, dr1, gn0, gn1, gd0, gd1, gw0, gw1, *weights, *momenta),
            limit=12,
        )
        return (home(out), pooled, home(gx), *values)

    ga0, gn0, dr0 = last_weight(n1, a0, st, mom10)
    gx = last(ga0, gz0, wr0)
    (de0, dk0), (de1, dk1), dm0, dm1 = side0, side1, dm0[0], dm1[0]
    pooled = pooled / (counts * float(rows * shape[1] * width))[:, None]

    def own(full):
        parts = full.reshape((devices, full.shape[0] // devices) + full.shape[1:])
        return jnp.sum(lax.all_to_all(parts, AX, 0, 0), axis=0)

    deltas = [
        jnp.stack([own(dr0), own(dr1[0])]),
        jnp.stack([own(dm0), own(dm1)]),
        jnp.stack([own(dk0[:27].T), own(dk1[:27].T)]),
        jnp.stack([own(de0), own(de1)]),
    ]

    def mine(vec0, vec1, row):
        share = vec0.shape[1] // devices
        both = jnp.stack([vec0[row], vec1[row]])
        return lax.dynamic_slice_in_dim(both, rank * share, share, axis=1)

    for first_part, second_part in ((gn0, gn1), (gd0, gd1), (gw0, gw1)):
        deltas.append(mine(first_part, second_part, 0))
        deltas.append(mine(first_part, second_part, 1))
    velocity = [MOMENTUM * momenta[i] + deltas[i] for i in range(10)]
    updated = [
        weights[i] - LEARN_RATE * (deltas[i] + MOMENTUM * velocity[i]) for i in range(10)
    ]
    return (home(out), pooled, home(gx), *deltas, *velocity, *updated)


def solution(mesh):
    field = P("dp", "fsdp", None, None)
    mat = P(None, AX, None)
    vec = P(None, AX)
    group = (mat,) * 4 + (vec,) * 6
    return jax.shard_map(
        body,
        mesh=mesh,
        in_specs=(field, field, P()) + group * 2,
        out_specs=(field, P(), field) + group * 3,
        check_vma=False,
    )
```

```python
import functools

import jax
import jax.numpy as jnp
from jax import lax
from jax.experimental import pallas as pl
from jax.experimental.pallas import tpu as pltpu
from jax.sharding import PartitionSpec as P

EPSILON = 1e-05
MOMENTUM = 0.9
LEARN_RATE = 0.0001
HIGHEST = lax.Precision.HIGHEST
AX = ("dp", "fsdp")
F32 = jnp.float32
BF16 = jnp.bfloat16
MIB = 1 << 20


VM = pl.BlockSpec(memory_space=pltpu.VMEM)
SM = pl.BlockSpec(memory_space=pltpu.SMEM)


def params(mib):
    return pltpu.CompilerParams(vmem_limit_bytes=mib * MIB)


def dot6(left, right):
    return jnp.dot(left, right, precision=HIGHEST, preferred_element_type=F32)


def dot6_rt(left, right):
    return lax.dot_general(
        left, right, (((1,), (1,)), ((), ())), precision=HIGHEST, preferred_element_type=F32
    )


def split2(value):
    high = value.astype(BF16)
    return high, (value - high.astype(F32)).astype(BF16)


def dot3(left, right):
    lh, ll = left
    rh, rl = right
    mm = functools.partial(jnp.dot, preferred_element_type=F32)
    return mm(lh, rh) + (mm(lh, rl) + mm(ll, rh))


def keep_split(value, parts_ref):
    rows = value.shape[0]
    for i in range(parts_ref.shape[0] // rows):
        high = value.astype(BF16)
        parts_ref[i * rows : (i + 1) * rows, :] = high
        value = value - high.astype(F32)


def dot_split(left, parts_ref, count):
    rows = parts_ref.shape[0] // count
    right = [parts_ref[i * rows : (i + 1) * rows, :] for i in range(count)]
    pieces = []
    for i in range(count):
        high = left.astype(BF16)
        pieces.append(high)
        left = left - high.astype(F32)
    mm = functools.partial(jnp.dot, preferred_element_type=F32)
    total = mm(pieces[0], right[1]) + mm(pieces[1], right[0])
    if count == 3:
        low = mm(pieces[1], right[1]) + mm(pieces[0], right[2]) + mm(pieces[2], right[0])
        total = total + low
    return mm(pieces[0], right[0]) + total


def total_rows(value):
    return jnp.sum(value, axis=0, keepdims=True)


def get(ref, start, count):
    return jnp.concatenate([ref[h, pl.ds(start, count), :] for h in range(ref.shape[0])], axis=1)


def put(ref, start, value):
    count = value.shape[0]
    for h in range(ref.shape[0]):
        ref[h, pl.ds(start, count), :] = value[:, h * 128 : h * 128 + 128]


def put_rows(st_ref, first, vec):
    for i in range(vec.shape[1] // 128):
        piece = vec[:, i * 128 : (i + 1) * 128]
        st_ref[:, first + i, :] = jnp.broadcast_to(piece, (st_ref.shape[0], 128))


def take_rows(st_ref, first, channels):
    return jnp.concatenate([st_ref[:, first + i, :] for i in range(channels // 128)], axis=1)


def take_sum(st_ref, first, channels):
    return total_rows(take_rows(st_ref, first, channels))


def narrow_moments(st_ref, channels, local, total):
    sums = take_rows(st_ref, 0, channels)
    squares = take_rows(st_ref, channels // 128, channels)
    mean = total_rows(sums) / total
    off = sums / local - mean
    var = (total_rows(squares) + local * total_rows(off * off)) / total
    return mean, lax.rsqrt(var + EPSILON)


def chunk_loop(voxels, chunk, step, carry):
    def one(i, carry):
        return step(pl.multiple_of(i * chunk, chunk), carry)

    return lax.fori_loop(0, voxels // chunk, one, carry)


def local_moments(ref, chunk):
    halves, voxels, _ = ref.shape
    zero = jnp.zeros((1, halves * 128), F32)
    total = chunk_loop(voxels, chunk, lambda i, acc: acc + total_rows(get(ref, i, chunk)), zero)
    mean = total / float(voxels)

    def squares(i, acc):
        value = get(ref, i, chunk) - mean
        return acc + total_rows(value * value)

    return total, chunk_loop(voxels, chunk, squares, zero)


def put_faces(ref, first, last, frames, start=0):
    halves = ref.shape[0]
    count = (ref.shape[1] - 2 * start) // frames
    for face, frame in ((first, 0), (last, frames - 1)):
        for h in range(halves):
            face[h, 0:count, :] = ref[h, pl.ds(start + frame, count, stride=frames), :]


STAGES = ((3, 4), (1, 2), (0,))


def slot_mask(slot):
    mask = 0
    for bits in STAGES:
        mask |= (slot & ((1 << len(bits)) - 1)) << bits[0]
        slot >>= len(bits)
    return mask


def order_rows(stacks, out_ref, me, first, rows, lanes=slice(None)):
    slot = 0
    for stack in stacks:
        for s in range(stack.shape[0]):
            where = pl.multiple_of(jnp.bitwise_xor(me, slot_mask(slot)) * rows, rows)
            out_ref[pl.ds(where, rows), :] = stack[s, first : first + rows, lanes]
            slot += 1


def k_stack(*refs):
    *parts, out = refs
    at = 0
    for part in parts:
        out[at : at + part.shape[0]] = part[...]
        at += part.shape[0]


def as_column(row):
    n = row.shape[1]
    same = lax.broadcasted_iota(jnp.int32, (n, n), 0) == lax.broadcasted_iota(jnp.int32, (n, n), 1)
    return jnp.sum(jnp.where(same, jnp.broadcast_to(row, (n, n)), 0.0), axis=1, keepdims=True)


def k_pack(wr, wm, dw, we, g1, b1, g2, b2, g3, b3, t1, t2):
    share, narrow = wm.shape[1:]
    share_w = wr.shape[1]
    wide = we.shape[2]
    t1[0, 0:share_w, :] = wr[0]
    t1[0, share_w : share_w + share, :] = wm[0]
    lane = lax.broadcasted_iota(jnp.int32, (share, narrow), 1)
    blocks = []
    for b in range(2):
        block = jnp.concatenate([dw[b], jnp.zeros((share, narrow - 27), F32)], axis=1)
        for i, vec in enumerate((g1, b1, g2, b2)):
            block = jnp.where(lane == 27 + i, as_column(vec[b : b + 1, :]), block)
        blocks.append(block)
    block = jnp.where(lane < 32, blocks[0], pltpu.roll(blocks[1], 32, 1))
    for c, (vec, b) in enumerate(((g3, 0), (b3, 0), (g3, 1), (b3, 1))):
        column = as_column(vec[b : b + 1, :])
        for q in range(share_w // share):
            part = column[q * share : (q + 1) * share]
            block = jnp.where(lane == 64 + 8 * q + c, part, block)
    t1[0, share_w + share :, :] = block
    t2[0:share_w, :] = wr[1]
    t2[share_w : share_w + share, :] = wm[1]
    at = share_w + share
    for b in range(2):
        for q in range(wide // narrow):
            t2[at : at + share, :] = we[b, :, q * narrow : (q + 1) * narrow]
            at += share


def k_open_early(me_ref, mine, theirs, wm, tv, vw, scr):
    narrow = wm.shape[0]
    share = scr.shape[0] // (mine.shape[0] * 2)
    share_w = mine.shape[1] - 2 * share
    order_rows((mine, theirs), wm, me_ref[0], share_w, share)
    order_rows((mine, theirs), scr, me_ref[0], share_w + share, share, slice(0, 128))
    turned = scr[...].T
    tv[0] = turned[0:32]
    tv[1] = turned[32:64]
    groups = share_w // share
    lane = lax.broadcasted_iota(jnp.int32, (8, 128), 1)
    for t in range(vw.shape[2] // 128):
        value = jnp.zeros((8, 128), F32)
        for d in range(128 // share_w):
            for q in range(groups):
                source = (t * (128 // share_w) + d) * share
                target = d * share_w + q * share
                moved = pltpu.roll(turned[64 + 8 * q : 72 + 8 * q], (target - source) % narrow, 1)
                here = jnp.logical_and(lane >= target, lane < target + share)
                value = jnp.where(here, moved[:, 0:128], value)
        vw[0, 0:2, t * 128 : (t + 1) * 128] = value[0:2]
        vw[1, 0:2, t * 128 : (t + 1) * 128] = value[2:4]


def k_open_later(later, wr, wm, we0, we1):
    wide, narrow = wr.shape
    devices = later.shape[0]
    share, share_w = narrow // devices, wide // devices
    wr[...] = later[:, 0:share_w, :].reshape(wide, narrow)
    wm[...] = later[:, share_w : share_w + share, :].reshape(narrow, narrow)
    at = share_w + share
    for we in (we0, we1):
        for q in range(wide // narrow):
            piece = later[:, at : at + share, :]
            we[:, q * narrow : (q + 1) * narrow] = piece.reshape(narrow, narrow)
            at += share


def run_moments(f, value, acc_ref):
    count = float(value.shape[0])
    total = total_rows(value)
    mean = total / count
    apart = value - mean
    squares = total_rows(apart * apart)

    @pl.when(f == 0)
    def _():
        acc_ref[0:1, :] = total
        acc_ref[1:2, :] = squares

    @pl.when(f > 0)
    def _():
        done = f.astype(F32) * count
        seen = acc_ref[0:1, :]
        delta = mean - seen / done
        acc_ref[1:2, :] = acc_ref[1:2, :] + squares + delta * delta * (done * count / (done + count))
        acc_ref[0:1, :] = seen + total


def put_narrow(f, steps, a, a_ref, face_f, face_l, st_ref, acc_ref, frames):
    put(a_ref, 0, a)
    put_faces(a_ref, face_f, face_l, frames)
    run_moments(f, a, acc_ref)

    @pl.when(f == steps - 1)
    def _():
        put_rows(st_ref, 0, acc_ref[0:1, :])
        put_rows(st_ref, a_ref.shape[0], acc_ref[1:2, :])


def k_first(frames, f, steps, me_ref, x_ref, *refs):
    *w_refs, a_ref, face_f, face_l, st_ref, w_out, w_parts, acc_ref = refs
    wide = x_ref.shape[3]
    chunk = a_ref.shape[1]

    @pl.when(f == 0)
    def _():
        if len(w_refs) == 2:
            order_rows(w_refs, w_out, me_ref[0], 0, wide // (2 * w_refs[0].shape[0]))
        else:
            w_out[...] = w_refs[0][...]
        keep_split(w_out[...], w_parts)

    a = dot_split(x_ref[...].reshape(chunk, wide), w_parts, 3)
    put_narrow(f, steps, a, a_ref, face_f, face_l, st_ref, acc_ref, frames)


def finish_narrow(a_ref, st_ref, line):
    total, squares = local_moments(a_ref, line)
    put_rows(st_ref, 0, total)
    put_rows(st_ref, a_ref.shape[0], squares)


def by_frame(keep_ref, o, frames):
    frame = lax.broadcasted_iota(jnp.int32, (8, 128), 0) % frames
    value = jnp.zeros((8, 128), F32)
    for f in range(frames):
        value = jnp.where(frame == f, keep_ref[o * frames + f], value)
    return value


def make_taps(k_ref, keep_ref, wt_ref, frames, flipped):
    for o in range(3):
        keep = by_frame(keep_ref, o, frames)
        for i in range(9):
            tap = 9 * o + i
            source = 26 - tap if flipped else tap
            for h in range(wt_ref.shape[0]):
                row = k_ref[source : source + 1, h * 128 : h * 128 + 128]
                wt_ref[h, tap] = jnp.broadcast_to(row, (8, 128)) * keep


def frame_of(rows, frames):
    return lax.broadcasted_iota(jnp.int32, (rows // 8, 8, 128), 1) % frames


def shift_frames(field, before, after, line, frames):
    halves, voxels, _ = field.shape
    frame = frame_of(line, frames)

    def step(i, carry):
        for h in range(halves):
            value = field[h, pl.ds(i, line), :].reshape(line // 8, 8, 128)
            earlier = jnp.where(frame == 0, 0.0, pltpu.roll(value, 1, 1))
            later = jnp.where(frame == frames - 1, 0.0, pltpu.roll(value, 7, 1))
            before[h, pl.ds(i, line), :] = earlier.reshape(line, 128)
            after[h, pl.ds(i, line), :] = later.reshape(line, 128)
        return carry

    chunk_loop(voxels, line, step, 0)


def put_frames(target, frame, frames, pieces_):
    start = 0
    for piece in pieces_:
        count = piece.shape[0]
        for h in range(target.shape[0]):
            part = piece[:, h * 128 : h * 128 + 128]
            target[h, pl.ds(start * frames + frame, count, stride=frames), :] = part
        start += count


def place_frames(target, line, frames, halos):
    halves, voxels, _ = target.shape

    def clear(i, carry):
        for h in range(halves):
            target[h, pl.ds(i, line), :] = jnp.zeros((line, 128), F32)
        return carry

    chunk_loop(voxels, line, clear, 0)
    put_frames(target, 0, frames, halos[0])
    put_frames(target, frames - 1, frames, halos[1])


def make_halo_taps(k_ref, keep_ref, wt_ref, frames, flipped):
    frame = lax.broadcasted_iota(jnp.int32, (8, 128), 0) % frames
    for i in range(9):
        for h in range(wt_ref.shape[0]):
            value = jnp.zeros((8, 128), F32)
            for o, place in ((0, 0), (2, frames - 1)):
                tap = 26 - (9 * o + i) if flipped else 9 * o + i
                row = k_ref[tap : tap + 1, h * 128 : h * 128 + 128] * keep_ref[o * frames + place]
                value = jnp.where(frame == place, jnp.broadcast_to(row, (8, 128)), value)
            wt_ref[h, i] = value


def column_views(value, first, last):
    n = value.shape[0] - 2
    upper = lax.broadcasted_iota(jnp.int32, (n, 8, 128), 1) < 4
    turned = pltpu.roll(value, 4, 1)
    left = jnp.where(upper, turned[0:n], turned[1 : n + 1])
    right = jnp.where(upper, turned[1 : n + 1], turned[2:])
    return left, value[1 : n + 1], right


def line_views(ref, h, start, line, part, parts):
    n = line // 8 // parts
    zero = jnp.zeros((1, 8, 128), F32)
    pieces = []
    if part == 0:
        pieces.append(zero)
    low = part * n - (part > 0)
    high = (part + 1) * n + (part < parts - 1)
    body = ref[h, pl.ds(start + low * 8, (high - low) * 8), :]
    pieces.append(body.reshape(high - low, 8, 128))
    if part == parts - 1:
        pieces.append(zero)
    value = jnp.concatenate(pieces, axis=0) if len(pieces) > 1 else pieces[0]
    return column_views(value, part == 0, part == parts - 1)


def stencil_into(fields, wt_ref, out_ref, line, base=None, done_half=None):
    halves, voxels, _ = out_ref.shape
    rows = voxels // line
    parts = 2 if (line // 8) % 2 == 0 else 1
    n = line // 8 // parts
    for h in range(halves):
        for part in range(parts):

            def row(j, older, old):
                new = jnp.zeros((n, 8, 128), F32)
                start = pl.multiple_of(j * line, line)
                for o in range(len(fields)):
                    views = line_views(fields[o], h, start, line, part, parts)
                    for q in range(3):
                        older = older + views[q] * wt_ref[h, 9 * o + 6 + q][None]
                        old = old + views[q] * wt_ref[h, 9 * o + 3 + q][None]
                        new = new + views[q] * wt_ref[h, 9 * o + q][None]
                return older, old, new

            zero = jnp.zeros((n, 8, 128), F32)

            def step(j, accs):
                done, old, new = row(j, accs[0], accs[1])

                @pl.when(j >= 2)
                def _():
                    where = pl.multiple_of((j - 2) * line, line) + part * n * 8
                    where = pl.ds(pl.multiple_of(where, 8), n * 8)
                    value = done.reshape(n * 8, 128)
                    if base is not None:
                        value = value + base[h, where, :]
                    out_ref[h, where, :] = value

                return old, new

            lax.fori_loop(0, rows + 2, step, (zero, zero))
        if done_half is not None:
            done_half(h)


def halo_pieces(i, face, up, down, top, bottom, act):
    edge = up.shape[2]
    above = act(get(up.at[i], 0, edge))
    below = above if down is up else act(get(down.at[i], 0, edge))
    return above * top, act(get(face, 0, face.shape[1])), below * bottom


def both(refs):
    return (refs[0], refs[-1])


def part_of(voxels, line):
    for count in (4, 2):
        if voxels % (count * 8) == 0:
            return voxels // count
    return voxels


def first_act(a, mom_ref, tv_ref):
    scale = tv_ref[27:28, :] * mom_ref[1:2, :]
    return jnp.maximum((a - mom_ref[0:1, :]) * scale + tv_ref[28:29, :], 0.0)


def k_mix_own(line, frames, total, keep_ref, a_ref, *refs, flush, ready):
    c_ref, mp_ref, before, after, mom_ref, wt_ref = refs[-6:]
    *rows, st_in, w_ref, tv_ref = refs[:-6]
    up_ref, dn_ref = both(rows)
    halves, voxels, _ = a_ref.shape
    narrow = halves * 128
    mean, inverse = narrow_moments(st_in, narrow, float(voxels), total)
    mom_ref[0:1, :] = mean
    mom_ref[1:2, :] = inverse

    def mixed(value):
        return dot6(first_act(value, mom_ref, tv_ref), w_ref[...])

    chunk = part_of(voxels, line)

    def own(i, carry):
        put(mp_ref, pl.multiple_of(line + i, 8), mixed(get(a_ref, i, chunk)))
        return carry

    chunk_loop(voxels, chunk, own, 0)
    ready()
    above = mixed(get(up_ref, 0, line))
    below = above if dn_ref is up_ref else mixed(get(dn_ref, 0, line))
    put(mp_ref, 0, above * keep_ref[3 * frames])
    put(mp_ref, line + voxels, below * keep_ref[3 * frames + 1])
    flush(1)
    make_taps(tv_ref, keep_ref, wt_ref, frames, False)
    shift_frames(mp_ref, before, after, line, frames)
    flush(2)
    flush(3)
    stencil_into((before, mp_ref, after), wt_ref, c_ref, line, None, lambda h: flush(0, h))


def k_mix(line, frames, keep_ref, part_ref, hp_ref, hn_ref, *refs, flush, ready):
    c_ref, placed, st_ref, wt_ref = refs[-4:]
    *corners, mom_ref, w_ref, tv_ref = refs[:-4]
    cu_ref, cd_ref = both(corners)
    top = keep_ref[3 * frames]
    bottom = keep_ref[3 * frames + 1]
    halos = [
        halo_pieces(
            i, face, cu_ref, cd_ref, top, bottom,
            lambda value: dot6(first_act(value, mom_ref, tv_ref), w_ref[...]),
        )
        for i, face in enumerate((hp_ref, hn_ref))
    ]
    place_frames(placed, line, frames, halos)
    flush(1)
    make_halo_taps(tv_ref, keep_ref, wt_ref, frames, False)
    ready()
    stencil_into((placed,), wt_ref, c_ref, line, part_ref, lambda h: flush(0, h))
    finish_narrow(c_ref, st_ref, line)


def second_act(c, mom, tv):
    return (c - mom[0:1, :]) * (tv[29:30, :] * mom[1:2, :]) + tv[30:31, :]


def k_expand(line, total, c_ref, st_in, w_ref, tv_ref, mom_ref, off_ref, sloc_ref, seen_ref, st_ref,
             s_ref):
    halves, voxels, _ = c_ref.shape
    narrow, wide = w_ref.shape
    local = float(voxels)
    mean, inverse = narrow_moments(st_in, narrow, local, total)
    mom_ref[0:1, :] = mean
    mom_ref[1:2, :] = inverse
    mom = mom_ref[...]

    def act(i, acc):
        s = jnp.maximum(second_act(get(c_ref, i, line), mom, tv_ref), 0.0)
        s_ref[pl.ds(i, line), :] = s
        return acc + total_rows(s)

    sums = chunk_loop(voxels, line, act, jnp.zeros((1, narrow), F32))
    center = sums / local
    sloc_ref[...] = jnp.broadcast_to(center, (8, narrow))
    put_rows(st_ref, 0, sums)
    chunk = part_of(voxels, line)

    mm = functools.partial(jnp.dot, preferred_element_type=F32)

    def gram(i, accs):
        s = s_ref[pl.ds(i, chunk), :] - center
        high, rest = s.astype(BF16), s - s.astype(BF16).astype(F32)
        mid = rest.astype(BF16)
        low = (rest - mid.astype(F32)).astype(BF16)
        high_t, low_t = split2(s.T)
        even = mm(high_t, high) + mm(low_t, mid)
        return accs[0] + even, accs[1] + (mm(high_t, mid) + mm(high_t, low))

    blank = jnp.zeros((narrow, narrow), F32)
    seen, mixed = chunk_loop(voxels, chunk, gram, (blank, blank))
    seen = seen + (mixed + mixed.T)
    seen = dot6(jnp.concatenate([seen, sloc_ref[...]], axis=0), w_ref[...])
    off_ref[...] = seen[narrow:]
    seen = seen[0:narrow]
    seen_ref[...] = seen
    put_rows(st_ref, halves, total_rows(seen * w_ref[...]))


def k_widen(f, steps, c_ref, mom_ref, tv_ref, sloc_ref, w_ref, e_ref, w_parts):
    @pl.when(f == 0)
    def _():
        keep_split(w_ref[...], w_parts)

    s = jnp.maximum(second_act(get(c_ref, 0, c_ref.shape[1]), mom_ref[...], tv_ref), 0.0)
    e_ref[...] = dot_split(s - sloc_ref[0:1, :], w_parts, 3)


def third_norm(st_in, w_ref, off_ref, vw_ref, momw_ref, smean_ref, local, total):
    narrow, wide = w_ref.shape
    s_means = take_rows(st_in, 0, narrow) / local
    squares = take_rows(st_in, narrow // 128, wide)
    e_means = dot6(s_means, w_ref[...])
    mean = jnp.mean(e_means, axis=0, keepdims=True)
    away = e_means - mean
    var = (total_rows(squares) + local * total_rows(away * away)) / total
    inverse = lax.rsqrt(var + EPSILON)
    scale = vw_ref[0:1, :] * inverse
    momw_ref[0:1, :] = scale
    momw_ref[1:2, :] = (off_ref[0:1, :] - mean) * scale + vw_ref[1:2, :]
    momw_ref[2:3, :] = inverse
    smean_ref[0:1, :] = jnp.mean(s_means, axis=0, keepdims=True)


def k_join(frames, total, local, f, steps, e_ref, x_ref, st_in, off_ref, w_ref, vw_ref, wr_ref, x_out,
           a_ref, face_f, face_l, momw_ref, smean_ref, st_ref, w_parts, acc_ref):

    @pl.when(f == 0)
    def _():
        third_norm(st_in, w_ref, off_ref, vw_ref, momw_ref, smean_ref, local, total)
        keep_split(wr_ref[...], w_parts)

    x = x_ref[...].reshape(x_out.shape)
    x = jnp.maximum(e_ref[...] * momw_ref[0:1, :] + momw_ref[1:2, :] + x, 0.0)
    x_out[...] = x
    a = dot_split(x, w_parts, 3)
    put_narrow(f, steps, a, a_ref, face_f, face_l, st_ref, acc_ref, frames)


def wide_step(gz, s, f, u_ref, p_ref, bias_acc, w_parts):
    put(u_ref, 0, dot_split(gz, w_parts, 2))
    p = dot3(split2(s.T), split2(gz))
    part = total_rows(gz)

    @pl.when(f == 0)
    def _():
        p_ref[...] = p
        bias_acc[0:1, :] = part

    @pl.when(f > 0)
    def _():
        p_ref[...] = p_ref[...] + p
        bias_acc[0:1, :] = bias_acc[0:1, :] + part


def centred_act(c_ref, mom_ref, tv_ref, smean_ref):
    c = get(c_ref, 0, c_ref.shape[1])
    return jnp.maximum(second_act(c, mom_ref[...], tv_ref), 0.0) - smean_ref[0:1, :]


def wide_finish(p_ref, w_ref, inverse, bias_acc, st_ref):
    wide = w_ref.shape[1]
    gain_sum = total_rows(p_ref[...] * w_ref[...]) * inverse
    put_rows(st_ref, 0, bias_acc[0:1, :])
    put_rows(st_ref, wide // 128, gain_sum)


def k_turn(total, local, f, steps, e_ref, x_ref, cot_ref, c_ref, st_in, off_ref, w_ref, vw_ref, mom_ref,
           tv_ref, out_ref, gz_ref, u_ref, p_ref, momw_ref, smean_ref, pool_ref, st_ref, w_parts,
           bias_acc):
    chunk, wide = x_ref.shape

    @pl.when(f == 0)
    def _():
        third_norm(st_in, w_ref, off_ref, vw_ref, momw_ref, smean_ref, local, total)
        keep_split((w_ref[...] * momw_ref[0:1, :]).T, w_parts)

    z = e_ref[...] * momw_ref[0:1, :] + momw_ref[1:2, :] + x_ref[...]
    out = jnp.maximum(z, 0.0)
    out_ref[...] = out.reshape(out_ref.shape)
    pooled = jnp.sum(out.reshape(chunk // 8, 8, wide), axis=0)

    @pl.when(f == 0)
    def _():
        pool_ref[...] = pooled

    @pl.when(f > 0)
    def _():
        pool_ref[...] = pool_ref[...] + pooled

    gz = jnp.where(z > 0.0, cot_ref[...].reshape(chunk, wide), 0.0)
    gz_ref[...] = gz
    s = centred_act(c_ref, mom_ref, tv_ref, smean_ref)
    wide_step(gz, s, f, u_ref, p_ref, bias_acc, w_parts)

    @pl.when(f == steps - 1)
    def _():
        wide_finish(p_ref, w_ref, momw_ref[2:3, :], bias_acc, st_ref)


def k_second(total, f, steps, u_ref, c_ref, st_in, w_ref, momw_ref, smean_ref, mom_ref, tv_ref, *refs):
    *more, n_ref, gw_ref, st_ref, q_parts, acc_ref = refs
    halves, chunk, _ = u_ref.shape
    narrow, wide = w_ref.shape

    @pl.when(f == 0)
    def _():
        bias_sum = take_sum(st_in, 0, wide)
        gain_sum = take_sum(st_in, wide // 128, wide)
        gw_ref[0:1, :] = gain_sum
        gw_ref[1:2, :] = bias_sum
        alpha = momw_ref[0:1, :]
        w = w_ref[...]
        wt = split2(w.T)
        q = dot3(split2(w * (alpha * momw_ref[2:3, :] * (gain_sum / total))), wt)
        keep_split(q, q_parts)
        acc_ref[0:2, :] = jnp.zeros((2, narrow), F32)
        d = dot3(split2(jnp.broadcast_to(alpha * (bias_sum / total), (8, wide))), wt)
        acc_ref[2:3, :] = d[0:1, :]

    mom = mom_ref[...]
    c = get(c_ref, 0, chunk)
    y = second_act(c, mom, tv_ref)
    corr = dot_split(jnp.maximum(y, 0.0) - smean_ref[0:1, :], q_parts, 2)
    n = jnp.where(y > 0.0, get(u_ref, 0, chunk) - corr - acc_ref[2:3, :], 0.0)
    put(n_ref, 0, n)
    xhat = (c - mom[0:1, :]) * mom[1:2, :]
    acc_ref[0:1, :] = acc_ref[0:1, :] + total_rows(n)
    acc_ref[1:2, :] = acc_ref[1:2, :] + total_rows(n * xhat)

    @pl.when(f == steps - 1)
    def _():
        put_rows(st_ref, 0, acc_ref[0:1, :])
        put_rows(st_ref, halves, acc_ref[1:2, :])
        if more:
            st_ref[:, 2 * halves :, :] = more[0][...]


def expand_grad(local, total, p_ref, w_ref, gw_ref, momw_ref, smean_ref, sloc_ref, seen_ref):
    apart = sloc_ref[...] - smean_ref[0:1, :]
    column = apart.T[:, 0:1] * local
    alpha = momw_ref[0:1, :]
    gamma = gw_ref[0:1, :] / total * momw_ref[2:3, :]
    beta = gw_ref[1:2, :] / total
    seen = seen_ref[...] + column * dot6(apart, w_ref[...])[0:1, :]
    return alpha * (p_ref[...] - column * beta - seen * gamma)


def norm_sums(f, st_in, out_ref):
    @pl.when(f == 0)
    def _():
        narrow = out_ref.shape[1]
        out_ref[0:1, :] = take_sum(st_in, narrow // 128, narrow)
        out_ref[1:2, :] = take_sum(st_in, 0, narrow)


def norm_back(n, a, gain, mom_ref, sums_ref, total):
    mom = mom_ref[...]
    xhat = (a - mom[0:1, :]) * mom[1:2, :]
    return gain * mom[1:2, :] * (n - sums_ref[1:2, :] / total - xhat * (sums_ref[0:1, :] / total))


def k_center(frames, total, f, steps, n_ref, c_ref, st_in, tv_ref, mom2_ref, gc_ref, face_f, face_l,
             gd_ref, *more):
    norm_sums(f, st_in, gd_ref)
    if more:
        more[0][...] = jnp.sum(st_in[:, 2 * gc_ref.shape[0] :, :], axis=0)
    chunk = n_ref.shape[1]
    n, c = get(n_ref, 0, chunk), get(c_ref, 0, chunk)
    put(gc_ref, 0, norm_back(n, c, tv_ref[29:30, :], mom2_ref, gd_ref, total))
    put_faces(gc_ref, face_f, face_l, frames)


def put_halves(piece, at, lower, mine, theirs):
    narrow = piece.shape[1]
    pairs = mine.shape[0]
    share = narrow // (2 * pairs)
    piece = piece.reshape(pairs, 2, share, narrow)
    mine[:, at : at + share, :] = jnp.where(lower, piece[:, 1], piece[:, 0])
    theirs[:, at : at + share, :] = jnp.where(lower, piece[:, 0], piece[:, 1])


def k_first_back(line, frames, more, keep_ref, gc_ref, hp_ref, hn_ref, *refs, flush, ready):
    *refs, gm_ref, gcp_ref, before, after, wt_ref, acc_ref = refs
    dm_refs = refs[-1:] if refs[-1].shape == acc_ref.shape else refs[-2:]
    *refs, n1_ref, st_ref = refs[: -len(dm_refs)]
    *refs, rest_ref = refs if more else (*refs, None)
    *refs, a_ref, w_ref, tv_ref, mom1_ref = refs
    rows, corners = refs[: len(refs) // 2], refs[len(refs) // 2 :]
    (up_ref, dn_ref), (cu_ref, cd_ref) = both(rows), both(corners)
    halves, voxels, _ = gc_ref.shape
    narrow = halves * 128
    top = keep_ref[3 * frames]
    bottom = keep_ref[3 * frames + 1]

    def own(i, carry):
        put(gcp_ref, pl.multiple_of(line + i, 8), get(gc_ref, i, line))
        return carry

    chunk_loop(voxels, line, own, 0)
    put(gcp_ref, 0, get(up_ref, 0, line) * top)
    put(gcp_ref, line + voxels, get(dn_ref, 0, line) * bottom)
    make_taps(tv_ref, keep_ref, wt_ref, frames, True)
    halos = [
        halo_pieces(i, face, cu_ref, cd_ref, top, bottom, lambda v: v)
        for i, face in enumerate((hp_ref, hn_ref))
    ]
    shift_frames(gcp_ref, before, after, line, frames)
    put_frames(before, 0, frames, halos[0])
    put_frames(after, frames - 1, frames, halos[1])
    stencil_into((before, gcp_ref, after), wt_ref, gm_ref, line)
    ready()
    wt = split2(w_ref[...].T)
    mom1 = mom1_ref[...]
    scale1 = tv_ref[27:28, :] * mom1[1:2, :]
    chunk = part_of(voxels, line)

    acc_ref[...] = jnp.zeros(acc_ref.shape, F32)

    def step(i, accs):
        gm = split2(get(gm_ref, i, chunk))
        gr = dot3(gm, wt)
        off = get(a_ref, i, chunk) - mom1[0:1, :]
        y = off * scale1 + tv_ref[28:29, :]
        n = jnp.where(y > 0.0, gr, 0.0)
        put(n1_ref, i, n)
        acc_ref[...] = acc_ref[...] + dot3(split2(jnp.maximum(y, 0.0).T), gm)
        return accs[0] + total_rows(n), accs[1] + total_rows(n * (off * mom1[1:2, :]))

    zero = jnp.zeros((1, narrow), F32)
    bias_acc, gain_acc = chunk_loop(voxels, chunk, step, (zero, zero))
    flush(0)
    put_rows(st_ref, 0, bias_acc)
    put_rows(st_ref, halves, gain_acc)
    if more:
        rest = rest_ref[...][None]
        st_ref[:, 2 * halves :, :] = jnp.broadcast_to(rest, (st_ref.shape[0],) + rest.shape[1:])
    if len(dm_refs) == 1:
        dm_refs[0][...] = acc_ref[...]
    else:
        put_halves(acc_ref[...], 0, top > 0.0, *dm_refs)


def k_side_grads(line, frames, total, keep_ref, gc_ref, mp_ref, before, after, placed, p_ref, w_ref, gw_ref,
                 momw_ref, smean_ref, sloc_ref, seen_ref, *refs):
    *out_refs, dk_ref = refs
    de = expand_grad(float(gc_ref.shape[1]), total, p_ref, w_ref, gw_ref, momw_ref, smean_ref, sloc_ref,
                     seen_ref)
    frame = frame_of(line, frames)

    def merge(i, carry):
        for h in range(gc_ref.shape[0]):
            where = pl.ds(i, line)
            halo_part = placed[h, where, :].reshape(line // 8, 8, 128)
            for target, place in ((before, 0), (after, frames - 1)):
                own = target[h, where, :].reshape(line // 8, 8, 128)
                own = jnp.where(frame == place, halo_part, own)
                target[h, where, :] = own.reshape(line, 128)
        return carry

    chunk_loop(placed.shape[1], line, merge, 0)
    halves, voxels, _ = gc_ref.shape
    narrow = halves * 128
    parts = 2 if (line // 8) % 2 == 0 else 1
    n = line // 8 // parts
    for h in range(halves):
        for o, field in enumerate((before, mp_ref, after)):

            def row(r, accs):
                accs = list(accs)
                for part in range(parts):
                    where = pl.multiple_of(r * line, line) + part * n * 8
                    g = gc_ref[h, pl.ds(pl.multiple_of(where, 8), n * 8), :].reshape(n, 8, 128)
                    for p in range(3):
                        start = pl.multiple_of((r + p) * line, line)
                        views = line_views(field, h, start, line, part, parts)
                        for q in range(3):
                            accs[3 * p + q] = accs[3 * p + q] + jnp.sum(g * views[q], axis=0)
                return tuple(accs)

            accs = lax.fori_loop(0, voxels // line, row, (jnp.zeros((8, 128), F32),) * 9)
            keep = by_frame(keep_ref, o, frames)
            for i in range(9):
                tap = 9 * o + i
                dk_ref[tap : tap + 1, h * 128 : h * 128 + 128] = total_rows(accs[i] * keep)
    dk_ref[27:128, :] = jnp.zeros((101, narrow), F32)
    whole = out_refs[0].shape == w_ref.shape
    if whole:
        out_refs[0][...] = de
        out_refs[1][...] = dk_ref[...]
    else:
        lower = keep_ref[3 * frames] > 0.0
        share = narrow // (2 * out_refs[0].shape[0])
        groups = de.shape[1] // narrow
        for g in range(groups):
            put_halves(de[:, g * narrow : (g + 1) * narrow], g * share, lower, *out_refs)
        turned = jnp.concatenate([dk_ref[...].T, jnp.zeros((narrow, narrow - 128), F32)], axis=1)
        put_halves(turned, groups * share, lower, *out_refs)


def k_add_grads(mine, theirs, mine_late, theirs_late, out):
    rows = mine.shape[1]
    out[:, 0:rows, :] = mine[...] + theirs[...]
    out[:, rows:, :] = mine_late[...] + theirs_late[...]


def k_update(*refs):
    me_ref, zero, one, reduce_zero, reduce_one = refs[:5]
    vecs = refs[5:11]
    params, momenta = refs[11:21], refs[21:31]
    grads, velocity, updated = refs[31:41], refs[41:51], refs[51:61]
    me = me_ref[0]
    share = params[1].shape[1]
    narrow = params[1].shape[2]
    groups = params[3].shape[2] // narrow

    def apply(i, b, grad, where=slice(None)):
        v = MOMENTUM * momenta[i][b, :, where] + grad
        grads[i][b, :, where] = grad
        velocity[i][b, :, where] = v
        updated[i][b, :, where] = params[i][b, :, where] - LEARN_RATE * (grad + MOMENTUM * v)

    packs = (jnp.sum(zero[...], axis=0), jnp.sum(one[...], axis=0))
    for b, (pack, reduce) in enumerate(zip(packs, (reduce_zero, reduce_one))):
        for g in range(groups):
            apply(3, b, pack[g * share : (g + 1) * share], slice(g * narrow, (g + 1) * narrow))
        at = groups * share
        apply(2, b, pack[at : at + share, 0:27])
        at += share
        apply(1, b, pack[at : at + share])
        apply(0, b, jnp.sum(reduce[...], axis=0))
    for j in range(3):
        for r in range(2):
            i = 4 + 2 * j + r
            pieces = []
            for b in range(2):
                value = vecs[2 * j + b][...]
                width = params[i].shape[1]
                length = value.shape[1]
                turned = pltpu.roll(value, length - me * width, 1)
                pieces.append(turned[r : r + 1, 0:width])
            grad = jnp.concatenate(pieces, axis=0)
            v = MOMENTUM * momenta[i][...] + grad
            grads[i][...] = grad
            velocity[i][...] = v
            updated[i][...] = params[i][...] - LEARN_RATE * (grad + MOMENTUM * v)


def put_by_core(dw, me_ref, out_refs):
    if len(out_refs) == 1:
        out_refs[0][...] = dw
    else:
        mine, theirs = out_refs
        dw = dw.reshape(mine.shape[0], 2, *mine.shape[1:])
        lower = me_ref[0] % 2 == 1
        mine[...] = jnp.where(lower, dw[:, 1], dw[:, 0])
        theirs[...] = jnp.where(lower, dw[:, 0], dw[:, 1])


def reduce_grad(ga, x, f, dwt):
    dw = dot3(split2(ga.T), split2(x))

    @pl.when(f == 0)
    def _():
        dwt[...] = dw

    @pl.when(f > 0)
    def _():
        dwt[...] = dwt[...] + dw


def k_between(total, f, steps, me_ref, n1_ref, a_ref, c_ref, x_ref, gz_in, st_in, tv_ref, mom1_ref,
              wr_ref, mom2_ref, tv2_ref, w_ref, momw_ref, smean_ref, gz_ref, u_ref, p_ref, gn_ref,
              st_ref, *refs):
    *dw_refs, wr_parts, w_parts, dwt, bias_acc = refs
    chunk, wide = x_ref.shape
    norm_sums(f, st_in, gn_ref)

    @pl.when(f == 0)
    def _():
        keep_split(wr_ref[...].T, wr_parts)
        keep_split((w_ref[...] * momw_ref[0:1, :]).T, w_parts)

    x = x_ref[...]
    n, a = get(n1_ref, 0, chunk), get(a_ref, 0, chunk)
    ga = norm_back(n, a, tv_ref[27:28, :], mom1_ref, gn_ref, total)
    gy = dot_split(ga, wr_parts, 2) + gz_in[...]
    gz = jnp.where(x > 0.0, gy, 0.0)
    gz_ref[...] = gz
    reduce_grad(ga, x, f, dwt)
    s = centred_act(c_ref, mom2_ref, tv2_ref, smean_ref)
    wide_step(gz, s, f, u_ref, p_ref, bias_acc, w_parts)

    @pl.when(f == steps - 1)
    def _():
        wide_finish(p_ref, w_ref, momw_ref[2:3, :], bias_acc, st_ref)
        put_by_core(dwt[...].T, me_ref, dw_refs)


def k_last_weight(total, f, steps, me_ref, n1_ref, a_ref, x_ref, st_in, tv_ref, mom1_ref, ga_ref,
                  gn_ref, *refs):
    *dw_refs, dwt = refs
    chunk = n1_ref.shape[1]
    norm_sums(f, st_in, gn_ref)
    n, a = get(n1_ref, 0, chunk), get(a_ref, 0, chunk)
    ga = norm_back(n, a, tv_ref[27:28, :], mom1_ref, gn_ref, total)
    put(ga_ref, 0, ga)
    reduce_grad(ga, x_ref[...].reshape(chunk, -1), f, dwt)

    @pl.when(f == steps - 1)
    def _():
        put_by_core(dwt[...].T, me_ref, dw_refs)


def k_last(f, steps, ga_ref, gz_in, wr_ref, gx_ref, wr_parts):
    @pl.when(f == 0)
    def _():
        keep_split(wr_ref[...].T, wr_parts)

    gy = dot_split(get(ga_ref, 0, ga_ref.shape[1]), wr_parts, 2) + gz_in[...]
    gx_ref[...] = gy.reshape(gx_ref.shape)


def exchange(rows):
    return lax.all_to_all(rows, AX, 0, 0)


def meet(value, bits, devices):
    parts = [value]
    for step in range(1, 1 << len(bits)):
        mask = step << bits[0]
        parts.append(lax.ppermute(value, AX, [(i, i ^ mask) for i in range(devices)]))
    return parts


def perm(step, shape):
    dp, fs = shape
    pairs = []
    for i in range(dp):
        for j in range(fs):
            a, b = i + step[0], j + step[1]
            if 0 <= a < dp and 0 <= b < fs:
                pairs.append((i * fs + j, a * fs + b))
    return pairs


def row_halo(field, line, shape):
    low, high = field[:, :line], field[:, field.shape[1] - line :]
    if shape[1] == 2:
        return [swap_cores(jnp.where(lax.axis_index("fsdp") == 0, high, low), shape)]
    move = lambda value, step: lax.ppermute(value, AX, perm(step, shape))
    return [move(high, (0, 1)), move(low, (0, -1))]


def frame_halo(first, last, width, shape, beside):
    count = first.shape[1]
    move = lambda value, step: lax.ppermute(value, AX, perm(step, shape))
    before, after = move(last, (1, 0)), move(first, (-1, 0))
    tops = jnp.stack([before[:, :width], after[:, :width]])
    ends = jnp.stack([before[:, count - width :], after[:, count - width :]])
    tops, ends, *beside = lax.optimization_barrier((tops, ends, *beside))
    if shape[1] == 2:
        corners = [swap_cores(jnp.where(lax.axis_index("fsdp") == 0, ends, tops), shape)]
    else:
        corners = [move(ends, (0, 1)), move(tops, (0, -1))]
    return [before, after, *corners], *beside


def tree_gather(part, devices, name):
    for bits in STAGES[:-1]:
        parts = meet(part, bits, devices)
        dims = (part.shape[0] * len(parts),) + part.shape[1:]
        part = call(k_stack, name, [(dims, HB)], [(piece, VM) for piece in parts], limit=4)[0]
    return meet(part, STAGES[-1], devices)


def core_sums(mine, theirs, shape):
    pairs = [(i, i ^ 1) for i in range(shape[0] * 2)]
    theirs = lax.ppermute(theirs, AX, pairs)
    return call(k_add, "core_add", [(mine.shape, HB)], [(mine, HB), (theirs, VM)], limit=8)[0]


def swap_cores(value, shape):
    return lax.ppermute(value, AX, [(i, i ^ 1) for i in range(shape[0] * 2)])


def k_add(left, right, out):
    out[...] = left[...] + right[...]


def owner_parts(parts, shape):
    return lax.all_to_all(parts, "dp", 0, 0)


HB = pl.BlockSpec(memory_space=pl.ANY)
FILLER = 1 << 31
HIDER = 1 << 32
MINOR = 1 << 27


def pieces(far, near):
    rows = near.shape[0]
    size = 4
    for dim in near.shape:
        size *= dim
    if size < MIB // 2:
        return [(far, near)]
    if len(near.shape) == 3 and rows <= 4:
        return [(far.at[i], near.at[i]) for i in range(rows)]
    if rows % 16 == 0:
        half = rows // 2
        return [(far.at[pl.ds(i * half, half)], near.at[pl.ds(i * half, half)]) for i in range(2)]
    return [(far, near)]


class Stream:
    def __init__(self, axis):
        self.axis = axis

    def part(self, ref, i, steps):
        size = ref.shape[self.axis] // steps
        where = pl.ds(i * size if isinstance(i, int) else pl.multiple_of(i * size, size), size)
        return ref.at[(slice(None),) * self.axis + (where,)]


WIDE, NARROW = Stream(0), Stream(1)
AHEAD = 2


def call(kernel, name, outs, ins, scratch=(), limit=24, steps=None, lazy=None, cost=1000):
    n_i, n_o, n_s = len(ins), len(outs), len(scratch)
    count = steps or 1
    near_i = [i for i in range(n_i) if ins[i][1] not in (SM, VM)]
    whole_i = [i for i in near_i if ins[i][1] is HB]
    flow_i = [i for i in near_i if ins[i][1] is not HB]
    whole_o = [i for i in range(n_o) if outs[i][1] is HB]
    flow_o = [i for i in range(n_o) if outs[i][1] is not HB]

    def run(*refs):
        far_in, far_out = refs[:n_i], refs[n_i : n_i + n_o]
        own = refs[n_i + n_o : n_i + n_o + n_s]
        near = refs[n_i + n_o + n_s : -2]
        sem, flow_sem = refs[-2:]
        in_refs, out_refs = list(far_in), list(near[len(near_i) :])
        for i, ref in zip(near_i, near):
            in_refs[i] = ref
        used = 0
        loads, late, stores = [], [], {}
        for i in whole_i:
            for src, dst in pieces(far_in[i], in_refs[i]):
                copy = pltpu.make_async_copy(src, dst, sem.at[used])
                (late if lazy and i in lazy else loads).append(copy)
                used += 1
        for i in whole_o:
            stores[i] = []
            for dst, src in pieces(far_out[i], out_refs[i]):
                stores[i].append(pltpu.make_async_copy(src, dst, sem.at[used]))
                used += 1
        started = set()

        def flush(i, part=None):
            for k, copy in enumerate(stores[i]):
                if part is None or k == part:
                    started.add((i, k))
                    copy.start()

        def ready():
            for copy in late:
                copy.wait()

        def flow_in(i):
            return [
                pltpu.make_async_copy(
                    ins[j][1].part(far_in[j], i, count),
                    ins[j][1].part(in_refs[j], i, count),
                    flow_sem.at[k, i],
                )
                for k, j in enumerate(flow_i)
            ]

        def flow_out(i):
            return [
                pltpu.make_async_copy(
                    outs[j][1].part(out_refs[j], i, count),
                    outs[j][1].part(far_out[j], i, count),
                    flow_sem.at[len(flow_i) + k, i],
                )
                for k, j in enumerate(flow_o)
            ]

        for copy in loads + late:
            copy.start()
        heavy = any(ins[j][1] is WIDE for j in flow_i)
        ahead = min(AHEAD, count) if heavy else count
        for i in range(ahead):
            for copy in flow_in(i):
                copy.start()
        for copy in loads:
            copy.wait()
        if steps is None:
            kernel(*in_refs, *out_refs, *own, **({} if lazy is None else {"flush": flush, "ready": ready}))
        else:

            def step(i, carry):
                for copy in flow_in(i):
                    copy.wait()
                if count > ahead:

                    @pl.when(i + ahead < count)
                    def _():
                        for copy in flow_in(i + ahead):
                            copy.start()

                views = list(in_refs) + list(out_refs)
                for j in flow_i:
                    views[j] = ins[j][1].part(in_refs[j], i, count)
                for j in flow_o:
                    views[n_i + j] = outs[j][1].part(out_refs[j], i, count)
                kernel(i, count, *views, *own)
                for copy in flow_out(i):
                    copy.start()
                return carry

            lax.fori_loop(0, count, step, 0)
        for i in whole_o:
            for k, copy in enumerate(stores[i]):
                if (i, k) not in started:
                    copy.start()
        for i in range(count):
            for copy in flow_out(i):
                copy.wait()
        for i in whole_o:
            for copy in stores[i]:
                copy.wait()

    values = [
        value if spec in (SM, VM) else pltpu.with_memory_space_constraint(value, pltpu.HBM)
        for value, spec in ins
    ]
    whole = 2 * (len(whole_i) + len(whole_o))
    flows = len(flow_i) + len(flow_o)
    return pl.pallas_call(
        run,
        in_specs=[spec if spec in (SM, VM) else HB for _, spec in ins],
        out_specs=(HB,) * n_o,
        out_shape=tuple(pltpu.HBM(shape, F32) for shape, _ in outs),
        scratch_shapes=[pltpu.VMEM(shape, dtype) for shape, dtype in scratch]
        + [pltpu.VMEM(ins[i][0].shape, F32) for i in near_i]
        + [pltpu.VMEM(shape, F32) for shape, _ in outs]
        + [pltpu.SemaphoreType.DMA((max(whole, 1),)), pltpu.SemaphoreType.DMA((max(flows, 1), count))],
        compiler_params=params(limit),
        cost_estimate=pl.CostEstimate(flops=cost, bytes_accessed=1000, transcendentals=0),
        name=name,
    )(*values)


def body(inputs, cotangent, clip_index, *args):
    weights, momenta = args[:10], args[10:]
    frames, rows, width, wide = inputs.shape
    narrow = weights[0].shape[2]
    halves = narrow // 128
    shape = (lax.axis_size("dp"), lax.axis_size("fsdp"))
    devices = shape[0] * shape[1]
    rank = lax.axis_index(AX)
    voxels = frames * rows * width
    line = width * frames
    total = float(voxels * devices)
    few = 2 if voxels % (2 * 8 * frames) == 0 else 1
    many = 7 if voxels % (7 * 8 * frames) == 0 else 1
    x0 = inputs.transpose(1, 2, 0, 3)
    cot = cotangent.transpose(1, 2, 0, 3)

    edge = jnp.full((1,), -1, jnp.int32)
    window = lax.dynamic_slice_in_dim(
        jnp.concatenate([edge, clip_index, edge]), lax.axis_index("dp") * frames, frames + 2
    )
    centre = window[1:-1]
    flags = jnp.concatenate(
        [
            (window[:-2] == centre).astype(F32),
            jnp.ones((frames,), F32),
            (window[2:] == centre).astype(F32),
            (lax.axis_index("fsdp") > 0).astype(F32)[None],
            (lax.axis_index("fsdp") < shape[1] - 1).astype(F32)[None],
        ]
    )
    me = rank.astype(jnp.int32)[None]

    field_n = (halves, voxels, 128)
    grown_n = (halves, voxels + 2 * line, 128)
    face_n = (halves, voxels // frames, 128)
    field_w = (voxels, wide)
    stat_n = (devices, 2 * halves, 128)
    stat_e = (devices, (narrow + wide) // 128, 128)
    stat_w = (devices, 2 * wide // 128, 128)
    mom_n, mom_w = (8, narrow), (8, wide)
    down_r, down_m, down_e = (wide, narrow), (narrow, narrow), (narrow, wide)
    parts = lambda *values: [(value, NARROW) for value in values]

    near = lambda *values: [(value, HB) for value in values]
    here = lambda *values: [(value, VM) for value in values]
    fix = near
    owned = devices == 32
    half = (devices // 2, wide // devices, narrow)
    down_halves = (half, half) if owned else (down_r,)
    share = narrow // devices
    side = (devices // 2, share * (wide // narrow + 1), narrow)
    side_halves = (side, side) if owned else (down_e, (128, narrow))
    mixed_halves = ((devices // 2, share, narrow),) * 2 if owned else (down_m,)

    def first(wr0):
        return call(
            functools.partial(k_first, frames),
            "first",
            [(field_n, NARROW), (face_n, NARROW), (face_n, NARROW)] + near(stat_n, down_r),
            [(me, SM), (x0, WIDE)] + (here if owned else near)(*wr0),
            scratch=[((3 * wide, narrow), BF16), (mom_n, F32)],
            limit=48,
            steps=many,
        )

    if owned:
        share_n, share_w = weights[1].shape[1], weights[0].shape[1]
        early, late = call(
            k_pack,
            "pack",
            near(
                (1, share_w + 2 * share_n, narrow),
                (share_w + share_n * (1 + 2 * (wide // narrow)), narrow),
            ),
            near(*weights),
            limit=4,
        )
        wr0 = slots = tree_gather(early, devices, "stack")
        late = lax.all_gather(late, AX, axis=0, tiled=False)
        a0, *faces, st, wr0 = first(wr0)
        wm0, tv, vw = call(
            k_open_early,
            "open_early",
            near(down_m, (2, 32, narrow), (2, 8, wide)),
            [(me, SM)] + near(*slots),
            scratch=[((narrow, 128), F32)],
            limit=8,
            cost=FILLER,
        )
        wr1, wm1, we0, we1 = call(
            k_open_later,
            "open_later",
            near(down_r, down_m, down_e, down_e),
            near(late),
            limit=16,
            cost=FILLER,
        )
    else:
        gather = lambda part: lax.all_gather(part, AX, axis=0, tiled=True)
        wr0, wr1 = [gather(weights[0][0])], gather(weights[0][1])
        wm0, wm1 = gather(weights[1][0]), gather(weights[1][1])
        we0, we1 = gather(weights[3][0]), gather(weights[3][1])
        small = jnp.concatenate([weights[2]] + [weights[i][..., None] for i in (4, 5, 6, 7)], axis=2)
        small = gather(small.transpose(1, 0, 2))
        tv = jnp.pad(small.transpose(1, 2, 0), ((0, 0), (0, 1), (0, 0)))
        large = gather(jnp.stack([weights[8], weights[9]], axis=2).transpose(1, 0, 2))
        vw = jnp.pad(large.transpose(1, 2, 0), ((0, 0), (0, 6), (0, 0)))

    def mix_own(block, a, rows, st, wm):
        return call(
            functools.partial(k_mix_own, line, frames, total),
            "mix_own",
            near(field_n, grown_n, grown_n, grown_n, mom_n),
            [(flags, SM)] + near(a) + here(*rows, st) + near(wm, tv[block]),
            scratch=[((halves, 27, 8, 128), F32)],
            limit=20,
            lazy=(),
            cost=MINOR,
        )

    def mix_halo(block, part, halos, mom, wm):
        return call(
            functools.partial(k_mix, line, frames),
            "mix",
            near(field_n, grown_n, stat_n),
            [(flags, SM)]
            + near(part, *halos[:2])
            + here(*halos[2:])
            + near(mom, wm, tv[block]),
            scratch=[((halves, 9, 8, 128), F32)],
            limit=20,
            lazy=(1,),
        )

    def mix(block, a, faces, st, wm):
        own = mix_own(block, a, row_halo(a, line, shape), st, wm)
        halos, part, *grown, mom = frame_halo(*faces, width, shape, own)
        c, placed, st = mix_halo(block, part, halos, mom, wm)
        return c, grown + [placed], mom, st

    def expand(block, c, st, we):
        return call(
            functools.partial(k_expand, line, total),
            "expand",
            near(mom_n, mom_w, mom_n, down_e, stat_e),
            near(c) + here(st, we) + near(tv[block]),
            scratch=[((voxels, narrow), F32)],
            limit=20,
        )

    def widen(block, c, mom2, sloc, we):
        return call(
            k_widen,
            "widen",
            [(field_w, WIDE)],
            [(c, NARROW)] + near(mom2, tv[block], sloc, we),
            scratch=[((3 * narrow, wide), BF16)],
            limit=48,
            steps=many,
            cost=FILLER,
        )[0]

    def join(e, x, st, off, we, wr):
        return call(
            functools.partial(k_join, frames, total, float(voxels)),
            "join",
            [(field_w, WIDE), (field_n, NARROW), (face_n, NARROW), (face_n, NARROW)]
            + near(mom_w, mom_n, stat_n),
            [(e, WIDE), (x, WIDE)] + here(st) + near(off, we, vw[0], wr),
            scratch=[((3 * wide, narrow), BF16), (mom_n, F32)],
            limit=56,
            steps=many,
        )

    def turn(e, x, c, st, off, we, mom2):
        return call(
            functools.partial(k_turn, total, float(voxels)),
            "turn",
            [((rows, width, frames, wide), WIDE), (field_w, WIDE), (field_n, NARROW)]
            + near(down_e, mom_w, mom_n, mom_w, stat_w),
            [(e, WIDE), (x, WIDE), (cot, WIDE), (c, NARROW)]
            + here(st)
            + near(off, we, vw[1], mom2, tv[1]),
            scratch=[((2 * wide, narrow), BF16), (mom_w, F32)],
            limit=58,
            steps=many,
        )

    def stat_with(more):
        return (devices, 2 * halves + sum(value.shape[-2] for value in more), 128)

    def second(block, u, c, st, we, momw, smean, mom2, *more):
        return call(
            functools.partial(k_second, total),
            "second",
            parts(field_n) + near(mom_w, stat_with(more)),
            parts(u, c) + here(st, we) + near(momw, smean, mom2, tv[block], *more),
            scratch=[((2 * narrow, narrow), BF16), (mom_n, F32)],
            limit=24,
            steps=few,
        )

    def center(block, n, c, st, mom2):
        return call(
            functools.partial(k_center, frames, total),
            "center",
            [(field_n, NARROW), (face_n, NARROW), (face_n, NARROW)]
            + near(mom_n, *([(st.shape[1] - 2 * halves, 128)] if st.shape[1] > 2 * halves else [])),
            parts(n, c) + here(st) + near(tv[block], mom2),
            limit=24,
            steps=many,
        )

    def first_back(block, gc, halos, a, wm, mom1, *more):
        return call(
            functools.partial(k_first_back, line, frames, len(more)),
            "first_back",
            near(field_n, stat_with(more), *mixed_halves),
            [(flags, SM)]
            + near(gc, *halos[:2])
            + here(*halos[2:])
            + near(a, wm, tv[block], mom1, *more),
            scratch=[(field_n, F32)] + [(grown_n, F32)] * 3
            + [((halves, 27, 8, 128), F32), (down_m, F32)],
            limit=20,
            lazy=(2 + len(halos), 3 + len(halos), 5 + len(halos)),
        )

    def side_grads(gc, grown, p, we, gw, momw, smean, sloc, seen):
        return call(
            functools.partial(k_side_grads, line, frames, total),
            "side_grads",
            near(*side_halves),
            [(flags, SM)] + near(gc, *grown, p, we, gw, momw, smean, sloc, seen),
            scratch=[((128, narrow), F32)],
            limit=24,
            cost=HIDER,
        )

    def add_grads(mine, theirs, mine_late, theirs_late):
        dims = (mine.shape[0], mine.shape[1] + mine_late.shape[1], narrow)
        return call(
            k_add_grads,
            "add_grads",
            near(dims),
            near(mine) + here(theirs) + near(mine_late) + here(theirs_late),
            limit=12,
        )[0]

    def between(n1, a, st, mom1, wr, x, gz, c, mom2, we, momw, smean):
        return call(
            functools.partial(k_between, total),
            "between",
            [(field_w, WIDE), (field_n, NARROW)] + near(down_e, mom_n, stat_w, *down_halves),
            [(me, SM)]
            + parts(n1, a, c)
            + [(x, WIDE), (gz, WIDE)]
            + here(st)
            + near(tv[1], mom1, wr, mom2, tv[0], we, momw, smean),
            scratch=[((2 * narrow, wide), BF16), ((2 * wide, narrow), BF16), (down_e, F32),
                     (mom_w, F32)],
            limit=58,
            steps=many,
        )

    def last_weight(n1, a, st, mom1):
        return call(
            functools.partial(k_last_weight, total),
            "last_weight",
            [(field_n, NARROW)] + near(mom_n, *down_halves),
            [(me, SM)] + parts(n1, a) + [(x0, WIDE)] + here(st) + near(tv[0], mom1),
            scratch=[(down_e, F32)],
            limit=48,
            steps=many,
        )

    def last(ga, gz, wr):
        return call(
            k_last,
            "last",
            [((rows, width, frames, wide), WIDE)],
            [(ga, NARROW), (gz, WIDE)] + near(wr),
            scratch=[((2 * narrow, wide), BF16)],
            limit=48,
            steps=many,
            cost=FILLER,
        )[0]


    if not owned:
        a0, *faces, st, wr0 = first(wr0)
    c0, grown0, mom10, st = mix(0, a0, faces, exchange(st), wm0)
    mom20, off0, sloc0, seen0, st = expand(0, c0, exchange(st), we0)
    e0 = widen(0, c0, mom20, sloc0, we0)
    x1, a1, *faces, momw0, smean0, st = join(e0, x0, exchange(st), off0, we0, wr1)
    c1, grown1, mom11, st = mix(1, a1, faces, exchange(st), wm1)
    mom21, off1, sloc1, seen1, st = expand(1, c1, exchange(st), we1)
    e1 = widen(1, c1, mom21, sloc1, we1)
    out, gz1, u1, p1, momw1, smean1, pool, st = turn(
        e1, x1, c1, exchange(st), off1, we1, mom21
    )

    clips = clip_index.shape[0] // 6
    labels = jnp.arange(clips, dtype=jnp.int32)
    hot = (centre[None, :] == labels[:, None]).astype(F32)
    pooled = jnp.dot(
        jnp.concatenate([hot] * (8 // frames), axis=1), pool, precision=HIGHEST,
        preferred_element_type=F32,
    )
    if owned:
        room = -(-clips * share_w // 128) * 128
        pooled = pooled.reshape(clips, devices, share_w).transpose(1, 0, 2).reshape(devices, -1)
        pooled = jnp.pad(pooled, ((0, 0), (0, room - clips * share_w)))
        more = (pooled.reshape(devices, room // 128, 128),)
    else:
        more = ()
        pooled = lax.psum(pooled, AX)
    counts = jnp.sum((clip_index[None, :] == labels[:, None]).astype(F32), axis=1)

    n, gw1, st = second(1, u1, c1, exchange(st), we1, momw1, smean1, mom21, *more)
    gc, face_f, face_l, gd1, *more = center(1, n, c1, exchange(st), mom21)
    faces = (face_f, face_l)
    side1 = side_grads(gc, grown1, p1, we1, gw1, momw1, smean1, sloc1, seen1)
    halos, *side1 = frame_halo(*faces, width, shape, side1)
    halos = halos[:2] + row_halo(gc, line, shape) + halos[2:]
    n1, st, *dm1 = first_back(1, gc, halos, a1, wm1, mom11, *more)
    st = exchange(st)
    if owned:
        one = add_grads(
            side1[0], swap_cores(side1[1], shape), dm1[0], swap_cores(dm1[1], shape)
        )
        one, st = lax.optimization_barrier((one, st))
        one = owner_parts(one, shape)
        pooled = st[:, 2 * halves :, :].reshape(devices, -1)[:, : clips * share_w]
        pooled = pooled.reshape(devices, clips, share_w).transpose(1, 0, 2).reshape(clips, wide)
    gz0, u0, p0, gn1, st, *dr1 = between(
        n1, a1, st, mom11, wr1, x1, gz1, c0, mom20, we0, momw0, smean0
    )
    if owned:
        st, one = lax.optimization_barrier((st, one))
    st = exchange(st)
    if owned:
        dr1 = core_sums(*dr1, shape)
        dr1, st = lax.optimization_barrier((dr1, st))
        dr1 = owner_parts(dr1, shape)
    n, gw0, st = second(0, u0, c0, st, we0, momw0, smean0, mom20)
    gc, *faces, gd0 = center(0, n, c0, exchange(st), mom20)
    side0 = side_grads(gc, grown0, p0, we0, gw0, momw0, smean0, sloc0, seen0)
    halos, *side0 = frame_halo(*faces, width, shape, side0)
    halos = halos[:2] + row_halo(gc, line, shape) + halos[2:]
    n1, st, *dm0 = first_back(0, gc, halos, a0, wm0, mom10)
    st = exchange(st)
    home = lambda field: field.transpose(2, 0, 1, 3)
    if owned:
        zero = add_grads(
            side0[0], swap_cores(side0[1], shape), dm0[0], swap_cores(dm0[1], shape)
        )
        zero, n1, dr1 = lax.optimization_barrier((zero, n1, dr1))
        zero = owner_parts(zero, shape)
        ga0, gn0, mine, theirs = last_weight(n1, a0, st, mom10)
        tail = owner_parts(core_sums(mine, theirs, shape), shape)
        gx = last(ga0, gz0, wr0)
        pooled = pooled / (counts * float(rows * shape[1] * width))[:, None]
        values = call(
            k_update,
            "update",
            near(*[weights[i].shape for i in range(10)] * 3),
            [(me, SM)]
            + near(zero, one, tail, dr1, gn0, gn1, gd0, gd1, gw0, gw1, *weights, *momenta),
            limit=12,
        )
        return (home(out), pooled, home(gx), *values)

    ga0, gn0, dr0 = last_weight(n1, a0, st, mom10)
    gx = last(ga0, gz0, wr0)
    (de0, dk0), (de1, dk1), dm0, dm1 = side0, side1, dm0[0], dm1[0]
    pooled = pooled / (counts * float(rows * shape[1] * width))[:, None]

    def own(full):
        parts = full.reshape((devices, full.shape[0] // devices) + full.shape[1:])
        return jnp.sum(lax.all_to_all(parts, AX, 0, 0), axis=0)

    deltas = [
        jnp.stack([own(dr0), own(dr1[0])]),
        jnp.stack([own(dm0), own(dm1)]),
        jnp.stack([own(dk0[:27].T), own(dk1[:27].T)]),
        jnp.stack([own(de0), own(de1)]),
    ]

    def mine(vec0, vec1, row):
        share = vec0.shape[1] // devices
        both = jnp.stack([vec0[row], vec1[row]])
        return lax.dynamic_slice_in_dim(both, rank * share, share, axis=1)

    for first_part, second_part in ((gn0, gn1), (gd0, gd1), (gw0, gw1)):
        deltas.append(mine(first_part, second_part, 0))
        deltas.append(mine(first_part, second_part, 1))
    velocity = [MOMENTUM * momenta[i] + deltas[i] for i in range(10)]
    updated = [
        weights[i] - LEARN_RATE * (deltas[i] + MOMENTUM * velocity[i]) for i in range(10)
    ]
    return (home(out), pooled, home(gx), *deltas, *velocity, *updated)


def solution(mesh):
    field = P("dp", "fsdp", None, None)
    mat = P(None, AX, None)
    vec = P(None, AX)
    group = (mat,) * 4 + (vec,) * 6
    return jax.shard_map(
        body,
        mesh=mesh,
        in_specs=(field, field, P()) + group * 2,
        out_specs=(field, P(), field) + group * 3,
        check_vma=False,
    )
```
